512 devices in a mesh: seq: 32 (over x, y, z_hi), tp: 16 (over z_lo, core).
Axes of the slice: x: 4, y: 4, z: 16 (z_hi: 2, z_lo: 8; z = z_hi * 8 + z_lo), core: 2. Of those that a mesh axis runs over, the one named last changes fastest.
Arguments:
- query_rows: bfloat16 [8192, 6144], P('seq', 'tp'), may hold values from -6 to 6
- key_rows: bfloat16 [8192, 6144], P('seq', 'tp'), may hold values from -6 to 6
- value_rows: bfloat16 [8192, 6144], P('seq', 'tp'), may hold values from -6 to 6
- log_decay: float32 [48, 8192], P('tp', 'seq'), as said below
- doc_starts: int32 [32, 3], P('seq'), may hold values from 0 to 256, as said below
- residual_in: bfloat16 [8192, 4096], P(('seq', 'tp')), may hold values from -6 to 6
- out_weight: bfloat16 [6144, 4096], P('tp'), may hold values from -0.078125 to 0.078125
- norm_gain: float32 [4096], replicated, may hold values from 0.5 to 1.5
Outputs:
- hidden_state: bfloat16 [8192, 4096], P(('seq', 'tp'))
- normed_state: bfloat16 [8192, 4096], P(('seq', 'tp'))
The draws below stay inside these ranges and needn't reach their ends.
Inputs may be any that keep to these rules, and one draw needn't show every extreme that they name: `doc_starts`: each entry is a document's start offset within its shard; 256 marks an unused slot; the last entry of every row is 256; the first entry of shard 0 is 0; entries may repeat and need not be sorted. `log_decay`: every entry is negative.
All inputs are finite; a program needn't handle non-finite values.
Results may differ from the reference program's by a relative error of at most 0.022.
Values may be sent and summed in bfloat16 or wider, within the bound.
No kernel may reach another device: no remote copies, remote signals or barrier semaphores. Data moves between devices by JAX's collectives and lax.ppermute only.
A program may use at most 64 MiB of HBM per device.

```python
import math
import jax
import jax.numpy as jnp
from jax import lax

D = 4096
HEADS_PER_SHARD = 48
HDIM = 128
SPAN = 256
MAXDOC = 3
SHARDS = 32
TOKEN_TOTAL = 8192
N_TP = 16


def draw_log_decay(key, part):
    key_entries = jax.random.split(key, 7)
    slow_rate = jnp.exp(jax.random.uniform(key_entries[0], (HEADS_PER_SHARD, 1), jnp.float32, math.log(0.1 / TOKEN_TOTAL), math.log(0.6 / TOKEN_TOTAL)))
    fast_rate = jnp.exp(jax.random.uniform(key_entries[1], (HEADS_PER_SHARD, 1), jnp.float32, math.log(0.004), math.log(0.05)))
    share = 0.5
    picked = jax.random.uniform(key_entries[2], (HEADS_PER_SHARD, 1), jnp.float32) < share
    decay_speed = jnp.where(picked, slow_rate, fast_rate)
    coarse_estimate = jnp.exp(jax.random.uniform(key_entries[3], (HEADS_PER_SHARD, TOKEN_TOTAL), jnp.float32, math.log(0.5), math.log(2.0)))
    block_list = jnp.exp(jax.random.uniform(key_entries[4], (HEADS_PER_SHARD, TOKEN_TOTAL // SPAN, 1), jnp.float32, math.log(0.5), math.log(2.0)))
    block_list = jnp.broadcast_to(block_list, (HEADS_PER_SHARD, TOKEN_TOTAL // SPAN, SPAN)).reshape(HEADS_PER_SHARD, TOKEN_TOTAL)
    sudden_jump = jax.random.uniform(key_entries[5], (HEADS_PER_SHARD, TOKEN_TOTAL), jnp.float32) < 3.0 / TOKEN_TOTAL
    decay_drop_amount = jnp.log(jax.random.uniform(key_entries[6], (HEADS_PER_SHARD, TOKEN_TOTAL), jnp.float32, 0.5, 0.8))
    return -(decay_speed * coarse_estimate * block_list) + jnp.where(sudden_jump, decay_drop_amount, 0.0)


def draw_doc_starts(key, part):
    raw = jax.random.randint(key, (SHARDS, MAXDOC - 1), 0, 8 * SPAN)
    picked = jnp.minimum(raw, SPAN).astype(jnp.int32)
    picked = picked.at[0, 0].set(0)
    unused = jnp.full((SHARDS, 1), SPAN, jnp.int32)
    return jnp.concatenate([picked, unused], axis=1)


def block_scale(own_key, extent, cuts, smallest, largest):
    gain = 1.0
    for dim, blocks in cuts:
        heights = jax.random.uniform(jax.random.fold_in(jax.random.fold_in(own_key, 6), dim), (blocks,), jnp.float32, smallest / len(cuts), largest / len(cuts))
        gain = gain * jnp.repeat(jnp.exp(heights), extent[dim] // blocks).reshape((-1,) + (1,) * (len(extent) - 1 - dim))
    return gain


def normal_values(own_key, shape, scale, bound, cuts=(), kind=jnp.bfloat16):
    entries = scale * jax.random.normal(own_key, shape, jnp.float32)
    if cuts:
        entries = entries * block_scale(own_key, shape, cuts, -0.22, 0.18)
    return jnp.clip(entries, -bound, bound).astype(kind)


def setup_inputs(seed: int = 0) -> dict:
    key_list = jax.random.split(jax.random.key(seed), 9)
    query_rows = normal_values(key_list[0], (TOKEN_TOTAL, HEADS_PER_SHARD * HDIM), 1.0, 6.0, ((0, 32), (1, 16)))
    key_rows = normal_values(key_list[1], (TOKEN_TOTAL, HEADS_PER_SHARD * HDIM), 1.0, 6.0, ((0, 32), (1, 16)))
    value_rows = normal_values(key_list[2], (TOKEN_TOTAL, HEADS_PER_SHARD * HDIM), 1.0, 6.0, ((0, 32), (1, 16)))
    log_decay = draw_log_decay(jax.random.fold_in(key_list[8], 71), 0)
    doc_starts = draw_doc_starts(jax.random.fold_in(key_list[8], 71), 0)
    residual_in = normal_values(key_list[5], (TOKEN_TOTAL, D), 1.0, 6.0, ((0, 512),))
    out_weight = normal_values(key_list[6], (HEADS_PER_SHARD * HDIM, D), (HEADS_PER_SHARD * HDIM) ** -0.5, 0.078125, ((0, 16),))
    norm_gain = jnp.clip(1.0 + 0.1 * jax.random.normal(key_list[7], (D,), jnp.float32), 0.5, 1.5)
    return {"query_rows": query_rows, "key_rows": key_rows, "value_rows": value_rows, "log_decay": log_decay, "doc_starts": doc_starts, "residual_in": residual_in, "out_weight": out_weight, "norm_gain": norm_gain}


def span_mix(query_c, key_c, value_c, decay_c, starts, state_in):
    length = query_c.shape[0]
    positions = jnp.arange(length, dtype=jnp.int32)
    segment = lax.optimization_barrier(jnp.sum((starts[None, :] <= positions[:, None]).astype(jnp.int32), axis=1))
    cumulative = jnp.cumsum(decay_c, axis=1)
    lower_mask = positions[:, None] >= positions[None, :]
    same_doc = lower_mask & (segment[:, None] == segment[None, :])
    spread = cumulative[:, :, None] - cumulative[:, None, :]
    decay_mat = jnp.exp(jnp.where(same_doc[None], spread, -jnp.inf))
    query_wide = query_c.astype(jnp.float32)
    key_wide = key_c.astype(jnp.float32)
    value_wide = value_c.astype(jnp.float32)
    scores = jnp.einsum('ihd,jhd->hij', query_wide, key_wide)
    weights = (scores * decay_mat).astype(jnp.bfloat16)
    intra_out = jnp.einsum('hij,jhd->ihd', weights.astype(jnp.float32), value_wide)
    first_doc = (segment == 0).astype(jnp.float32)
    carry_scale = jnp.exp(cumulative) * first_doc[None, :]
    state_low = state_in.astype(jnp.bfloat16).astype(jnp.float32)
    inter_out = jnp.einsum('ihd,hde->ihe', query_wide, state_low, precision=lax.Precision.HIGHEST) * carry_scale.T[:, :, None]
    last_seg = segment[length - 1]
    tail_weight = jnp.exp(cumulative[:, length - 1:] - cumulative) * (segment == last_seg).astype(jnp.float32)[None, :]
    decayed_keys = (key_wide * tail_weight.T[:, :, None]).astype(jnp.bfloat16).astype(jnp.float32)
    local_state = jnp.einsum('jhd,jhe->hde', decayed_keys, value_wide, precision=lax.Precision.HIGHEST)
    through = jnp.exp(cumulative[:, length - 1]) * (last_seg == 0).astype(jnp.float32)
    mixed = intra_out + inter_out
    normed = mixed * lax.rsqrt(lax.optimization_barrier(jnp.mean(mixed * mixed, axis=2, keepdims=True)) + 1e-06)
    return (normed.astype(jnp.bfloat16), through, local_state)

def reference(query_rows, key_rows, value_rows, log_decay, doc_starts, residual_in, out_weight, norm_gain):
    shards = TOKEN_TOTAL // SPAN
    heads_local = HEADS_PER_SHARD // N_TP
    query_all = query_rows.reshape(shards, SPAN, HEADS_PER_SHARD, HDIM)
    key_all = key_rows.reshape(shards, SPAN, HEADS_PER_SHARD, HDIM)
    value_all = value_rows.reshape(shards, SPAN, HEADS_PER_SHARD, HDIM)
    decay_all = log_decay.reshape(HEADS_PER_SHARD, shards, SPAN).transpose(1, 0, 2)

    def advance(state_in, inputs):
        query_c, key_c, value_c, decay_c, starts = inputs
        normed, through, local_state = span_mix(query_c, key_c, value_c, decay_c, starts, state_in)
        return (through[:, None, None] * state_in + local_state, normed)
    initial = jnp.zeros((HEADS_PER_SHARD, HDIM, HDIM), jnp.float32)
    final_state, attended = lax.scan(advance, initial, (query_all, key_all, value_all, decay_all, doc_starts))
    attended = attended.reshape(TOKEN_TOTAL, HEADS_PER_SHARD * HDIM)
    group_width = heads_local * HDIM
    summed = jnp.zeros((TOKEN_TOTAL, D), jnp.float32)
    for group in range(N_TP):
        piece = jnp.dot(attended[:, group * group_width:(group + 1) * group_width], out_weight[group * group_width:(group + 1) * group_width], preferred_element_type=jnp.float32).astype(jnp.bfloat16)
        summed = summed + piece.astype(jnp.float32)
    hidden = residual_in.astype(jnp.float32) + summed
    scale = lax.rsqrt(lax.optimization_barrier(jnp.mean(hidden * hidden, axis=1, keepdims=True)) + 1e-05)
    normed_state = (hidden * scale * norm_gain.astype(jnp.float32)[None, :]).astype(jnp.bfloat16)
    return (hidden.astype(jnp.bfloat16), normed_state)
```

```python
import jax
import jax.numpy as jnp
from jax import lax
from jax.experimental import pallas as pl
from jax.experimental.pallas import tpu as pltpu
from jax.sharding import PartitionSpec as P

SPAN = 256
HEADS = 3
HDIM = 128
STATE = HEADS * HDIM
PAYLOAD = STATE + 8
D = 4096
F32 = jnp.float32
BF16 = jnp.bfloat16

SHARDS = 32
FLIP_Z = [(i, i ^ 1) for i in range(SHARDS)]
ROW_Y = [[g + 2 * k for k in range(4)] for g in range(SHARDS) if g & 6 == 0]
ROW_X = [[g + 8 * k for k in range(4)] for g in range(8)]

VMEM = pl.BlockSpec(memory_space=pltpu.VMEM)
SMEM = pl.BlockSpec(memory_space=pltpu.SMEM)


def segment_of(starts_ref, positions):
    total = jnp.zeros(positions.shape, jnp.int32)
    for slot in range(3):
        total = total + (positions >= starts_ref[0, slot]).astype(jnp.int32)
    return total


def running_sums(weights, decay, column):
    dims = (((1,), (1,)), ((), ()))
    a, b = (weights, decay) if column else (decay, weights)
    return lax.dot_general(a, b, dims, precision=lax.Precision.HIGHEST, preferred_element_type=F32)


def grid_iotas():
    row = lax.broadcasted_iota(jnp.int32, (SPAN, SPAN), 0)
    col = lax.broadcasted_iota(jnp.int32, (SPAN, SPAN), 1)
    return row, col


def state_kernel(starts_ref, decay_ref, key_ref, value_ref, out_ref):
    row, col = grid_iotas()
    later = (col > row).astype(F32)
    decay = decay_ref[...]
    tail = running_sums(later, decay, True)
    segment = segment_of(starts_ref, lax.broadcasted_iota(jnp.int32, (SPAN, 1), 0))
    last = segment_of(starts_ref, jnp.full((1, 1), SPAN - 1, jnp.int32))
    tail_weight = jnp.exp(tail) * (segment == last).astype(F32)
    through = jnp.exp(jnp.sum(decay, axis=1, keepdims=True)) * (last == 0).astype(F32)
    high = through.astype(BF16).astype(F32)
    low = (through - high).astype(BF16).astype(F32)
    rows = jnp.concatenate([high, low, jnp.zeros((2, 1), F32)], axis=0)
    out_ref[STATE:, :] = jnp.broadcast_to(rows, (8, HDIM)).astype(BF16)
    for h in range(HEADS):
        cut = slice(h * HDIM, (h + 1) * HDIM)
        decayed = (key_ref[:, cut].astype(F32) * tail_weight[:, h : h + 1]).astype(BF16)
        out_ref[cut, :] = lax.dot_general(
            decayed, value_ref[:, cut], (((0,), (0,)), ((), ())), preferred_element_type=F32
        ).astype(BF16)


def intra_kernel(starts_ref, decay_ref, query_ref, key_ref, value_ref, out_ref):
    row, col = grid_iotas()
    lower = row >= col
    lower_f = lower.astype(F32)
    decay = decay_ref[...]
    cum_col = running_sums(lower_f, decay, True)
    cum_row = running_sums(lower_f, decay, False)
    seg_col = segment_of(starts_ref, lax.broadcasted_iota(jnp.int32, (SPAN, 1), 0))
    seg_row = segment_of(starts_ref, lax.broadcasted_iota(jnp.int32, (1, SPAN), 1))
    same = lower & (seg_col == seg_row)
    for h in range(HEADS):
        cut = slice(h * HDIM, (h + 1) * HDIM)
        spread = cum_col[:, h : h + 1] - cum_row[h : h + 1, :]
        decay_mat = jnp.exp(jnp.where(same, spread, -jnp.inf))
        scores = lax.dot_general(
            query_ref[:, cut], key_ref[:, cut], (((1,), (1,)), ((), ())), preferred_element_type=F32
        )
        weights = (scores * decay_mat).astype(BF16)
        out_ref[:, cut] = jnp.dot(weights, value_ref[:, cut], preferred_element_type=F32)


def decays(rows):
    rows = rows.astype(F32)
    return rows[0:HEADS] + rows[HEADS : 2 * HEADS]


def split_decay(decay):
    high = decay.astype(BF16).astype(F32)
    low = (decay - high).astype(BF16).astype(F32)
    return jnp.concatenate([high, low, jnp.zeros((2, HDIM), F32)], axis=0).astype(BF16)


def pair_kernel(place_ref, own_ref, other_ref, out_ref):
    odd = place_ref[0] & 1 == 1
    own_a, other_a = decays(own_ref[STATE:, :]), decays(other_ref[STATE:, :])
    later_a = jnp.where(odd, own_a, other_a)
    scales = split_decay(own_a * other_a)
    for k in range(4):
        out_ref[k, STATE:, :] = scales
    for h in range(HEADS):
        cut = slice(h * HDIM, (h + 1) * HDIM)
        own, other = own_ref[cut, :].astype(F32), other_ref[cut, :].astype(F32)
        first, second = jnp.where(odd, other, own), jnp.where(odd, own, other)
        total = (later_a[h : h + 1] * first + second).astype(BF16)
        for k in range(4):
            out_ref[k, cut, :] = total


def row_kernel(parts_ref, out_ref):
    scale = [decays(parts_ref[k, STATE:, :]) for k in range(4)]
    scales = split_decay(scale[0] * scale[1] * scale[2] * scale[3])
    for k in range(4):
        out_ref[k, STATE:, :] = scales
    for h in range(HEADS):
        cut = slice(h * HDIM, (h + 1) * HDIM)
        total = parts_ref[0, cut, :].astype(F32)
        for k in range(1, 4):
            total = scale[k][h : h + 1] * total + parts_ref[k, cut, :].astype(F32)
        total = total.astype(BF16)
        for k in range(4):
            out_ref[k, cut, :] = total


def before(parts_ref, scale, reached, h):
    cut = slice(h * HDIM, (h + 1) * HDIM)
    state = jnp.zeros((HDIM, HDIM), F32)
    through = jnp.ones((1, HDIM), F32)
    for k in range(3):
        a = scale[k][h : h + 1]
        state = jnp.where(k < reached, a * state + parts_ref[k, cut, :].astype(F32), state)
        through = jnp.where(k < reached, a * through, through)
    return state, through


def attend_kernel(
    place_ref, starts_ref, decay_ref, query_ref, intra_ref, other_ref, row_ref, col_ref,
    send_ref, keep_ref, mixed_ref,
):
    odd = place_ref[0] & 1 == 1
    row, col = grid_iotas()
    lower_f = (row >= col).astype(F32)
    cumulative = running_sums(lower_f, decay_ref[...], True)
    segment = segment_of(starts_ref, lax.broadcasted_iota(jnp.int32, (SPAN, 1), 0))
    carry = jnp.exp(cumulative) * (segment == 0).astype(F32)
    row_scale = [decays(row_ref[k, STATE:, :]) for k in range(3)]
    col_scale = [decays(col_ref[k, STATE:, :]) for k in range(3)]
    other_a = decays(other_ref[STATE:, :])
    for h in range(HEADS):
        cut = slice(h * HDIM, (h + 1) * HDIM)
        inner, inner_a = before(row_ref, row_scale, (place_ref[0] >> 1) & 3, h)
        outer, _ = before(col_ref, col_scale, place_ref[0] >> 3, h)
        state = inner_a * outer + inner
        state = jnp.where(odd, other_a[h : h + 1] * state + other_ref[cut, :].astype(F32), state)
        inter = jnp.dot(query_ref[:, cut], state.astype(BF16), preferred_element_type=F32)
        mixed = intra_ref[:, cut] + inter * carry[:, h : h + 1]
        scale = lax.rsqrt(jnp.mean(mixed * mixed, axis=1, keepdims=True) + 1e-06)
        mixed_ref[:, cut] = (mixed * scale).astype(BF16)
    core, parity, group = place_ref[1] & 1, (place_ref[1] >> 1) & 1, place_ref[1] >> 2
    for u in range(2):
        for k in range(4):
            chip = ((group + k) & 3) * 2 + (parity if u else 1 - parity)
            at = (u * 4 + k) * 16
            keep_ref[at : at + 16, :] = mixed_ref[pl.ds(pl.multiple_of(chip * 32 + core * 16, 16), 16), :]
            send_ref[at : at + 16, :] = mixed_ref[pl.ds(pl.multiple_of(chip * 32 + (1 - core) * 16, 16), 16), :]


def project_kernel(own_ref, other_ref, own_w_ref, other_w_ref, send_ref, keep_ref):
    total = jnp.dot(own_ref[...], own_w_ref[...], preferred_element_type=F32)
    total = total + jnp.dot(other_ref[...], other_w_ref[...], preferred_element_type=F32)
    total = total.astype(BF16)
    send_ref[...] = total[:64]
    keep_ref[...] = total[64:]


def pair_sum_kernel(keep_ref, got_ref, own_ref, a_ref, b_ref, c_ref):
    for k, ref in enumerate((own_ref, a_ref, b_ref, c_ref)):
        cut = slice(k * 16, (k + 1) * 16)
        total = keep_ref[cut, :].astype(F32) + got_ref[cut, :].astype(F32)
        ref[...] = total.astype(ref.dtype)


def finish_kernel(own_ref, a_ref, b_ref, c_ref, residual_ref, gain_ref, hidden_ref, normed_ref):
    total = own_ref[...] + a_ref[...].astype(F32) + b_ref[...].astype(F32) + c_ref[...].astype(F32)
    hidden = residual_ref[...].astype(F32) + total
    scale = lax.rsqrt(jnp.mean(hidden * hidden, axis=1, keepdims=True) + 1e-05)
    hidden_ref[...] = hidden.astype(BF16)
    normed_ref[...] = (hidden * scale * gain_ref[...]).astype(BF16)


def call(body, shapes, specs, *args, scratch=()):
    return pl.pallas_call(
        body,
        out_shape=shapes,
        in_specs=specs,
        out_specs=jax.tree.map(lambda _: VMEM, shapes),
        scratch_shapes=list(scratch),
        compiler_params=pltpu.CompilerParams(vmem_limit_bytes=40 * 1024 * 1024),
    )(*args)


def of(shape, dtype):
    return jax.ShapeDtypeStruct(shape, dtype)


def shards(
    query_rows, key_rows, value_rows, log_decay, doc_starts, residual_in, out_weight, norm_gain
):
    place = jnp.stack([lax.axis_index("seq"), lax.axis_index("tp")]).astype(jnp.int32)

    local = call(
        state_kernel, of((PAYLOAD, HDIM), BF16), [SMEM, VMEM, VMEM, VMEM],
        doc_starts, log_decay, key_rows, value_rows,
    )
    other = lax.ppermute(local, "seq", FLIP_Z)
    intra = call(
        intra_kernel, of((SPAN, STATE), F32), [SMEM, VMEM, VMEM, VMEM, VMEM],
        doc_starts, log_decay, query_rows, key_rows, value_rows,
    )
    _, late_weight = lax.optimization_barrier((intra, out_weight))
    other_weight = lax.ppermute(late_weight, "tp", [(i, i ^ 1) for i in range(16)])
    other, intra = lax.optimization_barrier((other, intra))
    four = of((4, PAYLOAD, HDIM), BF16)
    pairs = call(pair_kernel, four, [SMEM, VMEM, VMEM], place, local, other)
    rows = lax.all_to_all(pairs, "seq", 0, 0, axis_index_groups=ROW_Y)
    totals = call(row_kernel, four, [VMEM], rows)
    cols = lax.all_to_all(totals, "seq", 0, 0, axis_index_groups=ROW_X)
    half = of((SPAN // 2, STATE), BF16)
    send, keep = call(
        attend_kernel, (half, half), [SMEM, SMEM] + [VMEM] * 6,
        place, doc_starts, log_decay, query_rows, intra, other, rows, cols,
        scratch=[pltpu.VMEM((SPAN, STATE), BF16)],
    )
    got = lax.ppermute(send, "tp", [(i, i ^ 1) for i in range(16)])

    block = 1024
    whole = pl.BlockSpec((SPAN // 2, STATE), lambda j: (0, 0))
    piece = pl.BlockSpec((STATE, block), lambda j: (0, j))
    out = pl.BlockSpec((64, block), lambda j: (0, j))
    quarter = of((64, D), BF16)
    send, keep = pl.pallas_call(
        project_kernel,
        grid=(D // block,),
        in_specs=[whole, whole, piece, piece],
        out_specs=(out, out),
        out_shape=(quarter, quarter),
        compiler_params=pltpu.CompilerParams(vmem_limit_bytes=40 * 1024 * 1024),
    )(keep, got, out_weight, other_weight)
    got = lax.ppermute(send, "tp", [(i, i ^ 2) for i in range(16)])
    chunk = of((16, D), BF16)
    own, *parts = call(
        pair_sum_kernel, (of((16, D), F32), chunk, chunk, chunk), [VMEM, VMEM], keep, got
    )
    parts = [
        lax.ppermute(part, "tp", [(i, (i + 4 * k) % 16) for i in range(16)])
        for k, part in enumerate(parts, 1)
    ]
    return call(
        finish_kernel, (chunk, chunk), [VMEM] * 6, own, *parts, residual_in, norm_gain[None, :]
    )


def solution(mesh):
    return jax.shard_map(
        shards,
        mesh=mesh,
        in_specs=(
            P("seq", "tp"),
            P("seq", "tp"),
            P("seq", "tp"),
            P("tp", "seq"),
            P("seq", None),
            P(("seq", "tp"), None),
            P("tp", None),
            P(),
        ),
        out_specs=(P(("seq", "tp"), None), P(("seq", "tp"), None)),
        check_vma=False,
    )
```

```python
import jax
import jax.numpy as jnp
from jax import lax
from jax.experimental import pallas as pl
from jax.experimental.pallas import tpu as pltpu
from jax.sharding import PartitionSpec as P

SPAN = 256
HEADS = 3
HDIM = 128
STATE = HEADS * HDIM
PAYLOAD = STATE + 8
D = 4096
F32 = jnp.float32
BF16 = jnp.bfloat16

SHARDS = 32
FLIP_Z = [(i, i ^ 1) for i in range(SHARDS)]
ROW_Y = [[g + 2 * k for k in range(4)] for g in range(SHARDS) if g & 6 == 0]
ROW_X = [[g + 8 * k for k in range(4)] for g in range(8)]

VMEM = pl.BlockSpec(memory_space=pltpu.VMEM)
HBM = pl.BlockSpec(memory_space=pltpu.HBM)
SMEM = pl.BlockSpec(memory_space=pltpu.SMEM)


def segment_of(starts_ref, positions):
    total = jnp.zeros(positions.shape, jnp.int32)
    for slot in range(3):
        total = total + (positions >= starts_ref[0, slot]).astype(jnp.int32)
    return total


def running_sums(weights, decay, column):
    dims = (((1,), (1,)), ((), ()))
    a, b = (weights, decay) if column else (decay, weights)
    return lax.dot_general(a, b, dims, precision=lax.Precision.HIGHEST, preferred_element_type=F32)


def grid_iotas():
    row = lax.broadcasted_iota(jnp.int32, (SPAN, SPAN), 0)
    col = lax.broadcasted_iota(jnp.int32, (SPAN, SPAN), 1)
    return row, col


def state_kernel(
    starts_hbm, decay_hbm, key_hbm, value_hbm, out_ref,
    starts_ref, decay_ref, key_ref, value_ref, sems,
):
    sources = (decay_hbm, starts_hbm, key_hbm, value_hbm)
    targets = (decay_ref, starts_ref, key_ref, value_ref)
    copies = [
        pltpu.make_async_copy(source, target, sems.at[k])
        for k, (source, target) in enumerate(zip(sources, targets))
    ]
    for copy in copies:
        copy.start()
    row, col = grid_iotas()
    later = (col > row).astype(F32)
    copies[0].wait()
    decay = decay_ref[...]
    tail = running_sums(later, decay, True)
    copies[1].wait()
    segment = segment_of(starts_ref, lax.broadcasted_iota(jnp.int32, (SPAN, 1), 0))
    last = segment_of(starts_ref, jnp.full((1, 1), SPAN - 1, jnp.int32))
    tail_weight = jnp.exp(tail) * (segment == last).astype(F32)
    through = jnp.exp(jnp.sum(decay, axis=1, keepdims=True)) * (last == 0).astype(F32)
    high = through.astype(BF16).astype(F32)
    low = (through - high).astype(BF16).astype(F32)
    rows = jnp.concatenate([high, low, jnp.zeros((2, 1), F32)], axis=0)
    out_ref[STATE:, :] = jnp.broadcast_to(rows, (8, HDIM)).astype(BF16)
    copies[2].wait()
    copies[3].wait()
    for h in range(HEADS):
        cut = slice(h * HDIM, (h + 1) * HDIM)
        decayed = (key_ref[:, cut].astype(F32) * tail_weight[:, h : h + 1]).astype(BF16)
        out_ref[cut, :] = lax.dot_general(
            decayed, value_ref[:, cut], (((0,), (0,)), ((), ())), preferred_element_type=F32
        ).astype(BF16)


def intra_kernel(starts_ref, decay_ref, query_ref, key_ref, value_ref, out_ref):
    row, col = grid_iotas()
    lower = row >= col
    lower_f = lower.astype(F32)
    decay = decay_ref[...]
    cum_col = running_sums(lower_f, decay, True)
    cum_row = running_sums(lower_f, decay, False)
    seg_col = segment_of(starts_ref, lax.broadcasted_iota(jnp.int32, (SPAN, 1), 0))
    seg_row = segment_of(starts_ref, lax.broadcasted_iota(jnp.int32, (1, SPAN), 1))
    same = lower & (seg_col == seg_row)
    for h in range(HEADS):
        cut = slice(h * HDIM, (h + 1) * HDIM)
        spread = cum_col[:, h : h + 1] - cum_row[h : h + 1, :]
        decay_mat = jnp.exp(jnp.where(same, spread, -jnp.inf))
        scores = lax.dot_general(
            query_ref[:, cut], key_ref[:, cut], (((1,), (1,)), ((), ())), preferred_element_type=F32
        )
        weights = (scores * decay_mat).astype(BF16)
        out_ref[:, cut] = jnp.dot(weights, value_ref[:, cut], preferred_element_type=F32)


def decays(rows):
    rows = rows.astype(F32)
    return rows[0:HEADS] + rows[HEADS : 2 * HEADS]


def split_decay(decay):
    high = decay.astype(BF16).astype(F32)
    low = (decay - high).astype(BF16).astype(F32)
    return jnp.concatenate([high, low, jnp.zeros((2, HDIM), F32)], axis=0).astype(BF16)


def pair_kernel(place_ref, own_ref, other_ref, out_ref):
    odd = place_ref[0] & 1 == 1
    own_a, other_a = decays(own_ref[STATE:, :]), decays(other_ref[STATE:, :])
    later_a = jnp.where(odd, own_a, other_a)
    scales = split_decay(own_a * other_a)
    for k in range(4):
        out_ref[k, STATE:, :] = scales
    for h in range(HEADS):
        cut = slice(h * HDIM, (h + 1) * HDIM)
        own, other = own_ref[cut, :].astype(F32), other_ref[cut, :].astype(F32)
        first, second = jnp.where(odd, other, own), jnp.where(odd, own, other)
        total = (later_a[h : h + 1] * first + second).astype(BF16)
        for k in range(4):
            out_ref[k, cut, :] = total


def row_kernel(parts_ref, out_ref):
    scale = [decays(parts_ref[k, STATE:, :]) for k in range(4)]
    scales = split_decay(scale[0] * scale[1] * scale[2] * scale[3])
    for k in range(4):
        out_ref[k, STATE:, :] = scales
    for h in range(HEADS):
        cut = slice(h * HDIM, (h + 1) * HDIM)
        total = parts_ref[0, cut, :].astype(F32)
        for k in range(1, 4):
            total = scale[k][h : h + 1] * total + parts_ref[k, cut, :].astype(F32)
        total = total.astype(BF16)
        for k in range(4):
            out_ref[k, cut, :] = total


def before(parts_ref, scale, reached, h):
    cut = slice(h * HDIM, (h + 1) * HDIM)
    state = jnp.zeros((HDIM, HDIM), F32)
    through = jnp.ones((1, HDIM), F32)
    for k in range(3):
        a = scale[k][h : h + 1]
        state = jnp.where(k < reached, a * state + parts_ref[k, cut, :].astype(F32), state)
        through = jnp.where(k < reached, a * through, through)
    return state, through


def attend_kernel(
    place_ref, starts_ref, decay_ref, query_ref, intra_ref, other_ref, row_ref, col_ref,
    send_ref, keep_ref, mixed_ref,
):
    odd = place_ref[0] & 1 == 1
    row, col = grid_iotas()
    lower_f = (row >= col).astype(F32)
    cumulative = running_sums(lower_f, decay_ref[...], True)
    segment = segment_of(starts_ref, lax.broadcasted_iota(jnp.int32, (SPAN, 1), 0))
    carry = jnp.exp(cumulative) * (segment == 0).astype(F32)
    row_scale = [decays(row_ref[k, STATE:, :]) for k in range(3)]
    col_scale = [decays(col_ref[k, STATE:, :]) for k in range(3)]
    other_a = decays(other_ref[STATE:, :])
    for h in range(HEADS):
        cut = slice(h * HDIM, (h + 1) * HDIM)
        inner, inner_a = before(row_ref, row_scale, (place_ref[0] >> 1) & 3, h)
        outer, _ = before(col_ref, col_scale, place_ref[0] >> 3, h)
        state = inner_a * outer + inner
        state = jnp.where(odd, other_a[h : h + 1] * state + other_ref[cut, :].astype(F32), state)
        inter = jnp.dot(query_ref[:, cut], state.astype(BF16), preferred_element_type=F32)
        mixed = intra_ref[:, cut] + inter * carry[:, h : h + 1]
        scale = lax.rsqrt(jnp.mean(mixed * mixed, axis=1, keepdims=True) + 1e-06)
        mixed_ref[:, cut] = (mixed * scale).astype(BF16)
    core, parity, group = place_ref[1] & 1, (place_ref[1] >> 1) & 1, place_ref[1] >> 2
    for u in range(2):
        for k in range(4):
            chip = ((group + k) & 3) * 2 + (parity if u else 1 - parity)
            at = (u * 4 + k) * 16
            keep_ref[at : at + 16, :] = mixed_ref[pl.ds(pl.multiple_of(chip * 32 + core * 16, 16), 16), :]
            send_ref[at : at + 16, :] = mixed_ref[pl.ds(pl.multiple_of(chip * 32 + (1 - core) * 16, 16), 16), :]


def project_kernel(own_ref, other_ref, own_w_ref, other_w_ref, send_ref, keep_ref):
    total = jnp.dot(own_ref[...], own_w_ref[...], preferred_element_type=F32)
    total = total + jnp.dot(other_ref[...], other_w_ref[...], preferred_element_type=F32)
    total = total.astype(BF16)
    send_ref[...] = total[:64]
    keep_ref[...] = total[64:]


def pair_sum_kernel(keep_ref, got_ref, own_ref, a_ref, b_ref, c_ref):
    for k, ref in enumerate((own_ref, a_ref, b_ref, c_ref)):
        cut = slice(k * 16, (k + 1) * 16)
        total = keep_ref[cut, :].astype(F32) + got_ref[cut, :].astype(F32)
        ref[...] = total.astype(ref.dtype)


def finish_kernel(*refs):
    *sums, residual_ref, gain_ref, hidden_ref, normed_ref = refs
    width = D // 2
    square = jnp.zeros((16, 1), F32)
    sides = []
    for side in range(2):
        total = residual_ref[:, side * width : (side + 1) * width].astype(F32) + sums[side][...]
        for part in sums[2 + 3 * side : 5 + 3 * side]:
            total = total + part[...].astype(F32)
        square = square + jnp.sum(total * total, axis=1, keepdims=True)
        sides.append(total)
    scale = lax.rsqrt(square / D + 1e-05)
    for side, total in enumerate(sides):
        cut = slice(side * width, (side + 1) * width)
        hidden_ref[:, cut] = total.astype(BF16)
        normed_ref[:, cut] = (total * scale * gain_ref[:, cut]).astype(BF16)


def call(body, shapes, specs, *args, scratch=()):
    return pl.pallas_call(
        body,
        out_shape=shapes,
        in_specs=specs,
        out_specs=jax.tree.map(lambda _: VMEM, shapes),
        scratch_shapes=list(scratch),
        compiler_params=pltpu.CompilerParams(vmem_limit_bytes=16 * 1024 * 1024),
    )(*args)


def whole(*shape):
    return pl.BlockSpec(shape, lambda j: (0,) * len(shape))


def of(shape, dtype):
    return jax.ShapeDtypeStruct(shape, dtype)


def shards(
    query_rows, key_rows, value_rows, log_decay, doc_starts, residual_in, out_weight, norm_gain
):
    place = jnp.stack([lax.axis_index("seq"), lax.axis_index("tp")]).astype(jnp.int32)

    local = call(
        state_kernel, of((PAYLOAD, HDIM), BF16), [HBM] * 4,
        *(
            pltpu.with_memory_space_constraint(a, pltpu.HBM)
            for a in (doc_starts, log_decay, key_rows, value_rows)
        ),
        scratch=[
            pltpu.SMEM((1, 3), jnp.int32),
            pltpu.VMEM((HEADS, SPAN), F32),
            pltpu.VMEM((SPAN, STATE), BF16),
            pltpu.VMEM((SPAN, STATE), BF16),
            pltpu.SemaphoreType.DMA((4,)),
        ],
    )
    late_query = lax.optimization_barrier((local, query_rows))[1]
    other = lax.ppermute(local, "seq", FLIP_Z)
    intra = call(
        intra_kernel, of((SPAN, STATE), F32), [SMEM, VMEM, VMEM, VMEM, VMEM],
        doc_starts, log_decay, late_query, key_rows, value_rows,
    )
    late_weight = lax.optimization_barrier((local, out_weight))[1]
    other_weight = lax.ppermute(late_weight, "tp", [(i, i ^ 1) for i in range(16)])
    other, intra = lax.optimization_barrier((other, intra))
    four = of((4, PAYLOAD, HDIM), BF16)
    pairs = call(pair_kernel, four, [SMEM, VMEM, VMEM], place, local, other)
    rows = lax.all_to_all(pairs, "seq", 0, 0, axis_index_groups=ROW_Y)
    totals = call(row_kernel, four, [VMEM], rows)
    cols = lax.all_to_all(totals, "seq", 0, 0, axis_index_groups=ROW_X)
    half = of((SPAN // 2, STATE), BF16)
    send, keep = call(
        attend_kernel, (half, half), [SMEM, SMEM] + [VMEM] * 6,
        place, doc_starts, log_decay, query_rows, intra, other, rows, cols,
        scratch=[pltpu.VMEM((SPAN, STATE), BF16)],
    )
    got = lax.ppermute(send, "tp", [(i, i ^ 1) for i in range(16)])

    width = D // 2
    quarter, chunk = of((64, width), BF16), of((16, width), BF16)
    owned, others = [], []
    for side in range(2):
        piece = pl.BlockSpec((STATE, width), lambda j, side=side: (0, side))
        sent, kept = pl.pallas_call(
            project_kernel,
            grid=(1,),
            in_specs=[whole(SPAN // 2, STATE)] * 2 + [piece] * 2,
            out_specs=(whole(64, width),) * 2,
            out_shape=(quarter, quarter),
            compiler_params=pltpu.CompilerParams(vmem_limit_bytes=16 * 1024 * 1024),
        )(keep, got, out_weight, other_weight)
        near = lax.ppermute(sent, "tp", [(i, i ^ 2) for i in range(16)])
        own, *parts = call(
            pair_sum_kernel, (of((16, width), F32), chunk, chunk, chunk), [VMEM, VMEM], kept, near
        )
        owned.append(own)
        others += [
            lax.ppermute(part, "tp", [(i, (i + 4 * k) % 16) for i in range(16)])
            for k, part in enumerate(parts, 1)
        ]
    full = of((16, D), BF16)
    return call(
        finish_kernel, (full, full), [VMEM] * 10, *owned, *others, residual_in, norm_gain[None, :]
    )


def solution(mesh):
    return jax.shard_map(
        shards,
        mesh=mesh,
        in_specs=(
            P("seq", "tp"),
            P("seq", "tp"),
            P("seq", "tp"),
            P("tp", "seq"),
            P("seq", None),
            P(("seq", "tp"), None),
            P("tp", None),
            P(),
        ),
        out_specs=(P(("seq", "tp"), None), P(("seq", "tp"), None)),
        check_vma=False,
    )
```

```python
import jax
import jax.numpy as jnp
from jax import lax
from jax.experimental import pallas as pl
from jax.experimental.pallas import tpu as pltpu
from jax.sharding import PartitionSpec as P

SPAN = 256
HEADS = 3
HDIM = 128
STATE = HEADS * HDIM
PAYLOAD = STATE + 8
D = 4096
F32 = jnp.float32
BF16 = jnp.bfloat16

SHARDS = 32
FLIP_Z = [(i, i ^ 1) for i in range(SHARDS)]
ROW_Y = [[g + 2 * k for k in range(4)] for g in range(SHARDS) if g & 6 == 0]
ROW_X = [[g + 8 * k for k in range(4)] for g in range(8)]

VMEM = pl.BlockSpec(memory_space=pltpu.VMEM)
HBM = pl.BlockSpec(memory_space=pltpu.HBM)
SMEM = pl.BlockSpec(memory_space=pltpu.SMEM)


def segment_of(starts_ref, positions):
    total = jnp.zeros(positions.shape, jnp.int32)
    for slot in range(3):
        total = total + (positions >= starts_ref[0, slot]).astype(jnp.int32)
    return total


def running_sums(weights, decay, column):
    dims = (((1,), (1,)), ((), ()))
    a, b = (weights, decay) if column else (decay, weights)
    return lax.dot_general(a, b, dims, precision=lax.Precision.HIGHEST, preferred_element_type=F32)


def grid_iotas():
    row = lax.broadcasted_iota(jnp.int32, (SPAN, SPAN), 0)
    col = lax.broadcasted_iota(jnp.int32, (SPAN, SPAN), 1)
    return row, col


def state_kernel(
    starts_hbm, decay_hbm, key_hbm, value_hbm, out_ref,
    starts_ref, decay_ref, key_ref, value_ref, sems,
):
    sources = (decay_hbm, starts_hbm, key_hbm, value_hbm)
    targets = (decay_ref, starts_ref, key_ref, value_ref)
    copies = [
        pltpu.make_async_copy(source, target, sems.at[k])
        for k, (source, target) in enumerate(zip(sources, targets))
    ]
    for copy in copies:
        copy.start()
    row, col = grid_iotas()
    later = (col > row).astype(F32)
    copies[0].wait()
    decay = decay_ref[...]
    tail = running_sums(later, decay, True)
    copies[1].wait()
    segment = segment_of(starts_ref, lax.broadcasted_iota(jnp.int32, (SPAN, 1), 0))
    last = segment_of(starts_ref, jnp.full((1, 1), SPAN - 1, jnp.int32))
    tail_weight = jnp.exp(tail) * (segment == last).astype(F32)
    through = jnp.exp(jnp.sum(decay, axis=1, keepdims=True)) * (last == 0).astype(F32)
    high = through.astype(BF16).astype(F32)
    low = (through - high).astype(BF16).astype(F32)
    rows = jnp.concatenate([high, low, jnp.zeros((2, 1), F32)], axis=0)
    out_ref[STATE:, :] = jnp.broadcast_to(rows, (8, HDIM)).astype(BF16)
    copies[2].wait()
    copies[3].wait()
    for h in range(HEADS):
        cut = slice(h * HDIM, (h + 1) * HDIM)
        decayed = (key_ref[:, cut].astype(F32) * tail_weight[:, h : h + 1]).astype(BF16)
        out_ref[cut, :] = lax.dot_general(
            decayed, value_ref[:, cut], (((0,), (0,)), ((), ())), preferred_element_type=F32
        ).astype(BF16)


def intra_kernel(starts_ref, decay_ref, query_ref, key_ref, value_ref, out_ref):
    row, col = grid_iotas()
    lower = row >= col
    lower_f = lower.astype(F32)
    decay = decay_ref[...]
    cum_col = running_sums(lower_f, decay, True)
    cum_row = running_sums(lower_f, decay, False)
    seg_col = segment_of(starts_ref, lax.broadcasted_iota(jnp.int32, (SPAN, 1), 0))
    seg_row = segment_of(starts_ref, lax.broadcasted_iota(jnp.int32, (1, SPAN), 1))
    same = lower & (seg_col == seg_row)
    for h in range(HEADS):
        cut = slice(h * HDIM, (h + 1) * HDIM)
        spread = cum_col[:, h : h + 1] - cum_row[h : h + 1, :]
        decay_mat = jnp.exp(jnp.where(same, spread, -jnp.inf))
        scores = lax.dot_general(
            query_ref[:, cut], key_ref[:, cut], (((1,), (1,)), ((), ())), preferred_element_type=F32
        )
        weights = (scores * decay_mat).astype(BF16)
        out_ref[:, cut] = jnp.dot(weights, value_ref[:, cut], preferred_element_type=F32)


def decays(rows):
    rows = rows.astype(F32)
    return rows[0:HEADS] + rows[HEADS : 2 * HEADS]


def split_decay(decay):
    high = decay.astype(BF16).astype(F32)
    low = (decay - high).astype(BF16).astype(F32)
    return jnp.concatenate([high, low, jnp.zeros((2, HDIM), F32)], axis=0).astype(BF16)


def pair_kernel(place_ref, own_ref, other_ref, out_ref):
    odd = place_ref[0] & 1 == 1
    own_a, other_a = decays(own_ref[STATE:, :]), decays(other_ref[STATE:, :])
    later_a = jnp.where(odd, own_a, other_a)
    scales = split_decay(own_a * other_a)
    for k in range(4):
        out_ref[k, STATE:, :] = scales
    for h in range(HEADS):
        cut = slice(h * HDIM, (h + 1) * HDIM)
        own, other = own_ref[cut, :].astype(F32), other_ref[cut, :].astype(F32)
        first, second = jnp.where(odd, other, own), jnp.where(odd, own, other)
        total = (later_a[h : h + 1] * first + second).astype(BF16)
        for k in range(4):
            out_ref[k, cut, :] = total


def row_kernel(parts_ref, out_ref):
    scale = [decays(parts_ref[k, STATE:, :]) for k in range(4)]
    scales = split_decay(scale[0] * scale[1] * scale[2] * scale[3])
    for k in range(4):
        out_ref[k, STATE:, :] = scales
    for h in range(HEADS):
        cut = slice(h * HDIM, (h + 1) * HDIM)
        total = parts_ref[0, cut, :].astype(F32)
        for k in range(1, 4):
            total = scale[k][h : h + 1] * total + parts_ref[k, cut, :].astype(F32)
        total = total.astype(BF16)
        for k in range(4):
            out_ref[k, cut, :] = total


def before(parts_ref, scale, reached, h):
    cut = slice(h * HDIM, (h + 1) * HDIM)
    state = jnp.zeros((HDIM, HDIM), F32)
    through = jnp.ones((1, HDIM), F32)
    for k in range(3):
        a = scale[k][h : h + 1]
        state = jnp.where(k < reached, a * state + parts_ref[k, cut, :].astype(F32), state)
        through = jnp.where(k < reached, a * through, through)
    return state, through


def attend_kernel(
    place_ref, starts_ref, decay_ref, query_ref, intra_ref, other_ref, row_ref, col_ref,
    send_ref, keep_ref, mixed_ref,
):
    odd = place_ref[0] & 1 == 1
    row, col = grid_iotas()
    lower_f = (row >= col).astype(F32)
    cumulative = running_sums(lower_f, decay_ref[...], True)
    segment = segment_of(starts_ref, lax.broadcasted_iota(jnp.int32, (SPAN, 1), 0))
    carry = jnp.exp(cumulative) * (segment == 0).astype(F32)
    row_scale = [decays(row_ref[k, STATE:, :]) for k in range(3)]
    col_scale = [decays(col_ref[k, STATE:, :]) for k in range(3)]
    other_a = decays(other_ref[STATE:, :])
    for h in range(HEADS):
        cut = slice(h * HDIM, (h + 1) * HDIM)
        inner, inner_a = before(row_ref, row_scale, (place_ref[0] >> 1) & 3, h)
        outer, _ = before(col_ref, col_scale, place_ref[0] >> 3, h)
        state = inner_a * outer + inner
        state = jnp.where(odd, other_a[h : h + 1] * state + other_ref[cut, :].astype(F32), state)
        inter = jnp.dot(query_ref[:, cut], state.astype(BF16), preferred_element_type=F32)
        mixed = intra_ref[:, cut] + inter * carry[:, h : h + 1]
        scale = lax.rsqrt(jnp.mean(mixed * mixed, axis=1, keepdims=True) + 1e-06)
        mixed_ref[:, cut] = (mixed * scale).astype(BF16)
    core, chip = place_ref[1] & 1, place_ref[1] >> 1
    for k in range(8):
        start = (chip ^ (k & 3) ^ (0 if k & 4 else 4)) * 32
        cut = slice(k * 16, (k + 1) * 16)
        own, sibling = start + core * 16, start + (1 - core) * 16
        keep_ref[cut, :] = mixed_ref[pl.ds(pl.multiple_of(own, 16), 16), :]
        send_ref[cut, :] = mixed_ref[pl.ds(pl.multiple_of(sibling, 16), 16), :]


def project_kernel(own_ref, other_ref, own_w_ref, other_w_ref, *out_refs):
    total = jnp.dot(own_ref[...], own_w_ref[...], preferred_element_type=F32)
    total = total + jnp.dot(other_ref[...], other_w_ref[...], preferred_element_type=F32)
    for k, ref in enumerate(out_refs):
        ref[...] = total[k * 16 : (k + 1) * 16].astype(ref.dtype)


def sum_kernel(own_ref, a_ref, b_ref, c_ref, out_ref):
    total = own_ref[...] + a_ref[...].astype(F32) + b_ref[...].astype(F32) + c_ref[...].astype(F32)
    out_ref[...] = total.astype(BF16)


def finish_kernel(own_ref, *refs):
    *part_refs, residual_ref, gain_ref, hidden_ref, normed_ref = refs
    hidden = residual_ref[...].astype(F32) + own_ref[...]
    for ref in part_refs:
        hidden = hidden + ref[...].astype(F32)
    scale = lax.rsqrt(jnp.mean(hidden * hidden, axis=1, keepdims=True) + 1e-05)
    hidden_ref[...] = hidden.astype(BF16)
    normed_ref[...] = (hidden * scale * gain_ref[...]).astype(BF16)


def call(body, shapes, specs, *args, scratch=()):
    return pl.pallas_call(
        body,
        out_shape=shapes,
        in_specs=specs,
        out_specs=jax.tree.map(lambda _: VMEM, shapes),
        scratch_shapes=list(scratch),
        compiler_params=pltpu.CompilerParams(vmem_limit_bytes=16 * 1024 * 1024),
    )(*args)


def whole(*shape):
    return pl.BlockSpec(shape, lambda j: (0,) * len(shape))


def of(shape, dtype):
    return jax.ShapeDtypeStruct(shape, dtype)


def shards(
    query_rows, key_rows, value_rows, log_decay, doc_starts, residual_in, out_weight, norm_gain
):
    place = jnp.stack([lax.axis_index("seq"), lax.axis_index("tp")]).astype(jnp.int32)

    local = call(
        state_kernel, of((PAYLOAD, HDIM), BF16), [HBM] * 4,
        *(
            pltpu.with_memory_space_constraint(a, pltpu.HBM)
            for a in (doc_starts, log_decay, key_rows, value_rows)
        ),
        scratch=[
            pltpu.SMEM((1, 3), jnp.int32),
            pltpu.VMEM((HEADS, SPAN), F32),
            pltpu.VMEM((SPAN, STATE), BF16),
            pltpu.VMEM((SPAN, STATE), BF16),
            pltpu.SemaphoreType.DMA((4,)),
        ],
    )
    late_query = lax.optimization_barrier((local, query_rows))[1]
    other = lax.ppermute(local, "seq", FLIP_Z)
    intra = call(
        intra_kernel, of((SPAN, STATE), F32), [SMEM, VMEM, VMEM, VMEM, VMEM],
        doc_starts, log_decay, late_query, key_rows, value_rows,
    )
    late_weight = lax.optimization_barrier((local, out_weight))[1]
    other_weight = lax.ppermute(late_weight, "tp", [(i, i ^ 1) for i in range(16)])
    other, intra = lax.optimization_barrier((other, intra))
    four = of((4, PAYLOAD, HDIM), BF16)
    pairs = call(pair_kernel, four, [SMEM, VMEM, VMEM], place, local, other)
    rows = lax.all_to_all(pairs, "seq", 0, 0, axis_index_groups=ROW_Y)
    totals = call(row_kernel, four, [VMEM], rows)
    cols = lax.all_to_all(totals, "seq", 0, 0, axis_index_groups=ROW_X)
    half = of((SPAN // 2, STATE), BF16)
    send, keep = call(
        attend_kernel, (half, half), [SMEM, SMEM] + [VMEM] * 6,
        place, doc_starts, log_decay, query_rows, intra, other, rows, cols,
        scratch=[pltpu.VMEM((SPAN, STATE), BF16)],
    )
    got = lax.ppermute(send, "tp", [(i, i ^ 1) for i in range(16)])

    full, block = of((16, D), BF16), D // 2
    piece = pl.BlockSpec((STATE, block), lambda j: (0, j))
    halves = []
    for part in range(2):
        rows = pl.BlockSpec((SPAN // 4, STATE), lambda j, part=part: (part, 0))
        own, *parts = pl.pallas_call(
            project_kernel,
            grid=(D // block,),
            in_specs=[rows, rows, piece, piece],
            out_specs=(pl.BlockSpec((16, block), lambda j: (0, j)),) * 4,
            out_shape=(of((16, D), F32), full, full, full),
            compiler_params=pltpu.CompilerParams(vmem_limit_bytes=16 * 1024 * 1024),
        )(keep, got, out_weight, other_weight)
        near = [
            lax.ppermute(sent, "tp", [(i, i ^ (2 * k)) for i in range(16)])
            for k, sent in enumerate(parts, 1)
        ]
        halves.append((own, *near))
    away = call(sum_kernel, full, [VMEM] * 4, *halves[0])
    far = lax.ppermute(away, "tp", [(i, i ^ 8) for i in range(16)])
    return call(
        finish_kernel, (full, full), [VMEM] * 7, *halves[1], far, residual_in, norm_gain[None, :]
    )


def solution(mesh):
    return jax.shard_map(
        shards,
        mesh=mesh,
        in_specs=(
            P("seq", "tp"),
            P("seq", "tp"),
            P("seq", "tp"),
            P("tp", "seq"),
            P("seq", None),
            P(("seq", "tp"), None),
            P("tp", None),
            P(),
        ),
        out_specs=(P(("seq", "tp"), None), P(("seq", "tp"), None)),
        check_vma=False,
    )
```

```python
import jax
import jax.numpy as jnp
from jax import lax
from jax.experimental import pallas as pl
from jax.experimental.pallas import tpu as pltpu
from jax.sharding import PartitionSpec as P

SPAN = 256
HEADS = 3
HDIM = 128
STATE = HEADS * HDIM
PAYLOAD = STATE + 8
D = 4096
F32 = jnp.float32
BF16 = jnp.bfloat16

SHARDS = 32
FLIP_Z = [(i, i ^ 1) for i in range(SHARDS)]
ROW_Y = [[g + 2 * k for k in range(4)] for g in range(SHARDS) if g & 6 == 0]
ROW_X = [[g + 8 * k for k in range(4)] for g in range(8)]
NEAR_CHIPS = [[8 * g + 2 * k + core for k in range(4)] for g in range(2) for core in range(2)]

VMEM = pl.BlockSpec(memory_space=pltpu.VMEM)
HBM = pl.BlockSpec(memory_space=pltpu.HBM)
SMEM = pl.BlockSpec(memory_space=pltpu.SMEM)


def segment_of(starts_ref, positions):
    total = jnp.zeros(positions.shape, jnp.int32)
    for slot in range(3):
        total = total + (positions >= starts_ref[0, slot]).astype(jnp.int32)
    return total


def running_sums(weights, decay, column):
    dims = (((1,), (1,)), ((), ()))
    a, b = (weights, decay) if column else (decay, weights)
    return lax.dot_general(a, b, dims, precision=lax.Precision.HIGHEST, preferred_element_type=F32)


def grid_iotas():
    row = lax.broadcasted_iota(jnp.int32, (SPAN, SPAN), 0)
    col = lax.broadcasted_iota(jnp.int32, (SPAN, SPAN), 1)
    return row, col


def state_kernel(
    starts_hbm, decay_hbm, key_hbm, value_hbm, out_ref,
    starts_ref, decay_ref, key_ref, value_ref, sems,
):
    sources = (decay_hbm, starts_hbm, key_hbm, value_hbm)
    targets = (decay_ref, starts_ref, key_ref, value_ref)
    copies = [
        pltpu.make_async_copy(source, target, sems.at[k])
        for k, (source, target) in enumerate(zip(sources, targets))
    ]
    for copy in copies:
        copy.start()
    row, col = grid_iotas()
    later = (col > row).astype(F32)
    copies[0].wait()
    decay = decay_ref[...]
    tail = running_sums(later, decay, True)
    copies[1].wait()
    segment = segment_of(starts_ref, lax.broadcasted_iota(jnp.int32, (SPAN, 1), 0))
    last = segment_of(starts_ref, jnp.full((1, 1), SPAN - 1, jnp.int32))
    tail_weight = jnp.exp(tail) * (segment == last).astype(F32)
    through = jnp.exp(jnp.sum(decay, axis=1, keepdims=True)) * (last == 0).astype(F32)
    high = through.astype(BF16).astype(F32)
    low = (through - high).astype(BF16).astype(F32)
    rows = jnp.concatenate([high, low, jnp.zeros((2, 1), F32)], axis=0)
    out_ref[STATE:, :] = jnp.broadcast_to(rows, (8, HDIM)).astype(BF16)
    copies[2].wait()
    copies[3].wait()
    for h in range(HEADS):
        cut = slice(h * HDIM, (h + 1) * HDIM)
        decayed = (key_ref[:, cut].astype(F32) * tail_weight[:, h : h + 1]).astype(BF16)
        out_ref[cut, :] = lax.dot_general(
            decayed, value_ref[:, cut], (((0,), (0,)), ((), ())), preferred_element_type=F32
        ).astype(BF16)


def intra_kernel(starts_ref, decay_ref, query_ref, key_ref, value_ref, out_ref):
    row, col = grid_iotas()
    lower = row >= col
    lower_f = lower.astype(F32)
    decay = decay_ref[...]
    cum_col = running_sums(lower_f, decay, True)
    cum_row = running_sums(lower_f, decay, False)
    seg_col = segment_of(starts_ref, lax.broadcasted_iota(jnp.int32, (SPAN, 1), 0))
    seg_row = segment_of(starts_ref, lax.broadcasted_iota(jnp.int32, (1, SPAN), 1))
    same = lower & (seg_col == seg_row)
    for h in range(HEADS):
        cut = slice(h * HDIM, (h + 1) * HDIM)
        spread = cum_col[:, h : h + 1] - cum_row[h : h + 1, :]
        decay_mat = jnp.exp(jnp.where(same, spread, -jnp.inf))
        scores = lax.dot_general(
            query_ref[:, cut], key_ref[:, cut], (((1,), (1,)), ((), ())), preferred_element_type=F32
        )
        weights = (scores * decay_mat).astype(BF16)
        out_ref[:, cut] = jnp.dot(weights, value_ref[:, cut], preferred_element_type=F32)


def decays(rows):
    rows = rows.astype(F32)
    return rows[0:HEADS] + rows[HEADS : 2 * HEADS]


def split_decay(decay):
    high = decay.astype(BF16).astype(F32)
    low = (decay - high).astype(BF16).astype(F32)
    return jnp.concatenate([high, low, jnp.zeros((2, HDIM), F32)], axis=0).astype(BF16)


def pair_kernel(place_ref, own_ref, other_ref, out_ref):
    odd = place_ref[0] & 1 == 1
    own_a, other_a = decays(own_ref[STATE:, :]), decays(other_ref[STATE:, :])
    later_a = jnp.where(odd, own_a, other_a)
    scales = split_decay(own_a * other_a)
    for k in range(4):
        out_ref[k, STATE:, :] = scales
    for h in range(HEADS):
        cut = slice(h * HDIM, (h + 1) * HDIM)
        own, other = own_ref[cut, :].astype(F32), other_ref[cut, :].astype(F32)
        first, second = jnp.where(odd, other, own), jnp.where(odd, own, other)
        total = (later_a[h : h + 1] * first + second).astype(BF16)
        for k in range(4):
            out_ref[k, cut, :] = total


def row_kernel(parts_ref, out_ref):
    scale = [decays(parts_ref[k, STATE:, :]) for k in range(4)]
    scales = split_decay(scale[0] * scale[1] * scale[2] * scale[3])
    for k in range(4):
        out_ref[k, STATE:, :] = scales
    for h in range(HEADS):
        cut = slice(h * HDIM, (h + 1) * HDIM)
        total = parts_ref[0, cut, :].astype(F32)
        for k in range(1, 4):
            total = scale[k][h : h + 1] * total + parts_ref[k, cut, :].astype(F32)
        total = total.astype(BF16)
        for k in range(4):
            out_ref[k, cut, :] = total


def before(parts_ref, scale, reached, h):
    cut = slice(h * HDIM, (h + 1) * HDIM)
    state = jnp.zeros((HDIM, HDIM), F32)
    through = jnp.ones((1, HDIM), F32)
    for k in range(3):
        a = scale[k][h : h + 1]
        state = jnp.where(k < reached, a * state + parts_ref[k, cut, :].astype(F32), state)
        through = jnp.where(k < reached, a * through, through)
    return state, through


def attend_kernel(
    place_ref, starts_ref, decay_ref, query_ref, intra_ref, other_ref, row_ref, col_ref,
    send_ref, keep_ref, mixed_ref,
):
    odd = place_ref[0] & 1 == 1
    row, col = grid_iotas()
    lower_f = (row >= col).astype(F32)
    cumulative = running_sums(lower_f, decay_ref[...], True)
    segment = segment_of(starts_ref, lax.broadcasted_iota(jnp.int32, (SPAN, 1), 0))
    carry = jnp.exp(cumulative) * (segment == 0).astype(F32)
    row_scale = [decays(row_ref[k, STATE:, :]) for k in range(3)]
    col_scale = [decays(col_ref[k, STATE:, :]) for k in range(3)]
    other_a = decays(other_ref[STATE:, :])
    for h in range(HEADS):
        cut = slice(h * HDIM, (h + 1) * HDIM)
        inner, inner_a = before(row_ref, row_scale, (place_ref[0] >> 1) & 3, h)
        outer, _ = before(col_ref, col_scale, place_ref[0] >> 3, h)
        state = inner_a * outer + inner
        state = jnp.where(odd, other_a[h : h + 1] * state + other_ref[cut, :].astype(F32), state)
        inter = jnp.dot(query_ref[:, cut], state.astype(BF16), preferred_element_type=F32)
        mixed = intra_ref[:, cut] + inter * carry[:, h : h + 1]
        scale = lax.rsqrt(jnp.mean(mixed * mixed, axis=1, keepdims=True) + 1e-06)
        mixed_ref[:, cut] = (mixed * scale).astype(BF16)
    core, chip = place_ref[1] & 1, place_ref[1] >> 1
    for k in range(8):
        start = (chip ^ (k & 3) if k & 4 else ((chip & 4) ^ 4) + k) * 32
        cut = slice(k * 16, (k + 1) * 16)
        own, sibling = start + core * 16, start + (1 - core) * 16
        keep_ref[cut, :] = mixed_ref[pl.ds(pl.multiple_of(own, 16), 16), :]
        send_ref[cut, :] = mixed_ref[pl.ds(pl.multiple_of(sibling, 16), 16), :]


def base_kernel(own_ref, weight_ref, out_ref):
    out_ref[...] = jnp.dot(own_ref[...], weight_ref[...], preferred_element_type=F32)


def far_project_kernel(base_ref, other_ref, weight_ref, out_ref):
    total = jnp.dot(other_ref[...], weight_ref[...], preferred_element_type=F32)
    total = (total + base_ref[...]).astype(BF16)
    for k in range(4):
        out_ref[k] = total[k * 16 : (k + 1) * 16]


def near_project_kernel(base_ref, other_ref, weight_ref, *out_refs):
    total = jnp.dot(other_ref[...], weight_ref[...], preferred_element_type=F32)
    total = total + base_ref[...]
    for k, ref in enumerate(out_refs):
        ref[...] = total[k * 16 : (k + 1) * 16].astype(ref.dtype)


def sum_kernel(parts_ref, out_ref):
    total = parts_ref[0].astype(F32)
    for k in range(1, 4):
        total = total + parts_ref[k].astype(F32)
    out_ref[...] = total.astype(BF16)


def finish_kernel(own_ref, *refs):
    *part_refs, residual_ref, gain_ref, hidden_ref, normed_ref = refs
    hidden = residual_ref[...].astype(F32) + own_ref[...]
    for ref in part_refs:
        hidden = hidden + ref[...].astype(F32)
    scale = lax.rsqrt(jnp.mean(hidden * hidden, axis=1, keepdims=True) + 1e-05)
    hidden_ref[...] = hidden.astype(BF16)
    normed_ref[...] = (hidden * scale * gain_ref[...]).astype(BF16)


def call(body, shapes, specs, *args, scratch=()):
    return pl.pallas_call(
        body,
        out_shape=shapes,
        in_specs=specs,
        out_specs=jax.tree.map(lambda _: VMEM, shapes),
        scratch_shapes=list(scratch),
        compiler_params=pltpu.CompilerParams(vmem_limit_bytes=16 * 1024 * 1024),
    )(*args)


def whole(*shape):
    return pl.BlockSpec(shape, lambda j: (0,) * len(shape))


def blocked(body, shapes, specs, out_specs, *args):
    return pl.pallas_call(
        body,
        grid=(2,),
        in_specs=specs,
        out_specs=out_specs,
        out_shape=shapes,
        compiler_params=pltpu.CompilerParams(vmem_limit_bytes=16 * 1024 * 1024),
    )(*args)


def of(shape, dtype):
    return jax.ShapeDtypeStruct(shape, dtype)


def shards(
    query_rows, key_rows, value_rows, log_decay, doc_starts, residual_in, out_weight, norm_gain
):
    place = jnp.stack([lax.axis_index("seq"), lax.axis_index("tp")]).astype(jnp.int32)

    local = call(
        state_kernel, of((PAYLOAD, HDIM), BF16), [HBM] * 4,
        *(
            pltpu.with_memory_space_constraint(a, pltpu.HBM)
            for a in (doc_starts, log_decay, key_rows, value_rows)
        ),
        scratch=[
            pltpu.SMEM((1, 3), jnp.int32),
            pltpu.VMEM((HEADS, SPAN), F32),
            pltpu.VMEM((SPAN, STATE), BF16),
            pltpu.VMEM((SPAN, STATE), BF16),
            pltpu.SemaphoreType.DMA((4,)),
        ],
    )
    late_query = lax.optimization_barrier((local, query_rows))[1]
    other = lax.ppermute(local, "seq", FLIP_Z)
    intra = call(
        intra_kernel, of((SPAN, STATE), F32), [SMEM, VMEM, VMEM, VMEM, VMEM],
        doc_starts, log_decay, late_query, key_rows, value_rows,
    )
    late_weight = lax.optimization_barrier((local, out_weight))[1]
    other_weight = lax.ppermute(late_weight, "tp", [(i, i ^ 1) for i in range(16)])
    other, intra = lax.optimization_barrier((other, intra))
    four = of((4, PAYLOAD, HDIM), BF16)
    pairs = call(pair_kernel, four, [SMEM, VMEM, VMEM], place, local, other)
    rows = lax.all_to_all(pairs, "seq", 0, 0, axis_index_groups=ROW_Y)
    totals = call(row_kernel, four, [VMEM], rows)
    cols = lax.all_to_all(totals, "seq", 0, 0, axis_index_groups=ROW_X)
    half = of((SPAN // 2, STATE), BF16)
    send, keep = call(
        attend_kernel, (half, half), [SMEM, SMEM] + [VMEM] * 6,
        place, doc_starts, log_decay, query_rows, intra, other, rows, cols,
        scratch=[pltpu.VMEM((SPAN, STATE), BF16)],
    )
    got = lax.ppermute(send, "tp", [(i, i ^ 1) for i in range(16)])

    block = D // 2
    full = of((16, D), BF16)
    piece = pl.BlockSpec((STATE, block), lambda j: (0, j))
    base = blocked(
        base_kernel, of((SPAN // 2, D), F32), [whole(SPAN // 2, STATE), piece],
        pl.BlockSpec((SPAN // 2, block), lambda j: (0, j)), keep, out_weight,
    )

    def inputs(part):
        return [
            pl.BlockSpec((SPAN // 4, block), lambda j: (part, j)),
            pl.BlockSpec((SPAN // 4, STATE), lambda j: (part, 0)),
            piece,
        ]

    away = blocked(
        far_project_kernel, of((4, 16, D), BF16), inputs(0),
        pl.BlockSpec((4, 16, block), lambda j: (0, 0, j)), base, got, other_weight,
    )
    away = lax.all_to_all(away, "tp", 0, 0, axis_index_groups=NEAR_CHIPS)
    own, *parts = blocked(
        near_project_kernel, (of((16, D), F32), full, full, full), inputs(1),
        (pl.BlockSpec((16, block), lambda j: (0, j)),) * 4, base, got, other_weight,
    )
    near = [
        lax.ppermute(sent, "tp", [(i, i ^ (2 * k)) for i in range(16)])
        for k, sent in enumerate(parts, 1)
    ]
    away = call(sum_kernel, full, [VMEM], away)
    far = lax.ppermute(away, "tp", [(i, i ^ 8) for i in range(16)])
    return call(
        finish_kernel, (full, full), [VMEM] * 7, own, *near, far, residual_in, norm_gain[None, :]
    )


def solution(mesh):
    return jax.shard_map(
        shards,
        mesh=mesh,
        in_specs=(
            P("seq", "tp"),
            P("seq", "tp"),
            P("seq", "tp"),
            P("tp", "seq"),
            P("seq", None),
            P(("seq", "tp"), None),
            P("tp", None),
            P(),
        ),
        out_specs=(P(("seq", "tp"), None), P(("seq", "tp"), None)),
        check_vma=False,
    )
```

```python
import jax
import jax.numpy as jnp
from jax import lax
from jax.experimental import pallas as pl
from jax.experimental.pallas import tpu as pltpu
from jax.sharding import PartitionSpec as P

SPAN = 256
HEADS = 3
HDIM = 128
STATE = HEADS * HDIM
PAYLOAD = STATE + 8
D = 4096
F32 = jnp.float32
BF16 = jnp.bfloat16

SHARDS = 32
FLIP_Z = [(i, i ^ 1) for i in range(SHARDS)]
ROW_Y = [[g + 2 * k for k in range(4)] for g in range(SHARDS) if g & 6 == 0]
ROW_X = [[g + 8 * k for k in range(4)] for g in range(8)]
NEAR_CHIPS = [[8 * g + 2 * k + core for k in range(4)] for g in range(2) for core in range(2)]

VMEM = pl.BlockSpec(memory_space=pltpu.VMEM)
HBM = pl.BlockSpec(memory_space=pltpu.HBM)
SMEM = pl.BlockSpec(memory_space=pltpu.SMEM)


def segment_of(starts_ref, positions):
    total = jnp.zeros(positions.shape, jnp.int32)
    for slot in range(3):
        total = total + (positions >= starts_ref[0, slot]).astype(jnp.int32)
    return total


def running_sums(weights, decay, column):
    dims = (((1,), (1,)), ((), ()))
    a, b = (weights, decay) if column else (decay, weights)
    return lax.dot_general(a, b, dims, precision=lax.Precision.HIGHEST, preferred_element_type=F32)


def grid_iotas():
    row = lax.broadcasted_iota(jnp.int32, (SPAN, SPAN), 0)
    col = lax.broadcasted_iota(jnp.int32, (SPAN, SPAN), 1)
    return row, col


def state_kernel(
    starts_hbm, decay_hbm, key_hbm, value_hbm, out_ref,
    starts_ref, decay_ref, key_ref, value_ref, sems,
):
    sources = (decay_hbm, starts_hbm, key_hbm, value_hbm)
    targets = (decay_ref, starts_ref, key_ref, value_ref)
    copies = [
        pltpu.make_async_copy(source, target, sems.at[k])
        for k, (source, target) in enumerate(zip(sources, targets))
    ]
    for copy in copies:
        copy.start()
    row, col = grid_iotas()
    later = (col > row).astype(F32)
    copies[0].wait()
    decay = decay_ref[...]
    tail = running_sums(later, decay, True)
    copies[1].wait()
    segment = segment_of(starts_ref, lax.broadcasted_iota(jnp.int32, (SPAN, 1), 0))
    last = segment_of(starts_ref, jnp.full((1, 1), SPAN - 1, jnp.int32))
    tail_weight = jnp.exp(tail) * (segment == last).astype(F32)
    through = jnp.exp(jnp.sum(decay, axis=1, keepdims=True)) * (last == 0).astype(F32)
    high = through.astype(BF16).astype(F32)
    low = (through - high).astype(BF16).astype(F32)
    rows = jnp.concatenate([high, low, jnp.zeros((2, 1), F32)], axis=0)
    out_ref[STATE:, :] = jnp.broadcast_to(rows, (8, HDIM)).astype(BF16)
    copies[2].wait()
    copies[3].wait()
    for h in range(HEADS):
        cut = slice(h * HDIM, (h + 1) * HDIM)
        decayed = (key_ref[:, cut].astype(F32) * tail_weight[:, h : h + 1]).astype(BF16)
        out_ref[cut, :] = lax.dot_general(
            decayed, value_ref[:, cut], (((0,), (0,)), ((), ())), preferred_element_type=F32
        ).astype(BF16)


def intra_kernel(starts_ref, decay_ref, query_ref, key_ref, value_ref, out_ref):
    row, col = grid_iotas()
    lower = row >= col
    lower_f = lower.astype(F32)
    decay = decay_ref[...]
    cum_col = running_sums(lower_f, decay, True)
    cum_row = running_sums(lower_f, decay, False)
    seg_col = segment_of(starts_ref, lax.broadcasted_iota(jnp.int32, (SPAN, 1), 0))
    seg_row = segment_of(starts_ref, lax.broadcasted_iota(jnp.int32, (1, SPAN), 1))
    same = lower & (seg_col == seg_row)
    for h in range(HEADS):
        cut = slice(h * HDIM, (h + 1) * HDIM)
        spread = cum_col[:, h : h + 1] - cum_row[h : h + 1, :]
        decay_mat = jnp.exp(jnp.where(same, spread, -jnp.inf))
        scores = lax.dot_general(
            query_ref[:, cut], key_ref[:, cut], (((1,), (1,)), ((), ())), preferred_element_type=F32
        )
        weights = (scores * decay_mat).astype(BF16)
        out_ref[:, cut] = jnp.dot(weights, value_ref[:, cut], preferred_element_type=F32)


def decays(rows):
    rows = rows.astype(F32)
    return rows[0:HEADS] + rows[HEADS : 2 * HEADS]


def split_decay(decay):
    high = decay.astype(BF16).astype(F32)
    low = (decay - high).astype(BF16).astype(F32)
    return jnp.concatenate([high, low, jnp.zeros((2, HDIM), F32)], axis=0).astype(BF16)


def pair_kernel(place_ref, own_ref, other_ref, out_ref):
    odd = place_ref[0] & 1 == 1
    own_a, other_a = decays(own_ref[STATE:, :]), decays(other_ref[STATE:, :])
    later_a = jnp.where(odd, own_a, other_a)
    scales = split_decay(own_a * other_a)
    for k in range(4):
        out_ref[k, STATE:, :] = scales
    for h in range(HEADS):
        cut = slice(h * HDIM, (h + 1) * HDIM)
        own, other = own_ref[cut, :].astype(F32), other_ref[cut, :].astype(F32)
        first, second = jnp.where(odd, other, own), jnp.where(odd, own, other)
        total = (later_a[h : h + 1] * first + second).astype(BF16)
        for k in range(4):
            out_ref[k, cut, :] = total


def row_kernel(parts_ref, out_ref):
    scale = [decays(parts_ref[k, STATE:, :]) for k in range(4)]
    scales = split_decay(scale[0] * scale[1] * scale[2] * scale[3])
    for k in range(4):
        out_ref[k, STATE:, :] = scales
    for h in range(HEADS):
        cut = slice(h * HDIM, (h + 1) * HDIM)
        total = parts_ref[0, cut, :].astype(F32)
        for k in range(1, 4):
            total = scale[k][h : h + 1] * total + parts_ref[k, cut, :].astype(F32)
        total = total.astype(BF16)
        for k in range(4):
            out_ref[k, cut, :] = total


def before(parts_ref, scale, reached, h):
    cut = slice(h * HDIM, (h + 1) * HDIM)
    state = jnp.zeros((HDIM, HDIM), F32)
    through = jnp.ones((1, HDIM), F32)
    for k in range(3):
        a = scale[k][h : h + 1]
        state = jnp.where(k < reached, a * state + parts_ref[k, cut, :].astype(F32), state)
        through = jnp.where(k < reached, a * through, through)
    return state, through


def attend_kernel(
    place_ref, starts_ref, decay_ref, query_ref, intra_ref, other_ref, row_ref, col_ref,
    weight_ref, send_ref, keep_ref, mixed_ref, sibling_ref,
):
    odd = place_ref[0] & 1 == 1
    row, col = grid_iotas()
    lower_f = (row >= col).astype(F32)
    cumulative = running_sums(lower_f, decay_ref[...], True)
    segment = segment_of(starts_ref, lax.broadcasted_iota(jnp.int32, (SPAN, 1), 0))
    carry = jnp.exp(cumulative) * (segment == 0).astype(F32)
    row_scale = [decays(row_ref[k, STATE:, :]) for k in range(3)]
    col_scale = [decays(col_ref[k, STATE:, :]) for k in range(3)]
    other_a = decays(other_ref[STATE:, :])
    for h in range(HEADS):
        cut = slice(h * HDIM, (h + 1) * HDIM)
        inner, inner_a = before(row_ref, row_scale, (place_ref[0] >> 1) & 3, h)
        outer, _ = before(col_ref, col_scale, place_ref[0] >> 3, h)
        state = inner_a * outer + inner
        state = jnp.where(odd, other_a[h : h + 1] * state + other_ref[cut, :].astype(F32), state)
        inter = jnp.dot(query_ref[:, cut], state.astype(BF16), preferred_element_type=F32)
        mixed = intra_ref[:, cut] + inter * carry[:, h : h + 1]
        scale = lax.rsqrt(jnp.mean(mixed * mixed, axis=1, keepdims=True) + 1e-06)
        mixed_ref[:, cut] = (mixed * scale).astype(BF16)
    core, chip = place_ref[1] & 1, place_ref[1] >> 1
    for k in range(8):
        start = (chip ^ (k & 3) if k & 4 else ((chip & 4) ^ 4) + k) * 32
        cut = slice(k * 16, (k + 1) * 16)
        own, sibling = start + core * 16, start + (1 - core) * 16
        keep_ref[cut, :] = mixed_ref[pl.ds(pl.multiple_of(own, 16), 16), :]
        sibling_ref[cut, :] = mixed_ref[pl.ds(pl.multiple_of(sibling, 16), 16), :]
    send_ref[...] = jnp.dot(
        sibling_ref[...], weight_ref[...], preferred_element_type=F32
    ).astype(BF16)


def keep_kernel(own_ref, weight_ref, out_ref):
    out_ref[...] = jnp.dot(own_ref[...], weight_ref[...], preferred_element_type=F32)


def far_kernel(keep_ref, got_ref, out_ref, sum_ref, sems):
    copies = []
    for k in range(4):
        cut = slice(k * 16, (k + 1) * 16)
        sum_ref[k] = (keep_ref[cut, :] + got_ref[cut, :].astype(F32)).astype(BF16)
        copies.append(pltpu.make_async_copy(sum_ref.at[k], out_ref.at[k], sems.at[k]))
        copies[-1].start()
    for copy in copies:
        copy.wait()


def near_kernel(keep_ref, got_ref, *out_refs):
    for k, ref in enumerate(out_refs):
        cut = slice(64 + k * 16, 80 + k * 16)
        ref[...] = (keep_ref[cut, :] + got_ref[cut, :].astype(F32)).astype(ref.dtype)


def sum_kernel(parts_ref, out_ref):
    total = parts_ref[0].astype(F32)
    for k in range(1, 4):
        total = total + parts_ref[k].astype(F32)
    out_ref[...] = total.astype(BF16)


def finish_kernel(own_ref, *refs):
    *part_refs, residual_ref, gain_ref, hidden_ref, normed_ref = refs
    hidden = residual_ref[...].astype(F32) + own_ref[...]
    for ref in part_refs:
        hidden = hidden + ref[...].astype(F32)
    scale = lax.rsqrt(jnp.mean(hidden * hidden, axis=1, keepdims=True) + 1e-05)
    hidden_ref[...] = hidden.astype(BF16)
    normed_ref[...] = (hidden * scale * gain_ref[...]).astype(BF16)


def call(body, shapes, specs, *args, scratch=(), outs=VMEM):
    return pl.pallas_call(
        body,
        out_shape=shapes,
        in_specs=specs,
        out_specs=jax.tree.map(lambda _: outs, shapes),
        scratch_shapes=list(scratch),
        compiler_params=pltpu.CompilerParams(vmem_limit_bytes=16 * 1024 * 1024),
    )(*args)


def of(shape, dtype):
    return jax.ShapeDtypeStruct(shape, dtype)


def shards(
    query_rows, key_rows, value_rows, log_decay, doc_starts, residual_in, out_weight, norm_gain
):
    place = jnp.stack([lax.axis_index("seq"), lax.axis_index("tp")]).astype(jnp.int32)

    local = call(
        state_kernel, of((PAYLOAD, HDIM), BF16), [HBM] * 4,
        *(
            pltpu.with_memory_space_constraint(a, pltpu.HBM)
            for a in (doc_starts, log_decay, key_rows, value_rows)
        ),
        scratch=[
            pltpu.SMEM((1, 3), jnp.int32),
            pltpu.VMEM((HEADS, SPAN), F32),
            pltpu.VMEM((SPAN, STATE), BF16),
            pltpu.VMEM((SPAN, STATE), BF16),
            pltpu.SemaphoreType.DMA((4,)),
        ],
    )
    late_query = lax.optimization_barrier((local, query_rows))[1]
    other = lax.ppermute(local, "seq", FLIP_Z)
    intra = call(
        intra_kernel, of((SPAN, STATE), F32), [SMEM, VMEM, VMEM, VMEM, VMEM],
        doc_starts, log_decay, late_query, key_rows, value_rows,
    )
    other, intra = lax.optimization_barrier((other, intra))
    four = of((4, PAYLOAD, HDIM), BF16)
    pairs = call(pair_kernel, four, [SMEM, VMEM, VMEM], place, local, other)
    rows = lax.all_to_all(pairs, "seq", 0, 0, axis_index_groups=ROW_Y)
    totals = call(row_kernel, four, [VMEM], rows)
    cols = lax.all_to_all(totals, "seq", 0, 0, axis_index_groups=ROW_X)
    send, keep = call(
        attend_kernel, (of((SPAN // 2, D), BF16), of((SPAN // 2, STATE), BF16)),
        [SMEM, SMEM] + [VMEM] * 7,
        place, doc_starts, log_decay, query_rows, intra, other, rows, cols, out_weight,
        scratch=[pltpu.VMEM((SPAN, STATE), BF16), pltpu.VMEM((SPAN // 2, STATE), BF16)],
    )
    got = lax.ppermute(send, "tp", [(i, i ^ 1) for i in range(16)])
    keep = call(keep_kernel, of((SPAN // 2, D), F32), [VMEM, VMEM], keep, out_weight)
    full = of((16, D), BF16)
    away = call(
        far_kernel, pltpu.HBM((4, 16, D), BF16), [VMEM, VMEM], keep, got,
        scratch=[pltpu.VMEM((4, 16, D), BF16), pltpu.SemaphoreType.DMA((4,))], outs=HBM,
    )
    away = lax.all_to_all(away, "tp", 0, 0, axis_index_groups=NEAR_CHIPS)
    own, *parts = call(
        near_kernel, (of((16, D), F32), full, full, full), [VMEM, VMEM], keep, got
    )
    near = [
        lax.ppermute(sent, "tp", [(i, i ^ (2 * k)) for i in range(16)])
        for k, sent in enumerate(parts, 1)
    ]
    away = call(sum_kernel, full, [VMEM], away)
    far = lax.ppermute(away, "tp", [(i, i ^ 8) for i in range(16)])
    return call(
        finish_kernel, (full, full), [VMEM] * 7, own, *near, far, residual_in, norm_gain[None, :]
    )


def solution(mesh):
    return jax.shard_map(
        shards,
        mesh=mesh,
        in_specs=(
            P("seq", "tp"),
            P("seq", "tp"),
            P("seq", "tp"),
            P("tp", "seq"),
            P("seq", None),
            P(("seq", "tp"), None),
            P("tp", None),
            P(),
        ),
        out_specs=(P(("seq", "tp"), None), P(("seq", "tp"), None)),
        check_vma=False,
    )
```

```python
import jax
import jax.numpy as jnp
from jax import lax
from jax.experimental import pallas as pl
from jax.experimental.pallas import tpu as pltpu
from jax.sharding import PartitionSpec as P

SPAN = 256
HEADS = 3
HDIM = 128
STATE = HEADS * HDIM
PAYLOAD = STATE + 8
D = 4096
F32 = jnp.float32
BF16 = jnp.bfloat16

SHARDS = 32
FLIP_Z = [(i, i ^ 1) for i in range(SHARDS)]
ROW_Y = [[g + 2 * k for k in range(4)] for g in range(SHARDS) if g & 6 == 0]
ROW_X = [[g + 8 * k for k in range(4)] for g in range(8)]
NEAR_CHIPS = [[8 * g + 2 * k + core for k in range(4)] for g in range(2) for core in range(2)]
NEAR_ORDER = (0, 2, 1, 3)

VMEM = pl.BlockSpec(memory_space=pltpu.VMEM)
HBM = pl.BlockSpec(memory_space=pltpu.HBM)
SMEM = pl.BlockSpec(memory_space=pltpu.SMEM)


def segment_of(starts_ref, positions):
    total = jnp.zeros(positions.shape, jnp.int32)
    for slot in range(3):
        total = total + (positions >= starts_ref[0, slot]).astype(jnp.int32)
    return total


def running_sums(weights, decay, column):
    dims = (((1,), (1,)), ((), ()))
    a, b = (weights, decay) if column else (decay, weights)
    return lax.dot_general(a, b, dims, precision=lax.Precision.HIGHEST, preferred_element_type=F32)


def grid_iotas():
    row = lax.broadcasted_iota(jnp.int32, (SPAN, SPAN), 0)
    col = lax.broadcasted_iota(jnp.int32, (SPAN, SPAN), 1)
    return row, col


def state_kernel(
    starts_hbm, decay_hbm, key_hbm, value_hbm, out_ref,
    starts_ref, decay_ref, key_ref, value_ref, sems,
):
    sources = (decay_hbm, starts_hbm, key_hbm, value_hbm)
    targets = (decay_ref, starts_ref, key_ref, value_ref)
    copies = [
        pltpu.make_async_copy(source, target, sems.at[k])
        for k, (source, target) in enumerate(zip(sources, targets))
    ]
    for copy in copies:
        copy.start()
    row, col = grid_iotas()
    later = (col > row).astype(F32)
    copies[0].wait()
    decay = decay_ref[...]
    tail = running_sums(later, decay, True)
    copies[1].wait()
    segment = segment_of(starts_ref, lax.broadcasted_iota(jnp.int32, (SPAN, 1), 0))
    last = segment_of(starts_ref, jnp.full((1, 1), SPAN - 1, jnp.int32))
    tail_weight = jnp.exp(tail) * (segment == last).astype(F32)
    through = jnp.exp(jnp.sum(decay, axis=1, keepdims=True)) * (last == 0).astype(F32)
    high = through.astype(BF16).astype(F32)
    low = (through - high).astype(BF16).astype(F32)
    rows = jnp.concatenate([high, low, jnp.zeros((2, 1), F32)], axis=0)
    out_ref[STATE:, :] = jnp.broadcast_to(rows, (8, HDIM)).astype(BF16)
    copies[2].wait()
    copies[3].wait()
    for h in range(HEADS):
        cut = slice(h * HDIM, (h + 1) * HDIM)
        decayed = (key_ref[:, cut].astype(F32) * tail_weight[:, h : h + 1]).astype(BF16)
        out_ref[cut, :] = lax.dot_general(
            decayed, value_ref[:, cut], (((0,), (0,)), ((), ())), preferred_element_type=F32
        ).astype(BF16)


def intra_kernel(starts_ref, decay_ref, query_ref, key_ref, value_ref, out_ref):
    row, col = grid_iotas()
    lower = row >= col
    lower_f = lower.astype(F32)
    decay = decay_ref[...]
    cum_col = running_sums(lower_f, decay, True)
    cum_row = running_sums(lower_f, decay, False)
    seg_col = segment_of(starts_ref, lax.broadcasted_iota(jnp.int32, (SPAN, 1), 0))
    seg_row = segment_of(starts_ref, lax.broadcasted_iota(jnp.int32, (1, SPAN), 1))
    same = lower & (seg_col == seg_row)
    for h in range(HEADS):
        cut = slice(h * HDIM, (h + 1) * HDIM)
        spread = cum_col[:, h : h + 1] - cum_row[h : h + 1, :]
        decay_mat = jnp.exp(jnp.where(same, spread, -jnp.inf))
        scores = lax.dot_general(
            query_ref[:, cut], key_ref[:, cut], (((1,), (1,)), ((), ())), preferred_element_type=F32
        )
        weights = (scores * decay_mat).astype(BF16)
        out_ref[:, cut] = jnp.dot(weights, value_ref[:, cut], preferred_element_type=F32)


def decays(rows):
    rows = rows.astype(F32)
    return rows[0:HEADS] + rows[HEADS : 2 * HEADS]


def split_decay(decay):
    high = decay.astype(BF16).astype(F32)
    low = (decay - high).astype(BF16).astype(F32)
    return jnp.concatenate([high, low, jnp.zeros((2, HDIM), F32)], axis=0).astype(BF16)


def pair_kernel(place_ref, own_ref, other_ref, out_ref):
    odd = place_ref[0] & 1 == 1
    own_a, other_a = decays(own_ref[STATE:, :]), decays(other_ref[STATE:, :])
    later_a = jnp.where(odd, own_a, other_a)
    scales = split_decay(own_a * other_a)
    for k in range(4):
        out_ref[k, STATE:, :] = scales
    for h in range(HEADS):
        cut = slice(h * HDIM, (h + 1) * HDIM)
        own, other = own_ref[cut, :].astype(F32), other_ref[cut, :].astype(F32)
        first, second = jnp.where(odd, other, own), jnp.where(odd, own, other)
        total = (later_a[h : h + 1] * first + second).astype(BF16)
        for k in range(4):
            out_ref[k, cut, :] = total


def row_kernel(parts_ref, out_ref):
    scale = [decays(parts_ref[k, STATE:, :]) for k in range(4)]
    scales = split_decay(scale[0] * scale[1] * scale[2] * scale[3])
    for k in range(4):
        out_ref[k, STATE:, :] = scales
    for h in range(HEADS):
        cut = slice(h * HDIM, (h + 1) * HDIM)
        total = parts_ref[0, cut, :].astype(F32)
        for k in range(1, 4):
            total = scale[k][h : h + 1] * total + parts_ref[k, cut, :].astype(F32)
        total = total.astype(BF16)
        for k in range(4):
            out_ref[k, cut, :] = total


def before(parts_ref, scale, reached, h):
    cut = slice(h * HDIM, (h + 1) * HDIM)
    state = jnp.zeros((HDIM, HDIM), F32)
    through = jnp.ones((1, HDIM), F32)
    for k in range(3):
        a = scale[k][h : h + 1]
        state = jnp.where(k < reached, a * state + parts_ref[k, cut, :].astype(F32), state)
        through = jnp.where(k < reached, a * through, through)
    return state, through


def attend_kernel(
    place_ref, starts_ref, decay_ref, query_ref, intra_ref, other_ref, row_ref, col_ref,
    weight_ref, send_ref, keep_ref, mixed_ref, sibling_ref,
):
    odd = place_ref[0] & 1 == 1
    row, col = grid_iotas()
    lower_f = (row >= col).astype(F32)
    cumulative = running_sums(lower_f, decay_ref[...], True)
    segment = segment_of(starts_ref, lax.broadcasted_iota(jnp.int32, (SPAN, 1), 0))
    carry = jnp.exp(cumulative) * (segment == 0).astype(F32)
    row_scale = [decays(row_ref[k, STATE:, :]) for k in range(3)]
    col_scale = [decays(col_ref[k, STATE:, :]) for k in range(3)]
    other_a = decays(other_ref[STATE:, :])
    for h in range(HEADS):
        cut = slice(h * HDIM, (h + 1) * HDIM)
        inner, inner_a = before(row_ref, row_scale, (place_ref[0] >> 1) & 3, h)
        outer, _ = before(col_ref, col_scale, place_ref[0] >> 3, h)
        state = inner_a * outer + inner
        state = jnp.where(odd, other_a[h : h + 1] * state + other_ref[cut, :].astype(F32), state)
        inter = jnp.dot(query_ref[:, cut], state.astype(BF16), preferred_element_type=F32)
        mixed = intra_ref[:, cut] + inter * carry[:, h : h + 1]
        scale = lax.rsqrt(jnp.mean(mixed * mixed, axis=1, keepdims=True) + 1e-06)
        mixed_ref[:, cut] = (mixed * scale).astype(BF16)
    core, chip = place_ref[1] & 1, place_ref[1] >> 1
    for k in range(8):
        start = (chip ^ NEAR_ORDER[k - 4] if k & 4 else ((chip & 4) ^ 4) + k) * 32
        cut = slice(k * 16, (k + 1) * 16)
        own, sibling = start + core * 16, start + (1 - core) * 16
        keep_ref[cut, :] = mixed_ref[pl.ds(pl.multiple_of(own, 16), 16), :]
        sibling_ref[cut, :] = mixed_ref[pl.ds(pl.multiple_of(sibling, 16), 16), :]
    send_ref[...] = jnp.dot(
        sibling_ref[...], weight_ref[...], preferred_element_type=F32
    ).astype(BF16)


def keep_kernel(own_ref, weight_ref, out_ref):
    out_ref[...] = jnp.dot(own_ref[...], weight_ref[...], preferred_element_type=F32)


def far_kernel(keep_ref, got_ref, out_ref, sum_ref, sems):
    copies = []
    for k in range(4):
        cut = slice(k * 16, (k + 1) * 16)
        sum_ref[k] = (keep_ref[cut, :] + got_ref[cut, :].astype(F32)).astype(BF16)
        copies.append(pltpu.make_async_copy(sum_ref.at[k], out_ref.at[k], sems.at[k]))
        copies[-1].start()
    for copy in copies:
        copy.wait()


def near_kernel(keep_ref, got_ref, own_ref, next_ref, sent_ref):
    def rows(start, stop):
        return keep_ref[start:stop, :] + got_ref[start:stop, :].astype(F32)

    sent_ref[...] = rows(96, 128).astype(BF16)
    own_ref[...] = rows(64, 80)
    next_ref[...] = rows(80, 96)


def next_kernel(next_ref, got_ref, out_ref):
    out_ref[...] = (next_ref[...] + got_ref[16:, :].astype(F32)).astype(BF16)


def sum_kernel(parts_ref, out_ref):
    total = parts_ref[0].astype(F32)
    for k in range(1, 4):
        total = total + parts_ref[k].astype(F32)
    out_ref[...] = total.astype(BF16)


def finish_kernel(
    own_ref, first_ref, far_ref, second_ref, residual_ref, gain_ref, hidden_ref, normed_ref
):
    hidden = residual_ref[...].astype(F32) + own_ref[...] + first_ref[:16, :].astype(F32)
    hidden = hidden + second_ref[...].astype(F32) + far_ref[...].astype(F32)
    scale = lax.rsqrt(jnp.mean(hidden * hidden, axis=1, keepdims=True) + 1e-05)
    hidden_ref[...] = hidden.astype(BF16)
    normed_ref[...] = (hidden * scale * gain_ref[...]).astype(BF16)


def call(body, shapes, specs, *args, scratch=(), outs=VMEM):
    return pl.pallas_call(
        body,
        out_shape=shapes,
        in_specs=specs,
        out_specs=jax.tree.map(lambda _: outs, shapes),
        scratch_shapes=list(scratch),
        compiler_params=pltpu.CompilerParams(vmem_limit_bytes=16 * 1024 * 1024),
    )(*args)


def of(shape, dtype):
    return jax.ShapeDtypeStruct(shape, dtype)


def shards(
    query_rows, key_rows, value_rows, log_decay, doc_starts, residual_in, out_weight, norm_gain
):
    place = jnp.stack([lax.axis_index("seq"), lax.axis_index("tp")]).astype(jnp.int32)

    local = call(
        state_kernel, of((PAYLOAD, HDIM), BF16), [HBM] * 4,
        *(
            pltpu.with_memory_space_constraint(a, pltpu.HBM)
            for a in (doc_starts, log_decay, key_rows, value_rows)
        ),
        scratch=[
            pltpu.SMEM((1, 3), jnp.int32),
            pltpu.VMEM((HEADS, SPAN), F32),
            pltpu.VMEM((SPAN, STATE), BF16),
            pltpu.VMEM((SPAN, STATE), BF16),
            pltpu.SemaphoreType.DMA((4,)),
        ],
    )
    late_query = lax.optimization_barrier((local, query_rows))[1]
    other = lax.ppermute(local, "seq", FLIP_Z)
    intra = call(
        intra_kernel, of((SPAN, STATE), F32), [SMEM, VMEM, VMEM, VMEM, VMEM],
        doc_starts, log_decay, late_query, key_rows, value_rows,
    )
    other, intra = lax.optimization_barrier((other, intra))
    four = of((4, PAYLOAD, HDIM), BF16)
    pairs = call(pair_kernel, four, [SMEM, VMEM, VMEM], place, local, other)
    rows = lax.all_to_all(pairs, "seq", 0, 0, axis_index_groups=ROW_Y)
    totals = call(row_kernel, four, [VMEM], rows)
    cols = lax.all_to_all(totals, "seq", 0, 0, axis_index_groups=ROW_X)
    send, keep = call(
        attend_kernel, (of((SPAN // 2, D), BF16), of((SPAN // 2, STATE), BF16)),
        [SMEM, SMEM] + [VMEM] * 7,
        place, doc_starts, log_decay, query_rows, intra, other, rows, cols, out_weight,
        scratch=[pltpu.VMEM((SPAN, STATE), BF16), pltpu.VMEM((SPAN // 2, STATE), BF16)],
    )
    got = lax.ppermute(send, "tp", [(i, i ^ 1) for i in range(16)])
    keep = call(keep_kernel, of((SPAN // 2, D), F32), [VMEM, VMEM], keep, out_weight)
    full = of((16, D), BF16)
    away = call(
        far_kernel, pltpu.HBM((4, 16, D), BF16), [VMEM, VMEM], keep, got,
        scratch=[pltpu.VMEM((4, 16, D), BF16), pltpu.SemaphoreType.DMA((4,))], outs=HBM,
    )
    away = lax.all_to_all(away, "tp", 0, 0, axis_index_groups=NEAR_CHIPS)
    own, following, sent = call(
        near_kernel, (of((16, D), F32), of((16, D), F32), of((32, D), BF16)), [VMEM, VMEM],
        keep, got,
    )
    first = lax.ppermute(sent, "tp", [(i, i ^ 2) for i in range(16)])
    away = call(sum_kernel, full, [VMEM], away)
    following = call(next_kernel, full, [VMEM, VMEM], following, first)
    second = lax.ppermute(following, "tp", [(i, i ^ 4) for i in range(16)])
    far = lax.ppermute(away, "tp", [(i, i ^ 8) for i in range(16)])
    return call(
        finish_kernel, (full, full), [VMEM] * 6,
        own, first, far, second, residual_in, norm_gain[None, :],
    )


def solution(mesh):
    return jax.shard_map(
        shards,
        mesh=mesh,
        in_specs=(
            P("seq", "tp"),
            P("seq", "tp"),
            P("seq", "tp"),
            P("tp", "seq"),
            P("seq", None),
            P(("seq", "tp"), None),
            P("tp", None),
            P(),
        ),
        out_specs=(P(("seq", "tp"), None), P(("seq", "tp"), None)),
        check_vma=False,
    )
```

```python
import jax
import jax.numpy as jnp
from jax import lax
from jax.experimental import pallas as pl
from jax.experimental.pallas import tpu as pltpu
from jax.sharding import PartitionSpec as P

SPAN = 256
HEADS = 3
HDIM = 128
STATE = HEADS * HDIM
PAYLOAD = STATE + 8
D = 4096
F32 = jnp.float32
BF16 = jnp.bfloat16

SHARDS = 32
FLIP_Z = [(i, i ^ 1) for i in range(SHARDS)]
ROW_Y = [[g + 2 * k for k in range(4)] for g in range(SHARDS) if g & 6 == 0]
ROW_X = [[g + 8 * k for k in range(4)] for g in range(8)]
NEAR_CHIPS = [[8 * g + 2 * k + core for k in range(4)] for g in range(2) for core in range(2)]

VMEM = pl.BlockSpec(memory_space=pltpu.VMEM)
HBM = pl.BlockSpec(memory_space=pltpu.HBM)
SMEM = pl.BlockSpec(memory_space=pltpu.SMEM)


def segment_of(starts_ref, positions):
    total = jnp.zeros(positions.shape, jnp.int32)
    for slot in range(3):
        total = total + (positions >= starts_ref[0, slot]).astype(jnp.int32)
    return total


def running_sums(weights, decay, column):
    dims = (((1,), (1,)), ((), ()))
    a, b = (weights, decay) if column else (decay, weights)
    return lax.dot_general(a, b, dims, precision=lax.Precision.HIGHEST, preferred_element_type=F32)


def grid_iotas():
    row = lax.broadcasted_iota(jnp.int32, (SPAN, SPAN), 0)
    col = lax.broadcasted_iota(jnp.int32, (SPAN, SPAN), 1)
    return row, col


def state_kernel(
    starts_hbm, decay_hbm, key_hbm, value_hbm, out_ref,
    starts_ref, decay_ref, key_ref, value_ref, sems,
):
    sources = (decay_hbm, starts_hbm, key_hbm, value_hbm)
    targets = (decay_ref, starts_ref, key_ref, value_ref)
    copies = [
        pltpu.make_async_copy(source, target, sems.at[k])
        for k, (source, target) in enumerate(zip(sources, targets))
    ]
    for copy in copies:
        copy.start()
    row, col = grid_iotas()
    later = (col > row).astype(F32)
    copies[0].wait()
    decay = decay_ref[...]
    tail = running_sums(later, decay, True)
    copies[1].wait()
    segment = segment_of(starts_ref, lax.broadcasted_iota(jnp.int32, (SPAN, 1), 0))
    last = segment_of(starts_ref, jnp.full((1, 1), SPAN - 1, jnp.int32))
    tail_weight = jnp.exp(tail) * (segment == last).astype(F32)
    through = jnp.exp(jnp.sum(decay, axis=1, keepdims=True)) * (last == 0).astype(F32)
    high = through.astype(BF16).astype(F32)
    low = (through - high).astype(BF16).astype(F32)
    rows = jnp.concatenate([high, low, jnp.zeros((2, 1), F32)], axis=0)
    out_ref[STATE:, :] = jnp.broadcast_to(rows, (8, HDIM)).astype(BF16)
    copies[2].wait()
    copies[3].wait()
    for h in range(HEADS):
        cut = slice(h * HDIM, (h + 1) * HDIM)
        decayed = (key_ref[:, cut].astype(F32) * tail_weight[:, h : h + 1]).astype(BF16)
        out_ref[cut, :] = lax.dot_general(
            decayed, value_ref[:, cut], (((0,), (0,)), ((), ())), preferred_element_type=F32
        ).astype(BF16)


def intra_kernel(
    starts_ref, decay_ref, query_ref, key_ref, value_ref, weight_hbm,
    out_ref, carry_ref, weight_ref, sem,
):
    copy = pltpu.make_async_copy(weight_hbm, weight_ref, sem)
    copy.start()
    row, col = grid_iotas()
    lower = row >= col
    lower_f = lower.astype(F32)
    decay = decay_ref[...]
    cum_col = running_sums(lower_f, decay, True)
    cum_row = running_sums(lower_f, decay, False)
    seg_col = segment_of(starts_ref, lax.broadcasted_iota(jnp.int32, (SPAN, 1), 0))
    seg_row = segment_of(starts_ref, lax.broadcasted_iota(jnp.int32, (1, SPAN), 1))
    same = lower & (seg_col == seg_row)
    carry_ref[...] = jnp.exp(cum_col) * (seg_col == 0).astype(F32)
    for h in range(HEADS):
        cut = slice(h * HDIM, (h + 1) * HDIM)
        spread = cum_col[:, h : h + 1] - cum_row[h : h + 1, :]
        decay_mat = jnp.exp(jnp.where(same, spread, -jnp.inf))
        scores = lax.dot_general(
            query_ref[:, cut], key_ref[:, cut], (((1,), (1,)), ((), ())), preferred_element_type=F32
        )
        weights = (scores * decay_mat).astype(BF16)
        out_ref[:, cut] = jnp.dot(weights, value_ref[:, cut], preferred_element_type=F32)
    copy.wait()


def decays(rows):
    rows = rows.astype(F32)
    return rows[0:HEADS] + rows[HEADS : 2 * HEADS]


def split_decay(decay):
    high = decay.astype(BF16).astype(F32)
    low = (decay - high).astype(BF16).astype(F32)
    return jnp.concatenate([high, low, jnp.zeros((2, HDIM), F32)], axis=0).astype(BF16)


def pair_kernel(place_ref, own_ref, other_ref, out_ref):
    odd = place_ref[0] & 1 == 1
    own_a, other_a = decays(own_ref[STATE:, :]), decays(other_ref[STATE:, :])
    later_a = jnp.where(odd, own_a, other_a)
    scales = split_decay(own_a * other_a)
    for k in range(4):
        out_ref[k, STATE:, :] = scales
    for h in range(HEADS):
        cut = slice(h * HDIM, (h + 1) * HDIM)
        own, other = own_ref[cut, :].astype(F32), other_ref[cut, :].astype(F32)
        first, second = jnp.where(odd, other, own), jnp.where(odd, own, other)
        total = (later_a[h : h + 1] * first + second).astype(BF16)
        for k in range(4):
            out_ref[k, cut, :] = total


def row_kernel(parts_ref, out_ref):
    scale = [decays(parts_ref[k, STATE:, :]) for k in range(4)]
    scales = split_decay(scale[0] * scale[1] * scale[2] * scale[3])
    for k in range(4):
        out_ref[k, STATE:, :] = scales
    for h in range(HEADS):
        cut = slice(h * HDIM, (h + 1) * HDIM)
        total = parts_ref[0, cut, :].astype(F32)
        for k in range(1, 4):
            total = scale[k][h : h + 1] * total + parts_ref[k, cut, :].astype(F32)
        total = total.astype(BF16)
        for k in range(4):
            out_ref[k, cut, :] = total


def before(parts_ref, scale, reached, h):
    cut = slice(h * HDIM, (h + 1) * HDIM)
    state = jnp.zeros((HDIM, HDIM), F32)
    through = jnp.ones((1, HDIM), F32)
    for k in range(3):
        a = scale[k][h : h + 1]
        state = jnp.where(k < reached, a * state + parts_ref[k, cut, :].astype(F32), state)
        through = jnp.where(k < reached, a * through, through)
    return state, through


def attend_kernel(
    place_ref, query_ref, intra_ref, carry_ref, other_ref, row_ref, col_ref, weight_ref,
    send_ref, keep_ref, mixed_ref, sibling_ref,
):
    odd = place_ref[0] & 1 == 1
    carry = carry_ref[...]
    row_scale = [decays(row_ref[k, STATE:, :]) for k in range(3)]
    col_scale = [decays(col_ref[k, STATE:, :]) for k in range(3)]
    other_a = decays(other_ref[STATE:, :])
    for h in range(HEADS):
        cut = slice(h * HDIM, (h + 1) * HDIM)
        inner, inner_a = before(row_ref, row_scale, (place_ref[0] >> 1) & 3, h)
        outer, _ = before(col_ref, col_scale, place_ref[0] >> 3, h)
        state = inner_a * outer + inner
        state = jnp.where(odd, other_a[h : h + 1] * state + other_ref[cut, :].astype(F32), state)
        inter = jnp.dot(query_ref[:, cut], state.astype(BF16), preferred_element_type=F32)
        mixed = intra_ref[:, cut] + inter * carry[:, h : h + 1]
        scale = lax.rsqrt(jnp.mean(mixed * mixed, axis=1, keepdims=True) + 1e-06)
        mixed_ref[:, cut] = (mixed * scale).astype(BF16)
    core, chip = place_ref[1] & 1, place_ref[1] >> 1
    for k in range(8):
        start = (chip ^ (k & 3) if k & 4 else ((chip & 4) ^ 4) + k) * 32
        cut = slice(k * 16, (k + 1) * 16)
        own, sibling = start + core * 16, start + (1 - core) * 16
        keep_ref[cut, :] = mixed_ref[pl.ds(pl.multiple_of(own, 16), 16), :]
        sibling_ref[cut, :] = mixed_ref[pl.ds(pl.multiple_of(sibling, 16), 16), :]
    send_ref[...] = jnp.dot(
        sibling_ref[...], weight_ref[...], preferred_element_type=F32
    ).astype(BF16)


def keep_kernel(own_ref, weight_ref, out_ref):
    out_ref[...] = jnp.dot(own_ref[...], weight_ref[...], preferred_element_type=F32)


def far_kernel(keep_ref, got_ref, out_ref, sum_ref, sems):
    copies = []
    for k in range(4):
        cut = slice(k * 16, (k + 1) * 16)
        sum_ref[k] = (keep_ref[cut, :] + got_ref[cut, :].astype(F32)).astype(BF16)
        copies.append(pltpu.make_async_copy(sum_ref.at[k], out_ref.at[k], sems.at[k]))
        copies[-1].start()
    for copy in copies:
        copy.wait()


def near_kernel(keep_ref, got_ref, *out_refs):
    for k, ref in enumerate(out_refs):
        cut = slice(64 + k * 16, 80 + k * 16)
        ref[...] = (keep_ref[cut, :] + got_ref[cut, :].astype(F32)).astype(ref.dtype)


def sum_kernel(parts_ref, out_ref):
    total = parts_ref[0].astype(F32)
    for k in range(1, 4):
        total = total + parts_ref[k].astype(F32)
    out_ref[...] = total.astype(BF16)


def fold_kernel(own_ref, a_ref, b_ref, c_ref, residual_ref, out_ref):
    total = residual_ref[...].astype(F32) + own_ref[...]
    out_ref[...] = total + a_ref[...].astype(F32) + b_ref[...].astype(F32) + c_ref[...].astype(F32)


def finish_kernel(near_ref, far_ref, gain_ref, hidden_ref, normed_ref):
    hidden = near_ref[...] + far_ref[...].astype(F32)
    scale = lax.rsqrt(jnp.mean(hidden * hidden, axis=1, keepdims=True) + 1e-05)
    hidden_ref[...] = hidden.astype(BF16)
    normed_ref[...] = (hidden * scale * gain_ref[...]).astype(BF16)


def call(body, shapes, specs, *args, scratch=(), outs=VMEM):
    return pl.pallas_call(
        body,
        out_shape=shapes,
        in_specs=specs,
        out_specs=jax.tree.map(lambda _: outs, shapes),
        scratch_shapes=list(scratch),
        compiler_params=pltpu.CompilerParams(vmem_limit_bytes=16 * 1024 * 1024),
    )(*args)


def of(shape, dtype):
    return jax.ShapeDtypeStruct(shape, dtype)


def shards(
    query_rows, key_rows, value_rows, log_decay, doc_starts, residual_in, out_weight, norm_gain
):
    place = jnp.stack([lax.axis_index("seq"), lax.axis_index("tp")]).astype(jnp.int32)

    local = call(
        state_kernel, pltpu.VMEM((PAYLOAD, HDIM), BF16), [HBM] * 4,
        *(
            pltpu.with_memory_space_constraint(a, pltpu.HBM)
            for a in (doc_starts, log_decay, key_rows, value_rows)
        ),
        scratch=[
            pltpu.SMEM((1, 3), jnp.int32),
            pltpu.VMEM((HEADS, SPAN), F32),
            pltpu.VMEM((SPAN, STATE), BF16),
            pltpu.VMEM((SPAN, STATE), BF16),
            pltpu.SemaphoreType.DMA((4,)),
        ],
    )
    late_query = lax.optimization_barrier((local, query_rows))[1]
    other = lax.ppermute(local, "seq", FLIP_Z)
    intra, carry, weight = call(
        intra_kernel,
        (of((SPAN, STATE), F32), of((SPAN, HEADS), F32), pltpu.VMEM((STATE, D), BF16)),
        [SMEM, VMEM, VMEM, VMEM, VMEM, HBM],
        doc_starts, log_decay, late_query, key_rows, value_rows,
        pltpu.with_memory_space_constraint(out_weight, pltpu.HBM),
        scratch=[pltpu.SemaphoreType.DMA],
    )
    other, intra, carry = lax.optimization_barrier((other, intra, carry))
    four = of((4, PAYLOAD, HDIM), BF16)
    pairs = call(pair_kernel, four, [SMEM, VMEM, VMEM], place, local, other)
    rows = lax.all_to_all(pairs, "seq", 0, 0, axis_index_groups=ROW_Y)
    totals = call(row_kernel, four, [VMEM], rows)
    cols = lax.all_to_all(totals, "seq", 0, 0, axis_index_groups=ROW_X)
    send, keep = call(
        attend_kernel, (of((SPAN // 2, D), BF16), of((SPAN // 2, STATE), BF16)),
        [SMEM] + [VMEM] * 7,
        place, query_rows, intra, carry, other, rows, cols, weight,
        scratch=[pltpu.VMEM((SPAN, STATE), BF16), pltpu.VMEM((SPAN // 2, STATE), BF16)],
    )
    got = lax.ppermute(send, "tp", [(i, i ^ 1) for i in range(16)])
    keep = call(keep_kernel, of((SPAN // 2, D), F32), [VMEM, VMEM], keep, weight)
    full = of((16, D), BF16)
    away = call(
        far_kernel, pltpu.HBM((4, 16, D), BF16), [VMEM, VMEM], keep, got,
        scratch=[pltpu.VMEM((4, 16, D), BF16), pltpu.SemaphoreType.DMA((4,))], outs=HBM,
    )
    away = lax.all_to_all(away, "tp", 0, 0, axis_index_groups=NEAR_CHIPS)
    own, *parts = call(
        near_kernel, (of((16, D), F32), full, full, full), [VMEM, VMEM], keep, got
    )
    near = [
        lax.ppermute(sent, "tp", [(i, i ^ (2 * k)) for i in range(16)])
        for k, sent in enumerate(parts, 1)
    ]
    away = call(sum_kernel, full, [VMEM], away)
    far = lax.ppermute(away, "tp", [(i, i ^ 8) for i in range(16)])
    folded = call(fold_kernel, of((16, D), F32), [VMEM] * 5, own, *near, residual_in)
    return call(finish_kernel, (full, full), [VMEM] * 3, folded, far, norm_gain[None, :])


def solution(mesh):
    return jax.shard_map(
        shards,
        mesh=mesh,
        in_specs=(
            P("seq", "tp"),
            P("seq", "tp"),
            P("seq", "tp"),
            P("tp", "seq"),
            P("seq", None),
            P(("seq", "tp"), None),
            P("tp", None),
            P(),
        ),
        out_specs=(P(("seq", "tp"), None), P(("seq", "tp"), None)),
        check_vma=False,
    )
```

```python
import jax
import jax.numpy as jnp
from jax import lax
from jax.experimental import pallas as pl
from jax.experimental.pallas import tpu as pltpu
from jax.sharding import PartitionSpec as P

SPAN = 256
HEADS = 3
HDIM = 128
STATE = HEADS * HDIM
PAYLOAD = STATE + 8
D = 4096
F32 = jnp.float32
BF16 = jnp.bfloat16

SHARDS = 32
FLIP_Z = [(i, i ^ 1) for i in range(SHARDS)]
ROW_Y = [[g + 2 * k for k in range(4)] for g in range(SHARDS) if g & 6 == 0]
ROW_X = [[g + 8 * k for k in range(4)] for g in range(8)]
LONG = pl.CostEstimate(flops=10**11, bytes_accessed=0, transcendentals=0)
NEAR_CHIPS = [[8 * g + 2 * k + core for k in range(4)] for g in range(2) for core in range(2)]

VMEM = pl.BlockSpec(memory_space=pltpu.VMEM)
HBM = pl.BlockSpec(memory_space=pltpu.HBM)
SMEM = pl.BlockSpec(memory_space=pltpu.SMEM)


def segment_of(starts_ref, positions):
    total = jnp.zeros(positions.shape, jnp.int32)
    for slot in range(3):
        total = total + (positions >= starts_ref[0, slot]).astype(jnp.int32)
    return total


def running_sums(weights, decay, column):
    dims = (((1,), (1,)), ((), ()))
    a, b = (weights, decay) if column else (decay, weights)
    return lax.dot_general(a, b, dims, precision=lax.Precision.HIGHEST, preferred_element_type=F32)


def grid_iotas():
    row = lax.broadcasted_iota(jnp.int32, (SPAN, SPAN), 0)
    col = lax.broadcasted_iota(jnp.int32, (SPAN, SPAN), 1)
    return row, col


def state_kernel(
    starts_hbm, decay_hbm, key_hbm, value_hbm, out_ref,
    starts_ref, decay_ref, key_ref, value_ref, sems,
):
    sources = (decay_hbm, starts_hbm, key_hbm, value_hbm)
    targets = (decay_ref, starts_ref, key_ref, value_ref)
    copies = [
        pltpu.make_async_copy(source, target, sems.at[k])
        for k, (source, target) in enumerate(zip(sources, targets))
    ]
    for copy in copies:
        copy.start()
    row, col = grid_iotas()
    later = (col > row).astype(F32)
    copies[0].wait()
    decay = decay_ref[...]
    tail = running_sums(later, decay, True)
    copies[1].wait()
    segment = segment_of(starts_ref, lax.broadcasted_iota(jnp.int32, (SPAN, 1), 0))
    last = segment_of(starts_ref, jnp.full((1, 1), SPAN - 1, jnp.int32))
    tail_weight = jnp.exp(tail) * (segment == last).astype(F32)
    through = jnp.exp(jnp.sum(decay, axis=1, keepdims=True)) * (last == 0).astype(F32)
    high = through.astype(BF16).astype(F32)
    low = (through - high).astype(BF16).astype(F32)
    rows = jnp.concatenate([high, low, jnp.zeros((2, 1), F32)], axis=0)
    out_ref[STATE:, :] = jnp.broadcast_to(rows, (8, HDIM)).astype(BF16)
    copies[2].wait()
    copies[3].wait()
    for h in range(HEADS):
        cut = slice(h * HDIM, (h + 1) * HDIM)
        decayed = (key_ref[:, cut].astype(F32) * tail_weight[:, h : h + 1]).astype(BF16)
        out_ref[cut, :] = lax.dot_general(
            decayed, value_ref[:, cut], (((0,), (0,)), ((), ())), preferred_element_type=F32
        ).astype(BF16)


def intra_kernel(
    starts_ref, decay_ref, query_ref, key_ref, value_ref, weight_hbm,
    out_ref, carry_ref, weight_ref, sem,
):
    copy = pltpu.make_async_copy(weight_hbm, weight_ref, sem)
    copy.start()
    row, col = grid_iotas()
    lower = row >= col
    lower_f = lower.astype(F32)
    decay = decay_ref[...]
    cum_col = running_sums(lower_f, decay, True)
    cum_row = running_sums(lower_f, decay, False)
    seg_col = segment_of(starts_ref, lax.broadcasted_iota(jnp.int32, (SPAN, 1), 0))
    seg_row = segment_of(starts_ref, lax.broadcasted_iota(jnp.int32, (1, SPAN), 1))
    same = lower & (seg_col == seg_row)
    carry_ref[...] = jnp.exp(cum_col) * (seg_col == 0).astype(F32)
    for h in range(HEADS):
        cut = slice(h * HDIM, (h + 1) * HDIM)
        spread = cum_col[:, h : h + 1] - cum_row[h : h + 1, :]
        decay_mat = jnp.exp(jnp.where(same, spread, -jnp.inf))
        scores = lax.dot_general(
            query_ref[:, cut], key_ref[:, cut], (((1,), (1,)), ((), ())), preferred_element_type=F32
        )
        weights = (scores * decay_mat).astype(BF16)
        out_ref[:, cut] = jnp.dot(weights, value_ref[:, cut], preferred_element_type=F32)
    copy.wait()


def decays(rows):
    rows = rows.astype(F32)
    return rows[0:HEADS] + rows[HEADS : 2 * HEADS]


def split_decay(decay):
    high = decay.astype(BF16).astype(F32)
    low = (decay - high).astype(BF16).astype(F32)
    return jnp.concatenate([high, low, jnp.zeros((2, HDIM), F32)], axis=0).astype(BF16)


def pair_kernel(place_ref, own_ref, other_ref, out_ref):
    odd = place_ref[0] & 1 == 1
    own_a, other_a = decays(own_ref[STATE:, :]), decays(other_ref[STATE:, :])
    later_a = jnp.where(odd, own_a, other_a)
    scales = split_decay(own_a * other_a)
    for k in range(4):
        out_ref[k, STATE:, :] = scales
    for h in range(HEADS):
        cut = slice(h * HDIM, (h + 1) * HDIM)
        own, other = own_ref[cut, :].astype(F32), other_ref[cut, :].astype(F32)
        first, second = jnp.where(odd, other, own), jnp.where(odd, own, other)
        total = (later_a[h : h + 1] * first + second).astype(BF16)
        for k in range(4):
            out_ref[k, cut, :] = total


def row_kernel(parts_ref, out_ref):
    scale = [decays(parts_ref[k, STATE:, :]) for k in range(4)]
    scales = split_decay(scale[0] * scale[1] * scale[2] * scale[3])
    for k in range(4):
        out_ref[k, STATE:, :] = scales
    for h in range(HEADS):
        cut = slice(h * HDIM, (h + 1) * HDIM)
        total = parts_ref[0, cut, :].astype(F32)
        for k in range(1, 4):
            total = scale[k][h : h + 1] * total + parts_ref[k, cut, :].astype(F32)
        total = total.astype(BF16)
        for k in range(4):
            out_ref[k, cut, :] = total


def before(parts_ref, scale, reached, h):
    cut = slice(h * HDIM, (h + 1) * HDIM)
    state = jnp.zeros((HDIM, HDIM), F32)
    through = jnp.ones((1, HDIM), F32)
    for k in range(3):
        a = scale[k][h : h + 1]
        state = jnp.where(k < reached, a * state + parts_ref[k, cut, :].astype(F32), state)
        through = jnp.where(k < reached, a * through, through)
    return state, through


def attend_kernel(
    place_ref, query_ref, intra_ref, carry_ref, other_ref, row_ref, col_ref, weight_ref,
    send_ref, keep_ref, mixed_ref, sibling_ref,
):
    odd = place_ref[0] & 1 == 1
    carry = carry_ref[...]
    row_scale = [decays(row_ref[k, STATE:, :]) for k in range(3)]
    col_scale = [decays(col_ref[k, STATE:, :]) for k in range(3)]
    other_a = decays(other_ref[STATE:, :])
    for h in range(HEADS):
        cut = slice(h * HDIM, (h + 1) * HDIM)
        inner, inner_a = before(row_ref, row_scale, (place_ref[0] >> 1) & 3, h)
        outer, _ = before(col_ref, col_scale, place_ref[0] >> 3, h)
        state = inner_a * outer + inner
        state = jnp.where(odd, other_a[h : h + 1] * state + other_ref[cut, :].astype(F32), state)
        inter = jnp.dot(query_ref[:, cut], state.astype(BF16), preferred_element_type=F32)
        mixed = intra_ref[:, cut] + inter * carry[:, h : h + 1]
        scale = lax.rsqrt(jnp.mean(mixed * mixed, axis=1, keepdims=True) + 1e-06)
        mixed_ref[:, cut] = (mixed * scale).astype(BF16)
    core, chip = place_ref[1] & 1, place_ref[1] >> 1
    for k in range(8):
        start = ((chip & 4) + (k & 3) if k & 4 else chip ^ 4 ^ k) * 32
        cut = slice(k * 16, (k + 1) * 16)
        own, sibling = start + core * 16, start + (1 - core) * 16
        keep_ref[cut, :] = mixed_ref[pl.ds(pl.multiple_of(own, 16), 16), :]
        sibling_ref[cut, :] = mixed_ref[pl.ds(pl.multiple_of(sibling, 16), 16), :]
    send_ref[...] = jnp.dot(
        sibling_ref[...], weight_ref[...], preferred_element_type=F32
    ).astype(BF16)


def keep_kernel(own_ref, weight_ref, out_ref):
    out_ref[...] = jnp.dot(own_ref[...], weight_ref[...], preferred_element_type=F32)


def far_kernel(keep_ref, got_ref, *out_refs):
    for k, ref in enumerate(out_refs):
        cut = slice(k * 16, (k + 1) * 16)
        ref[...] = (keep_ref[cut, :] + got_ref[cut, :].astype(F32)).astype(ref.dtype)


def near_kernel(keep_ref, got_ref, out_ref, sum_ref, sems):
    copies = []
    for k in range(4):
        cut = slice(64 + k * 16, 80 + k * 16)
        sum_ref[k] = (keep_ref[cut, :] + got_ref[cut, :].astype(F32)).astype(BF16)
        copies.append(pltpu.make_async_copy(sum_ref.at[k], out_ref.at[k], sems.at[k]))
        copies[-1].start()
    for copy in copies:
        copy.wait()


def sum_kernel(own_ref, a_ref, b_ref, c_ref, out_ref):
    total = own_ref[...] + a_ref[...].astype(F32) + b_ref[...].astype(F32) + c_ref[...].astype(F32)
    out_ref[...] = total.astype(BF16)


def fold_kernel(parts_ref, residual_ref, out_ref):
    total = residual_ref[...].astype(F32)
    for k in range(4):
        total = total + parts_ref[k].astype(F32)
    out_ref[...] = total


def finish_kernel(near_ref, far_ref, gain_ref, hidden_ref, normed_ref):
    hidden = near_ref[...] + far_ref[...].astype(F32)
    scale = lax.rsqrt(jnp.mean(hidden * hidden, axis=1, keepdims=True) + 1e-05)
    hidden_ref[...] = hidden.astype(BF16)
    normed_ref[...] = (hidden * scale * gain_ref[...]).astype(BF16)


def call(body, shapes, specs, *args, scratch=(), outs=VMEM, cost=None):
    return pl.pallas_call(
        body,
        out_shape=shapes,
        in_specs=specs,
        out_specs=jax.tree.map(lambda _: outs, shapes),
        scratch_shapes=list(scratch),
        cost_estimate=cost,
        compiler_params=pltpu.CompilerParams(vmem_limit_bytes=16 * 1024 * 1024),
    )(*args)


def of(shape, dtype):
    return jax.ShapeDtypeStruct(shape, dtype)


def shards(
    query_rows, key_rows, value_rows, log_decay, doc_starts, residual_in, out_weight, norm_gain
):
    place = jnp.stack([lax.axis_index("seq"), lax.axis_index("tp")]).astype(jnp.int32)

    local = call(
        state_kernel, pltpu.VMEM((PAYLOAD, HDIM), BF16), [HBM] * 4,
        *(
            pltpu.with_memory_space_constraint(a, pltpu.HBM)
            for a in (doc_starts, log_decay, key_rows, value_rows)
        ),
        scratch=[
            pltpu.SMEM((1, 3), jnp.int32),
            pltpu.VMEM((HEADS, SPAN), F32),
            pltpu.VMEM((SPAN, STATE), BF16),
            pltpu.VMEM((SPAN, STATE), BF16),
            pltpu.SemaphoreType.DMA((4,)),
        ],
    )
    late_query = lax.optimization_barrier((local, query_rows))[1]
    other = lax.ppermute(local, "seq", FLIP_Z)
    intra, carry, weight = call(
        intra_kernel,
        (of((SPAN, STATE), F32), of((SPAN, HEADS), F32), pltpu.VMEM((STATE, D), BF16)),
        [SMEM, VMEM, VMEM, VMEM, VMEM, HBM],
        doc_starts, log_decay, late_query, key_rows, value_rows,
        pltpu.with_memory_space_constraint(out_weight, pltpu.HBM),
        scratch=[pltpu.SemaphoreType.DMA],
    )
    other, intra, carry = lax.optimization_barrier((other, intra, carry))
    four = of((4, PAYLOAD, HDIM), BF16)
    pairs = call(pair_kernel, four, [SMEM, VMEM, VMEM], place, local, other)
    rows = lax.all_to_all(pairs, "seq", 0, 0, axis_index_groups=ROW_Y)
    totals = call(row_kernel, four, [VMEM], rows)
    cols = lax.all_to_all(totals, "seq", 0, 0, axis_index_groups=ROW_X)
    send, keep = call(
        attend_kernel, (of((SPAN // 2, D), BF16), of((SPAN // 2, STATE), BF16)),
        [SMEM] + [VMEM] * 7,
        place, query_rows, intra, carry, other, rows, cols, weight,
        scratch=[pltpu.VMEM((SPAN, STATE), BF16), pltpu.VMEM((SPAN // 2, STATE), BF16)],
    )
    got = lax.ppermute(send, "tp", [(i, i ^ 1) for i in range(16)])
    keep = call(keep_kernel, of((SPAN // 2, D), F32), [VMEM, VMEM], keep, weight)
    full = of((16, D), BF16)
    own, *parts = call(
        far_kernel, (of((16, D), F32), full, full, full), [VMEM, VMEM], keep, got
    )
    parts = [
        lax.ppermute(sent, "tp", [(i, i ^ (2 * k)) for i in range(16)])
        for k, sent in enumerate(parts, 1)
    ]
    near = call(
        near_kernel, pltpu.HBM((4, 16, D), BF16), [VMEM, VMEM], keep, got,
        scratch=[pltpu.VMEM((4, 16, D), BF16), pltpu.SemaphoreType.DMA((4,))], outs=HBM,
    )
    near = lax.all_to_all(near, "tp", 0, 0, axis_index_groups=NEAR_CHIPS)
    away = call(sum_kernel, full, [VMEM] * 4, own, *parts, cost=LONG)
    far = lax.ppermute(away, "tp", [(i, i ^ 8) for i in range(16)])
    folded = call(fold_kernel, of((16, D), F32), [VMEM] * 2, near, residual_in)
    return call(finish_kernel, (full, full), [VMEM] * 3, folded, far, norm_gain[None, :])


def solution(mesh):
    return jax.shard_map(
        shards,
        mesh=mesh,
        in_specs=(
            P("seq", "tp"),
            P("seq", "tp"),
            P("seq", "tp"),
            P("tp", "seq"),
            P("seq", None),
            P(("seq", "tp"), None),
            P("tp", None),
            P(),
        ),
        out_specs=(P(("seq", "tp"), None), P(("seq", "tp"), None)),
        check_vma=False,
    )
```

```python
import jax
import jax.numpy as jnp
from jax import lax
from jax.experimental import pallas as pl
from jax.experimental.pallas import tpu as pltpu
from jax.sharding import PartitionSpec as P

SPAN = 256
HEADS = 3
HDIM = 128
STATE = HEADS * HDIM
PAYLOAD = STATE + 8
D = 4096
F32 = jnp.float32
BF16 = jnp.bfloat16

SHARDS = 32
FLIP_Z = [(i, i ^ 1) for i in range(SHARDS)]
ROW_Y = [[g + 2 * k for k in range(4)] for g in range(SHARDS) if g & 6 == 0]
ROW_X = [[g + 8 * k for k in range(4)] for g in range(8)]
FAR_ORDER = (0, 3, 2, 1)
LONG = pl.CostEstimate(flops=10**11, bytes_accessed=0, transcendentals=0)
NEAR_CHIPS = [[8 * g + 2 * k + core for k in range(4)] for g in range(2) for core in range(2)]

VMEM = pl.BlockSpec(memory_space=pltpu.VMEM)
HBM = pl.BlockSpec(memory_space=pltpu.HBM)
SMEM = pl.BlockSpec(memory_space=pltpu.SMEM)


def segment_of(starts_ref, positions):
    total = jnp.zeros(positions.shape, jnp.int32)
    for slot in range(3):
        total = total + (positions >= starts_ref[0, slot]).astype(jnp.int32)
    return total


def running_sums(weights, decay, column):
    dims = (((1,), (1,)), ((), ()))
    a, b = (weights, decay) if column else (decay, weights)
    return lax.dot_general(a, b, dims, precision=lax.Precision.HIGHEST, preferred_element_type=F32)


def grid_iotas():
    row = lax.broadcasted_iota(jnp.int32, (SPAN, SPAN), 0)
    col = lax.broadcasted_iota(jnp.int32, (SPAN, SPAN), 1)
    return row, col


def state_kernel(
    starts_hbm, decay_hbm, key_hbm, value_hbm, out_ref,
    starts_ref, decay_ref, key_ref, value_ref, sems,
):
    sources = (decay_hbm, starts_hbm, key_hbm, value_hbm)
    targets = (decay_ref, starts_ref, key_ref, value_ref)
    copies = [
        pltpu.make_async_copy(source, target, sems.at[k])
        for k, (source, target) in enumerate(zip(sources, targets))
    ]
    for copy in copies:
        copy.start()
    row, col = grid_iotas()
    later = (col > row).astype(F32)
    copies[0].wait()
    decay = decay_ref[...]
    tail = running_sums(later, decay, True)
    copies[1].wait()
    segment = segment_of(starts_ref, lax.broadcasted_iota(jnp.int32, (SPAN, 1), 0))
    last = segment_of(starts_ref, jnp.full((1, 1), SPAN - 1, jnp.int32))
    tail_weight = jnp.exp(tail) * (segment == last).astype(F32)
    through = jnp.exp(jnp.sum(decay, axis=1, keepdims=True)) * (last == 0).astype(F32)
    high = through.astype(BF16).astype(F32)
    low = (through - high).astype(BF16).astype(F32)
    rows = jnp.concatenate([high, low, jnp.zeros((2, 1), F32)], axis=0)
    out_ref[STATE:, :] = jnp.broadcast_to(rows, (8, HDIM)).astype(BF16)
    copies[2].wait()
    copies[3].wait()
    for h in range(HEADS):
        cut = slice(h * HDIM, (h + 1) * HDIM)
        decayed = (key_ref[:, cut].astype(F32) * tail_weight[:, h : h + 1]).astype(BF16)
        out_ref[cut, :] = lax.dot_general(
            decayed, value_ref[:, cut], (((0,), (0,)), ((), ())), preferred_element_type=F32
        ).astype(BF16)


def intra_kernel(
    starts_ref, decay_ref, query_ref, key_ref, value_ref, weight_hbm,
    out_ref, carry_ref, weight_ref, sem,
):
    copy = pltpu.make_async_copy(weight_hbm, weight_ref, sem)
    copy.start()
    row, col = grid_iotas()
    lower = row >= col
    lower_f = lower.astype(F32)
    decay = decay_ref[...]
    cum_col = running_sums(lower_f, decay, True)
    cum_row = running_sums(lower_f, decay, False)
    seg_col = segment_of(starts_ref, lax.broadcasted_iota(jnp.int32, (SPAN, 1), 0))
    seg_row = segment_of(starts_ref, lax.broadcasted_iota(jnp.int32, (1, SPAN), 1))
    same = lower & (seg_col == seg_row)
    carry_ref[...] = jnp.exp(cum_col) * (seg_col == 0).astype(F32)
    for h in range(HEADS):
        cut = slice(h * HDIM, (h + 1) * HDIM)
        spread = cum_col[:, h : h + 1] - cum_row[h : h + 1, :]
        decay_mat = jnp.exp(jnp.where(same, spread, -jnp.inf))
        scores = lax.dot_general(
            query_ref[:, cut], key_ref[:, cut], (((1,), (1,)), ((), ())), preferred_element_type=F32
        )
        weights = (scores * decay_mat).astype(BF16)
        out_ref[:, cut] = jnp.dot(weights, value_ref[:, cut], preferred_element_type=F32)
    copy.wait()


def decays(rows):
    rows = rows.astype(F32)
    return rows[0:HEADS] + rows[HEADS : 2 * HEADS]


def split_decay(decay):
    high = decay.astype(BF16).astype(F32)
    low = (decay - high).astype(BF16).astype(F32)
    return jnp.concatenate([high, low, jnp.zeros((2, HDIM), F32)], axis=0).astype(BF16)


def pair_kernel(place_ref, own_ref, other_ref, out_ref):
    odd = place_ref[0] & 1 == 1
    own_a, other_a = decays(own_ref[STATE:, :]), decays(other_ref[STATE:, :])
    later_a = jnp.where(odd, own_a, other_a)
    scales = split_decay(own_a * other_a)
    for k in range(4):
        out_ref[k, STATE:, :] = scales
    for h in range(HEADS):
        cut = slice(h * HDIM, (h + 1) * HDIM)
        own, other = own_ref[cut, :].astype(F32), other_ref[cut, :].astype(F32)
        first, second = jnp.where(odd, other, own), jnp.where(odd, own, other)
        total = (later_a[h : h + 1] * first + second).astype(BF16)
        for k in range(4):
            out_ref[k, cut, :] = total


def row_kernel(parts_ref, out_ref):
    scale = [decays(parts_ref[k, STATE:, :]) for k in range(4)]
    scales = split_decay(scale[0] * scale[1] * scale[2] * scale[3])
    for k in range(4):
        out_ref[k, STATE:, :] = scales
    for h in range(HEADS):
        cut = slice(h * HDIM, (h + 1) * HDIM)
        total = parts_ref[0, cut, :].astype(F32)
        for k in range(1, 4):
            total = scale[k][h : h + 1] * total + parts_ref[k, cut, :].astype(F32)
        total = total.astype(BF16)
        for k in range(4):
            out_ref[k, cut, :] = total


def before(parts_ref, scale, reached, h):
    cut = slice(h * HDIM, (h + 1) * HDIM)
    state = jnp.zeros((HDIM, HDIM), F32)
    through = jnp.ones((1, HDIM), F32)
    for k in range(3):
        a = scale[k][h : h + 1]
        state = jnp.where(k < reached, a * state + parts_ref[k, cut, :].astype(F32), state)
        through = jnp.where(k < reached, a * through, through)
    return state, through


def attend_kernel(
    place_ref, query_ref, intra_ref, carry_ref, other_ref, row_ref, col_ref, weight_ref,
    send_ref, keep_ref, mixed_ref, sibling_ref,
):
    odd = place_ref[0] & 1 == 1
    carry = carry_ref[...]
    row_scale = [decays(row_ref[k, STATE:, :]) for k in range(3)]
    col_scale = [decays(col_ref[k, STATE:, :]) for k in range(3)]
    other_a = decays(other_ref[STATE:, :])
    for h in range(HEADS):
        cut = slice(h * HDIM, (h + 1) * HDIM)
        inner, inner_a = before(row_ref, row_scale, (place_ref[0] >> 1) & 3, h)
        outer, _ = before(col_ref, col_scale, place_ref[0] >> 3, h)
        state = inner_a * outer + inner
        state = jnp.where(odd, other_a[h : h + 1] * state + other_ref[cut, :].astype(F32), state)
        inter = jnp.dot(query_ref[:, cut], state.astype(BF16), preferred_element_type=F32)
        mixed = intra_ref[:, cut] + inter * carry[:, h : h + 1]
        scale = lax.rsqrt(jnp.mean(mixed * mixed, axis=1, keepdims=True) + 1e-06)
        mixed_ref[:, cut] = (mixed * scale).astype(BF16)
    core, chip = place_ref[1] & 1, place_ref[1] >> 1
    for k in range(8):
        start = ((chip & 4) + (k & 3) if k & 4 else chip ^ 4 ^ FAR_ORDER[k]) * 32
        cut = slice(k * 16, (k + 1) * 16)
        own, sibling = start + core * 16, start + (1 - core) * 16
        keep_ref[cut, :] = mixed_ref[pl.ds(pl.multiple_of(own, 16), 16), :]
        sibling_ref[cut, :] = mixed_ref[pl.ds(pl.multiple_of(sibling, 16), 16), :]
    send_ref[...] = jnp.dot(
        sibling_ref[...], weight_ref[...], preferred_element_type=F32
    ).astype(BF16)


def keep_kernel(own_ref, weight_ref, out_ref):
    out_ref[...] = jnp.dot(own_ref[...], weight_ref[...], preferred_element_type=F32)


def far_kernel(keep_ref, got_ref, *out_refs):
    for k, ref in enumerate(out_refs):
        cut = slice(k * 16, (k + 1) * 16)
        ref[...] = (keep_ref[cut, :] + got_ref[cut, :].astype(F32)).astype(ref.dtype)


def near_kernel(keep_ref, got_ref, out_ref, sum_ref, sems):
    copies = []
    for k in range(4):
        cut = slice(64 + k * 16, 80 + k * 16)
        sum_ref[k] = (keep_ref[cut, :] + got_ref[cut, :].astype(F32)).astype(BF16)
        copies.append(pltpu.make_async_copy(sum_ref.at[k], out_ref.at[k], sems.at[k]))
        copies[-1].start()
    for copy in copies:
        copy.wait()


def sum_kernel(own_ref, a_ref, b_ref, c_ref, out_ref):
    total = own_ref[...] + a_ref[...].astype(F32) + b_ref[...].astype(F32) + c_ref[...].astype(F32)
    out_ref[...] = total.astype(BF16)


def fold_kernel(parts_ref, residual_ref, out_ref):
    total = residual_ref[...].astype(F32)
    for k in range(4):
        total = total + parts_ref[k].astype(F32)
    out_ref[...] = total


def finish_kernel(near_ref, far_ref, gain_ref, hidden_ref, normed_ref):
    hidden = near_ref[...] + far_ref[...].astype(F32)
    scale = lax.rsqrt(jnp.mean(hidden * hidden, axis=1, keepdims=True) + 1e-05)
    hidden_ref[...] = hidden.astype(BF16)
    normed_ref[...] = (hidden * scale * gain_ref[...]).astype(BF16)


def call(body, shapes, specs, *args, scratch=(), outs=VMEM, cost=None):
    return pl.pallas_call(
        body,
        out_shape=shapes,
        in_specs=specs,
        out_specs=jax.tree.map(lambda _: outs, shapes),
        scratch_shapes=list(scratch),
        cost_estimate=cost,
        compiler_params=pltpu.CompilerParams(vmem_limit_bytes=16 * 1024 * 1024),
    )(*args)


def of(shape, dtype):
    return jax.ShapeDtypeStruct(shape, dtype)


def shards(
    query_rows, key_rows, value_rows, log_decay, doc_starts, residual_in, out_weight, norm_gain
):
    place = jnp.stack([lax.axis_index("seq"), lax.axis_index("tp")]).astype(jnp.int32)

    local = call(
        state_kernel, pltpu.VMEM((PAYLOAD, HDIM), BF16), [HBM] * 4,
        *(
            pltpu.with_memory_space_constraint(a, pltpu.HBM)
            for a in (doc_starts, log_decay, key_rows, value_rows)
        ),
        scratch=[
            pltpu.SMEM((1, 3), jnp.int32),
            pltpu.VMEM((HEADS, SPAN), F32),
            pltpu.VMEM((SPAN, STATE), BF16),
            pltpu.VMEM((SPAN, STATE), BF16),
            pltpu.SemaphoreType.DMA((4,)),
        ],
    )
    late_query = lax.optimization_barrier((local, query_rows))[1]
    other = lax.ppermute(local, "seq", FLIP_Z)
    intra, carry, weight = call(
        intra_kernel,
        (of((SPAN, STATE), F32), of((SPAN, HEADS), F32), pltpu.VMEM((STATE, D), BF16)),
        [SMEM, VMEM, VMEM, VMEM, VMEM, HBM],
        doc_starts, log_decay, late_query, key_rows, value_rows,
        pltpu.with_memory_space_constraint(out_weight, pltpu.HBM),
        scratch=[pltpu.SemaphoreType.DMA],
    )
    other, intra, carry = lax.optimization_barrier((other, intra, carry))
    four = of((4, PAYLOAD, HDIM), BF16)
    pairs = call(pair_kernel, four, [SMEM, VMEM, VMEM], place, local, other)
    rows = lax.all_to_all(pairs, "seq", 0, 0, axis_index_groups=ROW_Y)
    totals = call(row_kernel, four, [VMEM], rows)
    cols = lax.all_to_all(totals, "seq", 0, 0, axis_index_groups=ROW_X)
    send, keep = call(
        attend_kernel, (of((SPAN // 2, D), BF16), of((SPAN // 2, STATE), BF16)),
        [SMEM] + [VMEM] * 7,
        place, query_rows, intra, carry, other, rows, cols, weight,
        scratch=[pltpu.VMEM((SPAN, STATE), BF16), pltpu.VMEM((SPAN // 2, STATE), BF16)],
    )
    got = lax.ppermute(send, "tp", [(i, i ^ 1) for i in range(16)])
    keep = call(keep_kernel, of((SPAN // 2, D), F32), [VMEM, VMEM], keep, weight)
    full = of((16, D), BF16)
    own, *parts = call(
        far_kernel, (of((16, D), F32), full, full, full), [VMEM, VMEM], keep, got
    )
    parts = [
        lax.ppermute(sent, "tp", [(i, i ^ (2 * k)) for i in range(16)])
        for k, sent in zip(FAR_ORDER[1:], parts)
    ]
    near = call(
        near_kernel, pltpu.HBM((4, 16, D), BF16), [VMEM, VMEM], keep, got,
        scratch=[pltpu.VMEM((4, 16, D), BF16), pltpu.SemaphoreType.DMA((4,))], outs=HBM,
    )
    near = lax.all_to_all(near, "tp", 0, 0, axis_index_groups=NEAR_CHIPS)
    away = call(sum_kernel, full, [VMEM] * 4, own, *parts, cost=LONG)
    far = lax.ppermute(away, "tp", [(i, i ^ 8) for i in range(16)])
    folded = call(fold_kernel, of((16, D), F32), [VMEM] * 2, near, residual_in)
    return call(finish_kernel, (full, full), [VMEM] * 3, folded, far, norm_gain[None, :])


def solution(mesh):
    return jax.shard_map(
        shards,
        mesh=mesh,
        in_specs=(
            P("seq", "tp"),
            P("seq", "tp"),
            P("seq", "tp"),
            P("tp", "seq"),
            P("seq", None),
            P(("seq", "tp"), None),
            P("tp", None),
            P(),
        ),
        out_specs=(P(("seq", "tp"), None), P(("seq", "tp"), None)),
        check_vma=False,
    )
```

```python
import jax
import jax.numpy as jnp
from jax import lax
from jax.experimental import pallas as pl
from jax.experimental.pallas import tpu as pltpu
from jax.sharding import PartitionSpec as P

SPAN = 256
HEADS = 3
HDIM = 128
STATE = HEADS * HDIM
PAYLOAD = STATE + 8
D = 4096
F32 = jnp.float32
BF16 = jnp.bfloat16

SHARDS = 32
FLIP_Z = [(i, i ^ 1) for i in range(SHARDS)]
ROW_Y = [[g + 2 * k for k in range(4)] for g in range(SHARDS) if g & 6 == 0]
ROW_X = [[g + 8 * k for k in range(4)] for g in range(8)]
FAR_ORDER, NEAR_ORDER = (0, 3, 2, 1), (0, 2, 1, 3)
LONG = pl.CostEstimate(flops=10**11, bytes_accessed=0, transcendentals=0)

VMEM = pl.BlockSpec(memory_space=pltpu.VMEM)
HBM = pl.BlockSpec(memory_space=pltpu.HBM)
SMEM = pl.BlockSpec(memory_space=pltpu.SMEM)


def segment_of(starts_ref, positions):
    total = jnp.zeros(positions.shape, jnp.int32)
    for slot in range(3):
        total = total + (positions >= starts_ref[0, slot]).astype(jnp.int32)
    return total


def running_sums(weights, decay, column):
    dims = (((1,), (1,)), ((), ()))
    a, b = (weights, decay) if column else (decay, weights)
    return lax.dot_general(a, b, dims, precision=lax.Precision.HIGHEST, preferred_element_type=F32)


def grid_iotas():
    row = lax.broadcasted_iota(jnp.int32, (SPAN, SPAN), 0)
    col = lax.broadcasted_iota(jnp.int32, (SPAN, SPAN), 1)
    return row, col


def state_kernel(
    starts_hbm, decay_hbm, key_hbm, value_hbm, out_ref,
    starts_ref, decay_ref, key_ref, value_ref, sems,
):
    sources = (decay_hbm, starts_hbm, key_hbm, value_hbm)
    targets = (decay_ref, starts_ref, key_ref, value_ref)
    copies = [
        pltpu.make_async_copy(source, target, sems.at[k])
        for k, (source, target) in enumerate(zip(sources, targets))
    ]
    for copy in copies:
        copy.start()
    row, col = grid_iotas()
    later = (col > row).astype(F32)
    copies[0].wait()
    decay = decay_ref[...]
    tail = running_sums(later, decay, True)
    copies[1].wait()
    segment = segment_of(starts_ref, lax.broadcasted_iota(jnp.int32, (SPAN, 1), 0))
    last = segment_of(starts_ref, jnp.full((1, 1), SPAN - 1, jnp.int32))
    tail_weight = jnp.exp(tail) * (segment == last).astype(F32)
    through = jnp.exp(jnp.sum(decay, axis=1, keepdims=True)) * (last == 0).astype(F32)
    high = through.astype(BF16).astype(F32)
    low = (through - high).astype(BF16).astype(F32)
    rows = jnp.concatenate([high, low, jnp.zeros((2, 1), F32)], axis=0)
    out_ref[STATE:, :] = jnp.broadcast_to(rows, (8, HDIM)).astype(BF16)
    copies[2].wait()
    copies[3].wait()
    for h in range(HEADS):
        cut = slice(h * HDIM, (h + 1) * HDIM)
        decayed = (key_ref[:, cut].astype(F32) * tail_weight[:, h : h + 1]).astype(BF16)
        out_ref[cut, :] = lax.dot_general(
            decayed, value_ref[:, cut], (((0,), (0,)), ((), ())), preferred_element_type=F32
        ).astype(BF16)


def intra_kernel(
    starts_ref, decay_ref, query_ref, key_ref, value_ref, weight_hbm,
    out_ref, carry_ref, weight_ref, sem,
):
    copy = pltpu.make_async_copy(weight_hbm, weight_ref, sem)
    copy.start()
    row, col = grid_iotas()
    lower = row >= col
    lower_f = lower.astype(F32)
    decay = decay_ref[...]
    cum_col = running_sums(lower_f, decay, True)
    cum_row = running_sums(lower_f, decay, False)
    seg_col = segment_of(starts_ref, lax.broadcasted_iota(jnp.int32, (SPAN, 1), 0))
    seg_row = segment_of(starts_ref, lax.broadcasted_iota(jnp.int32, (1, SPAN), 1))
    same = lower & (seg_col == seg_row)
    carry_ref[...] = jnp.exp(cum_col) * (seg_col == 0).astype(F32)
    for h in range(HEADS):
        cut = slice(h * HDIM, (h + 1) * HDIM)
        spread = cum_col[:, h : h + 1] - cum_row[h : h + 1, :]
        decay_mat = jnp.exp(jnp.where(same, spread, -jnp.inf))
        scores = lax.dot_general(
            query_ref[:, cut], key_ref[:, cut], (((1,), (1,)), ((), ())), preferred_element_type=F32
        )
        weights = (scores * decay_mat).astype(BF16)
        out_ref[:, cut] = jnp.dot(weights, value_ref[:, cut], preferred_element_type=F32)
    copy.wait()


def decays(rows):
    rows = rows.astype(F32)
    return rows[0:HEADS] + rows[HEADS : 2 * HEADS]


def split_decay(decay):
    high = decay.astype(BF16).astype(F32)
    low = (decay - high).astype(BF16).astype(F32)
    return jnp.concatenate([high, low, jnp.zeros((2, HDIM), F32)], axis=0).astype(BF16)


def pair_kernel(place_ref, own_ref, other_ref, out_ref):
    odd = place_ref[0] & 1 == 1
    own_a, other_a = decays(own_ref[STATE:, :]), decays(other_ref[STATE:, :])
    later_a = jnp.where(odd, own_a, other_a)
    scales = split_decay(own_a * other_a)
    for k in range(4):
        out_ref[k, STATE:, :] = scales
    for h in range(HEADS):
        cut = slice(h * HDIM, (h + 1) * HDIM)
        own, other = own_ref[cut, :].astype(F32), other_ref[cut, :].astype(F32)
        first, second = jnp.where(odd, other, own), jnp.where(odd, own, other)
        total = (later_a[h : h + 1] * first + second).astype(BF16)
        for k in range(4):
            out_ref[k, cut, :] = total


def row_kernel(parts_ref, out_ref):
    scale = [decays(parts_ref[k, STATE:, :]) for k in range(4)]
    scales = split_decay(scale[0] * scale[1] * scale[2] * scale[3])
    for k in range(4):
        out_ref[k, STATE:, :] = scales
    for h in range(HEADS):
        cut = slice(h * HDIM, (h + 1) * HDIM)
        total = parts_ref[0, cut, :].astype(F32)
        for k in range(1, 4):
            total = scale[k][h : h + 1] * total + parts_ref[k, cut, :].astype(F32)
        total = total.astype(BF16)
        for k in range(4):
            out_ref[k, cut, :] = total


def before(parts_ref, scale, reached, h):
    cut = slice(h * HDIM, (h + 1) * HDIM)
    state = jnp.zeros((HDIM, HDIM), F32)
    through = jnp.ones((1, HDIM), F32)
    for k in range(3):
        a = scale[k][h : h + 1]
        state = jnp.where(k < reached, a * state + parts_ref[k, cut, :].astype(F32), state)
        through = jnp.where(k < reached, a * through, through)
    return state, through


def attend_kernel(
    place_ref, query_ref, intra_ref, carry_ref, other_ref, row_ref, col_ref, weight_ref,
    send_ref, keep_ref, mixed_ref, sibling_ref,
):
    odd = place_ref[0] & 1 == 1
    carry = carry_ref[...]
    row_scale = [decays(row_ref[k, STATE:, :]) for k in range(3)]
    col_scale = [decays(col_ref[k, STATE:, :]) for k in range(3)]
    other_a = decays(other_ref[STATE:, :])
    for h in range(HEADS):
        cut = slice(h * HDIM, (h + 1) * HDIM)
        inner, inner_a = before(row_ref, row_scale, (place_ref[0] >> 1) & 3, h)
        outer, _ = before(col_ref, col_scale, place_ref[0] >> 3, h)
        state = inner_a * outer + inner
        state = jnp.where(odd, other_a[h : h + 1] * state + other_ref[cut, :].astype(F32), state)
        inter = jnp.dot(query_ref[:, cut], state.astype(BF16), preferred_element_type=F32)
        mixed = intra_ref[:, cut] + inter * carry[:, h : h + 1]
        scale = lax.rsqrt(jnp.mean(mixed * mixed, axis=1, keepdims=True) + 1e-06)
        mixed_ref[:, cut] = (mixed * scale).astype(BF16)
    core, chip = place_ref[1] & 1, place_ref[1] >> 1
    for k in range(8):
        start = (chip ^ NEAR_ORDER[k - 4] if k & 4 else chip ^ 4 ^ FAR_ORDER[k]) * 32
        cut = slice(k * 16, (k + 1) * 16)
        own, sibling = start + core * 16, start + (1 - core) * 16
        keep_ref[cut, :] = mixed_ref[pl.ds(pl.multiple_of(own, 16), 16), :]
        sibling_ref[cut, :] = mixed_ref[pl.ds(pl.multiple_of(sibling, 16), 16), :]
    send_ref[...] = jnp.dot(
        sibling_ref[...], weight_ref[...], preferred_element_type=F32
    ).astype(BF16)


def keep_kernel(own_ref, weight_ref, out_ref):
    out_ref[...] = jnp.dot(own_ref[...], weight_ref[...], preferred_element_type=F32)


def far_kernel(keep_ref, got_ref, *out_refs):
    for k, ref in enumerate(out_refs):
        cut = slice(k * 16, (k + 1) * 16)
        ref[...] = (keep_ref[cut, :] + got_ref[cut, :].astype(F32)).astype(ref.dtype)


def near_kernel(keep_ref, got_ref, own_ref, next_ref, sent_ref):
    def rows(start, stop):
        return keep_ref[start:stop, :] + got_ref[start:stop, :].astype(F32)

    sent_ref[...] = rows(96, 128).astype(BF16)
    own_ref[...] = rows(64, 80)
    next_ref[...] = rows(80, 96)


def next_kernel(own_ref, next_ref, got_ref, residual_ref, folded_ref, out_ref):
    out_ref[...] = (next_ref[...] + got_ref[16:, :].astype(F32)).astype(BF16)
    folded = residual_ref[...].astype(F32) + own_ref[...]
    folded_ref[...] = folded + got_ref[:16, :].astype(F32)


def sum_kernel(own_ref, a_ref, b_ref, c_ref, out_ref):
    total = own_ref[...] + a_ref[...].astype(F32) + b_ref[...].astype(F32) + c_ref[...].astype(F32)
    out_ref[...] = total.astype(BF16)


def finish_kernel(folded_ref, near_ref, far_ref, gain_ref, hidden_ref, normed_ref):
    hidden = folded_ref[...] + near_ref[...].astype(F32) + far_ref[...].astype(F32)
    scale = lax.rsqrt(jnp.mean(hidden * hidden, axis=1, keepdims=True) + 1e-05)
    hidden_ref[...] = hidden.astype(BF16)
    normed_ref[...] = (hidden * scale * gain_ref[...]).astype(BF16)


def call(body, shapes, specs, *args, scratch=(), outs=VMEM, cost=None):
    return pl.pallas_call(
        body,
        out_shape=shapes,
        in_specs=specs,
        out_specs=jax.tree.map(lambda _: outs, shapes),
        scratch_shapes=list(scratch),
        cost_estimate=cost,
        compiler_params=pltpu.CompilerParams(vmem_limit_bytes=16 * 1024 * 1024),
    )(*args)


def of(shape, dtype):
    return jax.ShapeDtypeStruct(shape, dtype)


def shards(
    query_rows, key_rows, value_rows, log_decay, doc_starts, residual_in, out_weight, norm_gain
):
    place = jnp.stack([lax.axis_index("seq"), lax.axis_index("tp")]).astype(jnp.int32)

    local = call(
        state_kernel, pltpu.VMEM((PAYLOAD, HDIM), BF16), [HBM] * 4,
        *(
            pltpu.with_memory_space_constraint(a, pltpu.HBM)
            for a in (doc_starts, log_decay, key_rows, value_rows)
        ),
        scratch=[
            pltpu.SMEM((1, 3), jnp.int32),
            pltpu.VMEM((HEADS, SPAN), F32),
            pltpu.VMEM((SPAN, STATE), BF16),
            pltpu.VMEM((SPAN, STATE), BF16),
            pltpu.SemaphoreType.DMA((4,)),
        ],
    )
    late_query = lax.optimization_barrier((local, query_rows))[1]
    other = lax.ppermute(local, "seq", FLIP_Z)
    intra, carry, weight = call(
        intra_kernel,
        (of((SPAN, STATE), F32), of((SPAN, HEADS), F32), pltpu.VMEM((STATE, D), BF16)),
        [SMEM, VMEM, VMEM, VMEM, VMEM, HBM],
        doc_starts, log_decay, late_query, key_rows, value_rows,
        pltpu.with_memory_space_constraint(out_weight, pltpu.HBM),
        scratch=[pltpu.SemaphoreType.DMA],
    )
    other, intra, carry = lax.optimization_barrier((other, intra, carry))
    four = of((4, PAYLOAD, HDIM), BF16)
    pairs = call(pair_kernel, four, [SMEM, VMEM, VMEM], place, local, other)
    rows = lax.all_to_all(pairs, "seq", 0, 0, axis_index_groups=ROW_Y)
    totals = call(row_kernel, four, [VMEM], rows)
    cols = lax.all_to_all(totals, "seq", 0, 0, axis_index_groups=ROW_X)
    send, keep = call(
        attend_kernel, (of((SPAN // 2, D), BF16), of((SPAN // 2, STATE), BF16)),
        [SMEM] + [VMEM] * 7,
        place, query_rows, intra, carry, other, rows, cols, weight,
        scratch=[pltpu.VMEM((SPAN, STATE), BF16), pltpu.VMEM((SPAN // 2, STATE), BF16)],
    )
    got = lax.ppermute(send, "tp", [(i, i ^ 1) for i in range(16)])
    keep = call(keep_kernel, of((SPAN // 2, D), F32), [VMEM, VMEM], keep, weight)
    full = of((16, D), BF16)
    own, *parts = call(
        far_kernel, (of((16, D), F32), full, full, full), [VMEM, VMEM], keep, got
    )
    parts = [
        lax.ppermute(sent, "tp", [(i, i ^ (2 * k)) for i in range(16)])
        for k, sent in zip(FAR_ORDER[1:], parts)
    ]
    wide = of((16, D), F32)
    mine, following, sent = call(
        near_kernel, (wide, wide, of((32, D), BF16)), [VMEM, VMEM], keep, got
    )
    first = lax.ppermute(sent, "tp", [(i, i ^ 2) for i in range(16)])
    away = call(sum_kernel, full, [VMEM] * 4, own, *parts, cost=LONG)
    far = lax.ppermute(away, "tp", [(i, i ^ 8) for i in range(16)])
    folded, following = call(
        next_kernel, (wide, full), [VMEM] * 4, mine, following, first, residual_in
    )
    second = lax.ppermute(following, "tp", [(i, i ^ 4) for i in range(16)])
    return call(finish_kernel, (full, full), [VMEM] * 4, folded, second, far, norm_gain[None, :])


def solution(mesh):
    return jax.shard_map(
        shards,
        mesh=mesh,
        in_specs=(
            P("seq", "tp"),
            P("seq", "tp"),
            P("seq", "tp"),
            P("tp", "seq"),
            P("seq", None),
            P(("seq", "tp"), None),
            P("tp", None),
            P(),
        ),
        out_specs=(P(("seq", "tp"), None), P(("seq", "tp"), None)),
        check_vma=False,
    )
```

```python
import jax
import jax.numpy as jnp
from jax import lax
from jax.experimental import pallas as pl
from jax.experimental.pallas import tpu as pltpu
from jax.sharding import PartitionSpec as P

SPAN = 256
HEADS = 3
HDIM = 128
STATE = HEADS * HDIM
PAYLOAD = STATE + 8
D = 4096
F32 = jnp.float32
BF16 = jnp.bfloat16

SHARDS = 32
TP = 16


def hop_z(core, steps):
    pairs = []
    for place in range(SHARDS // 2):
        for z in range(TP):
            to = (z + steps) % TP
            pairs.append(
                tuple((place * 2 + a // 8) * TP + a % 8 * 2 + core for a in (z, to))
            )
    return pairs


ROW_Y = [[g + 2 * k for k in range(4)] for g in range(SHARDS) if g & 6 == 0]
ROW_X = [[g + 8 * k for k in range(4)] for g in range(8)]
FAR_ORDER = (0, 3, 2, 1)
LONG = pl.CostEstimate(flops=10**11, bytes_accessed=0, transcendentals=0)
NEAR_CHIPS = [[8 * g + 2 * k + core for k in range(4)] for g in range(2) for core in range(2)]

VMEM = pl.BlockSpec(memory_space=pltpu.VMEM)
HBM = pl.BlockSpec(memory_space=pltpu.HBM)
SMEM = pl.BlockSpec(memory_space=pltpu.SMEM)


def segment_of(starts_ref, positions):
    total = jnp.zeros(positions.shape, jnp.int32)
    for slot in range(3):
        total = total + (positions >= starts_ref[0, slot]).astype(jnp.int32)
    return total


def running_sums(weights, decay, column):
    dims = (((1,), (1,)), ((), ()))
    a, b = (weights, decay) if column else (decay, weights)
    return lax.dot_general(a, b, dims, precision=lax.Precision.HIGHEST, preferred_element_type=F32)


def grid_iotas():
    row = lax.broadcasted_iota(jnp.int32, (SPAN, SPAN), 0)
    col = lax.broadcasted_iota(jnp.int32, (SPAN, SPAN), 1)
    return row, col


def state_kernel(
    starts_hbm, decay_hbm, key_hbm, value_hbm, out_ref,
    starts_ref, decay_ref, key_ref, value_ref, sems,
):
    sources = (decay_hbm, starts_hbm, key_hbm, value_hbm)
    targets = (decay_ref, starts_ref, key_ref, value_ref)
    copies = [
        pltpu.make_async_copy(source, target, sems.at[k])
        for k, (source, target) in enumerate(zip(sources, targets))
    ]
    for copy in copies:
        copy.start()
    row, col = grid_iotas()
    later = (col > row).astype(F32)
    copies[0].wait()
    decay = decay_ref[...]
    tail = running_sums(later, decay, True)
    copies[1].wait()
    segment = segment_of(starts_ref, lax.broadcasted_iota(jnp.int32, (SPAN, 1), 0))
    last = segment_of(starts_ref, jnp.full((1, 1), SPAN - 1, jnp.int32))
    tail_weight = jnp.exp(tail) * (segment == last).astype(F32)
    through = jnp.exp(jnp.sum(decay, axis=1, keepdims=True)) * (last == 0).astype(F32)
    high = through.astype(BF16).astype(F32)
    low = (through - high).astype(BF16).astype(F32)
    rows = jnp.concatenate([high, low, jnp.zeros((2, 1), F32)], axis=0)
    out_ref[STATE:, :] = jnp.broadcast_to(rows, (8, HDIM)).astype(BF16)
    copies[2].wait()
    copies[3].wait()
    for h in range(HEADS):
        cut = slice(h * HDIM, (h + 1) * HDIM)
        decayed = (key_ref[:, cut].astype(F32) * tail_weight[:, h : h + 1]).astype(BF16)
        out_ref[cut, :] = lax.dot_general(
            decayed, value_ref[:, cut], (((0,), (0,)), ((), ())), preferred_element_type=F32
        ).astype(BF16)


def intra_kernel(
    starts_ref, decay_ref, query_ref, key_ref, value_ref, weight_hbm,
    out_ref, carry_ref, weight_ref, sem,
):
    copy = pltpu.make_async_copy(weight_hbm, weight_ref, sem)
    copy.start()
    row, col = grid_iotas()
    lower = row >= col
    lower_f = lower.astype(F32)
    decay = decay_ref[...]
    cum_col = running_sums(lower_f, decay, True)
    cum_row = running_sums(lower_f, decay, False)
    seg_col = segment_of(starts_ref, lax.broadcasted_iota(jnp.int32, (SPAN, 1), 0))
    seg_row = segment_of(starts_ref, lax.broadcasted_iota(jnp.int32, (1, SPAN), 1))
    same = lower & (seg_col == seg_row)
    carry_ref[...] = jnp.exp(cum_col) * (seg_col == 0).astype(F32)
    for h in range(HEADS):
        cut = slice(h * HDIM, (h + 1) * HDIM)
        spread = cum_col[:, h : h + 1] - cum_row[h : h + 1, :]
        decay_mat = jnp.exp(jnp.where(same, spread, -jnp.inf))
        scores = lax.dot_general(
            query_ref[:, cut], key_ref[:, cut], (((1,), (1,)), ((), ())), preferred_element_type=F32
        )
        weights = (scores * decay_mat).astype(BF16)
        out_ref[:, cut] = jnp.dot(weights, value_ref[:, cut], preferred_element_type=F32)
    copy.wait()


def decays(rows):
    rows = rows.astype(F32)
    return rows[0:HEADS] + rows[HEADS : 2 * HEADS]


def split_decay(decay):
    high = decay.astype(BF16).astype(F32)
    low = (decay - high).astype(BF16).astype(F32)
    return jnp.concatenate([high, low, jnp.zeros((2, HDIM), F32)], axis=0).astype(BF16)


def pair_kernel(place_ref, own_ref, straight_ref, around_ref, out_ref, other_ref):
    other_ref[...] = jnp.where(place_ref[1] & 1 == 1, around_ref[...], straight_ref[...])
    odd = place_ref[0] & 1 == 1
    own_a, other_a = decays(own_ref[STATE:, :]), decays(other_ref[STATE:, :])
    later_a = jnp.where(odd, own_a, other_a)
    scales = split_decay(own_a * other_a)
    for k in range(4):
        out_ref[k, STATE:, :] = scales
    for h in range(HEADS):
        cut = slice(h * HDIM, (h + 1) * HDIM)
        own, other = own_ref[cut, :].astype(F32), other_ref[cut, :].astype(F32)
        first, second = jnp.where(odd, other, own), jnp.where(odd, own, other)
        total = (later_a[h : h + 1] * first + second).astype(BF16)
        for k in range(4):
            out_ref[k, cut, :] = total


def row_kernel(parts_ref, out_ref):
    scale = [decays(parts_ref[k, STATE:, :]) for k in range(4)]
    scales = split_decay(scale[0] * scale[1] * scale[2] * scale[3])
    for k in range(4):
        out_ref[k, STATE:, :] = scales
    for h in range(HEADS):
        cut = slice(h * HDIM, (h + 1) * HDIM)
        total = parts_ref[0, cut, :].astype(F32)
        for k in range(1, 4):
            total = scale[k][h : h + 1] * total + parts_ref[k, cut, :].astype(F32)
        total = total.astype(BF16)
        for k in range(4):
            out_ref[k, cut, :] = total


def before(parts_ref, scale, reached, h):
    cut = slice(h * HDIM, (h + 1) * HDIM)
    state = jnp.zeros((HDIM, HDIM), F32)
    through = jnp.ones((1, HDIM), F32)
    for k in range(3):
        a = scale[k][h : h + 1]
        state = jnp.where(k < reached, a * state + parts_ref[k, cut, :].astype(F32), state)
        through = jnp.where(k < reached, a * through, through)
    return state, through


def attend_kernel(
    place_ref, query_ref, intra_ref, carry_ref, other_ref, row_ref, col_ref, weight_ref,
    send_ref, keep_ref, mixed_ref, sibling_ref,
):
    odd = place_ref[0] & 1 == 1
    carry = carry_ref[...]
    row_scale = [decays(row_ref[k, STATE:, :]) for k in range(3)]
    col_scale = [decays(col_ref[k, STATE:, :]) for k in range(3)]
    other_a = decays(other_ref[STATE:, :])
    for h in range(HEADS):
        cut = slice(h * HDIM, (h + 1) * HDIM)
        inner, inner_a = before(row_ref, row_scale, (place_ref[0] >> 1) & 3, h)
        outer, _ = before(col_ref, col_scale, place_ref[0] >> 3, h)
        state = inner_a * outer + inner
        state = jnp.where(odd, other_a[h : h + 1] * state + other_ref[cut, :].astype(F32), state)
        inter = jnp.dot(query_ref[:, cut], state.astype(BF16), preferred_element_type=F32)
        mixed = intra_ref[:, cut] + inter * carry[:, h : h + 1]
        scale = lax.rsqrt(jnp.mean(mixed * mixed, axis=1, keepdims=True) + 1e-06)
        mixed_ref[:, cut] = (mixed * scale).astype(BF16)
    core, chip = place_ref[1] & 1, place_ref[1] >> 1
    for k in range(8):
        start = ((chip & 4) + (k & 3) if k & 4 else chip ^ 4 ^ FAR_ORDER[k]) * 32
        cut = slice(k * 16, (k + 1) * 16)
        own, sibling = start + core * 16, start + (1 - core) * 16
        keep_ref[cut, :] = mixed_ref[pl.ds(pl.multiple_of(own, 16), 16), :]
        sibling_ref[cut, :] = mixed_ref[pl.ds(pl.multiple_of(sibling, 16), 16), :]
    send_ref[...] = jnp.dot(
        sibling_ref[...], weight_ref[...], preferred_element_type=F32
    ).astype(BF16)


def keep_kernel(own_ref, weight_ref, out_ref):
    out_ref[...] = jnp.dot(own_ref[...], weight_ref[...], preferred_element_type=F32)


def far_kernel(keep_ref, got_ref, *out_refs):
    for k, ref in enumerate(out_refs):
        cut = slice(k * 16, (k + 1) * 16)
        ref[...] = (keep_ref[cut, :] + got_ref[cut, :].astype(F32)).astype(ref.dtype)


def near_kernel(keep_ref, got_ref, out_ref, sum_ref, sems):
    copies = []
    for k in range(4):
        cut = slice(64 + k * 16, 80 + k * 16)
        sum_ref[k] = (keep_ref[cut, :] + got_ref[cut, :].astype(F32)).astype(BF16)
        copies.append(pltpu.make_async_copy(sum_ref.at[k], out_ref.at[k], sems.at[k]))
        copies[-1].start()
    for copy in copies:
        copy.wait()


def sum_kernel(own_ref, a_ref, b_ref, c_ref, out_ref):
    total = own_ref[...] + a_ref[...].astype(F32) + b_ref[...].astype(F32) + c_ref[...].astype(F32)
    out_ref[...] = total.astype(BF16)


def fold_kernel(parts_ref, residual_ref, out_ref):
    total = residual_ref[...].astype(F32)
    for k in range(4):
        total = total + parts_ref[k].astype(F32)
    out_ref[...] = total


def finish_kernel(near_ref, far_ref, gain_ref, hidden_ref, normed_ref):
    hidden = near_ref[...] + far_ref[...].astype(F32)
    scale = lax.rsqrt(jnp.mean(hidden * hidden, axis=1, keepdims=True) + 1e-05)
    hidden_ref[...] = hidden.astype(BF16)
    normed_ref[...] = (hidden * scale * gain_ref[...]).astype(BF16)


def call(body, shapes, specs, *args, scratch=(), outs=VMEM, cost=None):
    return pl.pallas_call(
        body,
        out_shape=shapes,
        in_specs=specs,
        out_specs=jax.tree.map(lambda _: outs, shapes),
        scratch_shapes=list(scratch),
        cost_estimate=cost,
        compiler_params=pltpu.CompilerParams(vmem_limit_bytes=16 * 1024 * 1024),
    )(*args)


def of(shape, dtype):
    return jax.ShapeDtypeStruct(shape, dtype)


def shards(
    query_rows, key_rows, value_rows, log_decay, doc_starts, residual_in, out_weight, norm_gain
):
    place = jnp.stack([lax.axis_index("seq"), lax.axis_index("tp")]).astype(jnp.int32)

    local = call(
        state_kernel, pltpu.VMEM((PAYLOAD, HDIM), BF16), [HBM] * 4,
        *(
            pltpu.with_memory_space_constraint(a, pltpu.HBM)
            for a in (doc_starts, log_decay, key_rows, value_rows)
        ),
        scratch=[
            pltpu.SMEM((1, 3), jnp.int32),
            pltpu.VMEM((HEADS, SPAN), F32),
            pltpu.VMEM((SPAN, STATE), BF16),
            pltpu.VMEM((SPAN, STATE), BF16),
            pltpu.SemaphoreType.DMA((4,)),
        ],
    )
    late_query = lax.optimization_barrier((local, query_rows))[1]
    straight = lax.ppermute(local, ("seq", "tp"), hop_z(0, 8))
    halfway = lax.ppermute(local, ("seq", "tp"), hop_z(1, -4))
    around = lax.ppermute(halfway, ("seq", "tp"), hop_z(1, -4))
    intra, carry, weight = call(
        intra_kernel,
        (of((SPAN, STATE), F32), of((SPAN, HEADS), F32), pltpu.VMEM((STATE, D), BF16)),
        [SMEM, VMEM, VMEM, VMEM, VMEM, HBM],
        doc_starts, log_decay, late_query, key_rows, value_rows,
        pltpu.with_memory_space_constraint(out_weight, pltpu.HBM),
        scratch=[pltpu.SemaphoreType.DMA],
    )
    straight, around, intra, carry = lax.optimization_barrier((straight, around, intra, carry))
    four = of((4, PAYLOAD, HDIM), BF16)
    pairs, other = call(
        pair_kernel, (four, of((PAYLOAD, HDIM), BF16)), [SMEM] + [VMEM] * 3,
        place, local, straight, around,
    )
    rows = lax.all_to_all(pairs, "seq", 0, 0, axis_index_groups=ROW_Y)
    totals = call(row_kernel, four, [VMEM], rows)
    cols = lax.all_to_all(totals, "seq", 0, 0, axis_index_groups=ROW_X)
    send, keep = call(
        attend_kernel, (of((SPAN // 2, D), BF16), of((SPAN // 2, STATE), BF16)),
        [SMEM] + [VMEM] * 7,
        place, query_rows, intra, carry, other, rows, cols, weight,
        scratch=[pltpu.VMEM((SPAN, STATE), BF16), pltpu.VMEM((SPAN // 2, STATE), BF16)],
    )
    got = lax.ppermute(send, "tp", [(i, i ^ 1) for i in range(16)])
    keep = call(keep_kernel, of((SPAN // 2, D), F32), [VMEM, VMEM], keep, weight)
    full = of((16, D), BF16)
    own, *parts = call(
        far_kernel, (of((16, D), F32), full, full, full), [VMEM, VMEM], keep, got
    )
    parts = [
        lax.ppermute(sent, "tp", [(i, i ^ (2 * k)) for i in range(16)])
        for k, sent in zip(FAR_ORDER[1:], parts)
    ]
    near = call(
        near_kernel, pltpu.HBM((4, 16, D), BF16), [VMEM, VMEM], keep, got,
        scratch=[pltpu.VMEM((4, 16, D), BF16), pltpu.SemaphoreType.DMA((4,))], outs=HBM,
    )
    near = lax.all_to_all(near, "tp", 0, 0, axis_index_groups=NEAR_CHIPS)
    away = call(sum_kernel, full, [VMEM] * 4, own, *parts, cost=LONG)
    far = lax.ppermute(away, "tp", [(i, i ^ 8) for i in range(16)])
    folded = call(fold_kernel, of((16, D), F32), [VMEM] * 2, near, residual_in)
    return call(finish_kernel, (full, full), [VMEM] * 3, folded, far, norm_gain[None, :])


def solution(mesh):
    return jax.shard_map(
        shards,
        mesh=mesh,
        in_specs=(
            P("seq", "tp"),
            P("seq", "tp"),
            P("seq", "tp"),
            P("tp", "seq"),
            P("seq", None),
            P(("seq", "tp"), None),
            P("tp", None),
            P(),
        ),
        out_specs=(P(("seq", "tp"), None), P(("seq", "tp"), None)),
        check_vma=False,
    )
```

```python
import functools

import jax
import jax.numpy as jnp
from jax import lax
from jax.experimental import pallas as pl
from jax.experimental.pallas import tpu as pltpu
from jax.sharding import PartitionSpec as P

SPAN = 256
HEADS = 3
HDIM = 128
STATE = HEADS * HDIM
PAYLOAD = STATE + 8
D = 4096
F32 = jnp.float32
BF16 = jnp.bfloat16

SHARDS = 32
FLIP_Z = [(i, i ^ 1) for i in range(SHARDS)]
ROW_Y = [[g + 2 * k for k in range(4)] for g in range(SHARDS) if g & 6 == 0]
ROW_X = [[g + 8 * k for k in range(4)] for g in range(8)]
FAR_ORDER, NEAR_ORDER = (0, 3, 2, 1), (1, 3, 2, 0)
LONG = pl.CostEstimate(flops=10**11, bytes_accessed=0, transcendentals=0)

VMEM = pl.BlockSpec(memory_space=pltpu.VMEM)
HBM = pl.BlockSpec(memory_space=pltpu.HBM)
SMEM = pl.BlockSpec(memory_space=pltpu.SMEM)


def segment_of(starts_ref, positions):
    total = jnp.zeros(positions.shape, jnp.int32)
    for slot in range(3):
        total = total + (positions >= starts_ref[0, slot]).astype(jnp.int32)
    return total


def running_sums(weights, decay, column):
    dims = (((1,), (1,)), ((), ()))
    a, b = (weights, decay) if column else (decay, weights)
    return lax.dot_general(a, b, dims, precision=lax.Precision.HIGHEST, preferred_element_type=F32)


def grid_iotas():
    row = lax.broadcasted_iota(jnp.int32, (SPAN, SPAN), 0)
    col = lax.broadcasted_iota(jnp.int32, (SPAN, SPAN), 1)
    return row, col


def state_kernel(
    starts_hbm, decay_hbm, key_hbm, value_hbm, out_ref,
    starts_ref, decay_ref, key_ref, value_ref, sems,
):
    sources = (decay_hbm, starts_hbm, key_hbm, value_hbm)
    targets = (decay_ref, starts_ref, key_ref, value_ref)
    copies = [
        pltpu.make_async_copy(source, target, sems.at[k])
        for k, (source, target) in enumerate(zip(sources, targets))
    ]
    for copy in copies:
        copy.start()
    row, col = grid_iotas()
    later = (col > row).astype(F32)
    copies[0].wait()
    decay = decay_ref[...]
    tail = running_sums(later, decay, True)
    copies[1].wait()
    segment = segment_of(starts_ref, lax.broadcasted_iota(jnp.int32, (SPAN, 1), 0))
    last = segment_of(starts_ref, jnp.full((1, 1), SPAN - 1, jnp.int32))
    tail_weight = jnp.exp(tail) * (segment == last).astype(F32)
    through = jnp.exp(jnp.sum(decay, axis=1, keepdims=True)) * (last == 0).astype(F32)
    high = through.astype(BF16).astype(F32)
    low = (through - high).astype(BF16).astype(F32)
    rows = jnp.concatenate([high, low, jnp.zeros((2, 1), F32)], axis=0)
    out_ref[STATE:, :] = jnp.broadcast_to(rows, (8, HDIM)).astype(BF16)
    copies[2].wait()
    copies[3].wait()
    for h in range(HEADS):
        cut = slice(h * HDIM, (h + 1) * HDIM)
        decayed = (key_ref[:, cut].astype(F32) * tail_weight[:, h : h + 1]).astype(BF16)
        out_ref[cut, :] = lax.dot_general(
            decayed, value_ref[:, cut], (((0,), (0,)), ((), ())), preferred_element_type=F32
        ).astype(BF16)


def intra_kernel(
    starts_ref, decay_ref, query_ref, key_ref, value_ref, weight_hbm,
    out_ref, carry_ref, weight_ref, sem,
):
    copy = pltpu.make_async_copy(weight_hbm, weight_ref, sem)
    copy.start()
    row, col = grid_iotas()
    lower = row >= col
    lower_f = lower.astype(F32)
    decay = decay_ref[...]
    cum_col = running_sums(lower_f, decay, True)
    cum_row = running_sums(lower_f, decay, False)
    seg_col = segment_of(starts_ref, lax.broadcasted_iota(jnp.int32, (SPAN, 1), 0))
    seg_row = segment_of(starts_ref, lax.broadcasted_iota(jnp.int32, (1, SPAN), 1))
    same = lower & (seg_col == seg_row)
    carry_ref[...] = jnp.exp(cum_col) * (seg_col == 0).astype(F32)
    for h in range(HEADS):
        cut = slice(h * HDIM, (h + 1) * HDIM)
        spread = cum_col[:, h : h + 1] - cum_row[h : h + 1, :]
        decay_mat = jnp.exp(jnp.where(same, spread, -jnp.inf))
        scores = lax.dot_general(
            query_ref[:, cut], key_ref[:, cut], (((1,), (1,)), ((), ())), preferred_element_type=F32
        )
        weights = (scores * decay_mat).astype(BF16)
        out_ref[:, cut] = jnp.dot(weights, value_ref[:, cut], preferred_element_type=F32)
    copy.wait()


def decays(rows):
    rows = rows.astype(F32)
    return rows[0:HEADS] + rows[HEADS : 2 * HEADS]


def split_decay(decay):
    high = decay.astype(BF16).astype(F32)
    low = (decay - high).astype(BF16).astype(F32)
    return jnp.concatenate([high, low, jnp.zeros((2, HDIM), F32)], axis=0).astype(BF16)


def pair_kernel(place_ref, own_ref, other_ref, out_ref):
    odd = place_ref[0] & 1 == 1
    own_a, other_a = decays(own_ref[STATE:, :]), decays(other_ref[STATE:, :])
    later_a = jnp.where(odd, own_a, other_a)
    scales = split_decay(own_a * other_a)
    for k in range(4):
        out_ref[k, STATE:, :] = scales
    for h in range(HEADS):
        cut = slice(h * HDIM, (h + 1) * HDIM)
        own, other = own_ref[cut, :].astype(F32), other_ref[cut, :].astype(F32)
        first, second = jnp.where(odd, other, own), jnp.where(odd, own, other)
        total = (later_a[h : h + 1] * first + second).astype(BF16)
        for k in range(4):
            out_ref[k, cut, :] = total


def row_kernel(parts_ref, out_ref):
    scale = [decays(parts_ref[k, STATE:, :]) for k in range(4)]
    scales = split_decay(scale[0] * scale[1] * scale[2] * scale[3])
    for k in range(4):
        out_ref[k, STATE:, :] = scales
    for h in range(HEADS):
        cut = slice(h * HDIM, (h + 1) * HDIM)
        total = parts_ref[0, cut, :].astype(F32)
        for k in range(1, 4):
            total = scale[k][h : h + 1] * total + parts_ref[k, cut, :].astype(F32)
        total = total.astype(BF16)
        for k in range(4):
            out_ref[k, cut, :] = total


def before(parts_ref, scale, reached, h):
    cut = slice(h * HDIM, (h + 1) * HDIM)
    state = jnp.zeros((HDIM, HDIM), F32)
    through = jnp.ones((1, HDIM), F32)
    for k in range(3):
        a = scale[k][h : h + 1]
        state = jnp.where(k < reached, a * state + parts_ref[k, cut, :].astype(F32), state)
        through = jnp.where(k < reached, a * through, through)
    return state, through


def attend_kernel(
    place_ref, query_ref, intra_ref, carry_ref, other_ref, row_ref, col_ref, weight_ref,
    send_ref, keep_ref, mixed_ref, sibling_ref,
):
    odd = place_ref[0] & 1 == 1
    carry = carry_ref[...]
    row_scale = [decays(row_ref[k, STATE:, :]) for k in range(3)]
    col_scale = [decays(col_ref[k, STATE:, :]) for k in range(3)]
    other_a = decays(other_ref[STATE:, :])
    for h in range(HEADS):
        cut = slice(h * HDIM, (h + 1) * HDIM)
        inner, inner_a = before(row_ref, row_scale, (place_ref[0] >> 1) & 3, h)
        outer, _ = before(col_ref, col_scale, place_ref[0] >> 3, h)
        state = inner_a * outer + inner
        state = jnp.where(odd, other_a[h : h + 1] * state + other_ref[cut, :].astype(F32), state)
        inter = jnp.dot(query_ref[:, cut], state.astype(BF16), preferred_element_type=F32)
        mixed = intra_ref[:, cut] + inter * carry[:, h : h + 1]
        scale = lax.rsqrt(jnp.mean(mixed * mixed, axis=1, keepdims=True) + 1e-06)
        mixed_ref[:, cut] = (mixed * scale).astype(BF16)
    core, chip = place_ref[1] & 1, place_ref[1] >> 1
    for k in range(8):
        start = (chip ^ NEAR_ORDER[k - 4] if k & 4 else chip ^ 4 ^ FAR_ORDER[k]) * 32
        cut = slice(k * 16, (k + 1) * 16)
        own, sibling = start + core * 16, start + (1 - core) * 16
        keep_ref[cut, :] = mixed_ref[pl.ds(pl.multiple_of(own, 16), 16), :]
        sibling_ref[cut, :] = mixed_ref[pl.ds(pl.multiple_of(sibling, 16), 16), :]
    send_ref[...] = jnp.dot(
        sibling_ref[...], weight_ref[...], preferred_element_type=F32
    ).astype(BF16)


def keep_kernel(own_ref, weight_ref, out_ref):
    out_ref[...] = jnp.dot(own_ref[...], weight_ref[...], preferred_element_type=F32)


def slab_kernel(slabs, keep_ref, got_ref, *out_refs):
    for (start, stop), ref in zip(slabs, out_refs):
        cut = slice(start, stop)
        ref[...] = (keep_ref[cut, :] + got_ref[cut, :].astype(F32)).astype(ref.dtype)


def sum_kernel(own_ref, a_ref, b_ref, c_ref, out_ref):
    total = own_ref[...] + a_ref[...].astype(F32) + b_ref[...].astype(F32)
    out_ref[...] = (total + c_ref[:16, :].astype(F32)).astype(BF16)


def fold_kernel(own_ref, a_ref, b_ref, c_ref, residual_ref, out_ref):
    total = residual_ref[...].astype(F32) + own_ref[...]
    total = total + a_ref[...].astype(F32) + b_ref[...].astype(F32)
    out_ref[...] = total + c_ref[16:, :].astype(F32)


def finish_kernel(near_ref, far_ref, gain_ref, hidden_ref, normed_ref):
    hidden = near_ref[...] + far_ref[...].astype(F32)
    scale = lax.rsqrt(jnp.mean(hidden * hidden, axis=1, keepdims=True) + 1e-05)
    hidden_ref[...] = hidden.astype(BF16)
    normed_ref[...] = (hidden * scale * gain_ref[...]).astype(BF16)


def call(body, shapes, specs, *args, scratch=(), outs=VMEM, cost=None):
    return pl.pallas_call(
        body,
        out_shape=shapes,
        in_specs=specs,
        out_specs=jax.tree.map(lambda _: outs, shapes),
        scratch_shapes=list(scratch),
        cost_estimate=cost,
        compiler_params=pltpu.CompilerParams(vmem_limit_bytes=16 * 1024 * 1024),
    )(*args)


def of(shape, dtype):
    return jax.ShapeDtypeStruct(shape, dtype)


def shards(
    query_rows, key_rows, value_rows, log_decay, doc_starts, residual_in, out_weight, norm_gain
):
    place = jnp.stack([lax.axis_index("seq"), lax.axis_index("tp")]).astype(jnp.int32)

    local = call(
        state_kernel, pltpu.VMEM((PAYLOAD, HDIM), BF16), [HBM] * 4,
        *(
            pltpu.with_memory_space_constraint(a, pltpu.HBM)
            for a in (doc_starts, log_decay, key_rows, value_rows)
        ),
        scratch=[
            pltpu.SMEM((1, 3), jnp.int32),
            pltpu.VMEM((HEADS, SPAN), F32),
            pltpu.VMEM((SPAN, STATE), BF16),
            pltpu.VMEM((SPAN, STATE), BF16),
            pltpu.SemaphoreType.DMA((4,)),
        ],
    )
    late_query = lax.optimization_barrier((local, query_rows))[1]
    other = lax.ppermute(local, "seq", FLIP_Z)
    intra, carry, weight = call(
        intra_kernel,
        (of((SPAN, STATE), F32), of((SPAN, HEADS), F32), pltpu.VMEM((STATE, D), BF16)),
        [SMEM, VMEM, VMEM, VMEM, VMEM, HBM],
        doc_starts, log_decay, late_query, key_rows, value_rows,
        pltpu.with_memory_space_constraint(out_weight, pltpu.HBM),
        scratch=[pltpu.SemaphoreType.DMA],
    )
    other, intra, carry = lax.optimization_barrier((other, intra, carry))
    four = of((4, PAYLOAD, HDIM), BF16)
    pairs = call(pair_kernel, four, [SMEM, VMEM, VMEM], place, local, other)
    rows = lax.all_to_all(pairs, "seq", 0, 0, axis_index_groups=ROW_Y)
    totals = call(row_kernel, four, [VMEM], rows)
    cols = lax.all_to_all(totals, "seq", 0, 0, axis_index_groups=ROW_X)
    send, keep = call(
        attend_kernel, (of((SPAN // 2, D), BF16), of((SPAN // 2, STATE), BF16)),
        [SMEM] + [VMEM] * 7,
        place, query_rows, intra, carry, other, rows, cols, weight,
        scratch=[pltpu.VMEM((SPAN, STATE), BF16), pltpu.VMEM((SPAN // 2, STATE), BF16)],
    )
    got = lax.ppermute(send, "tp", [(i, i ^ 1) for i in range(16)])
    keep = call(keep_kernel, of((SPAN // 2, D), F32), [VMEM, VMEM], keep, weight)
    full = of((16, D), BF16)
    wide = of((16, D), F32)

    def to_chip(sent, k):
        return lax.ppermute(sent, "tp", [(i, i ^ (2 * k)) for i in range(16)])

    own, far_c, far_b, both = call(
        functools.partial(slab_kernel, ((0, 16), (16, 32), (32, 48), (48, 80))),
        (wide, full, full, of((32, D), BF16)), [VMEM, VMEM], keep, got,
    )
    far_c, far_b, both = to_chip(far_c, 3), to_chip(far_b, 2), to_chip(both, 1)
    near_c, near_b, mine = call(
        functools.partial(slab_kernel, ((80, 96), (96, 112), (112, 128))),
        (full, full, wide), [VMEM, VMEM], keep, got, cost=LONG,
    )
    near_c, near_b = to_chip(near_c, 3), to_chip(near_b, 2)
    away = call(sum_kernel, full, [VMEM] * 4, own, far_c, far_b, both, cost=LONG)
    far = lax.ppermute(away, "tp", [(i, i ^ 8) for i in range(16)])
    folded = call(fold_kernel, wide, [VMEM] * 5, mine, near_c, near_b, both, residual_in)
    return call(finish_kernel, (full, full), [VMEM] * 3, folded, far, norm_gain[None, :])


def solution(mesh):
    return jax.shard_map(
        shards,
        mesh=mesh,
        in_specs=(
            P("seq", "tp"),
            P("seq", "tp"),
            P("seq", "tp"),
            P("tp", "seq"),
            P("seq", None),
            P(("seq", "tp"), None),
            P("tp", None),
            P(),
        ),
        out_specs=(P(("seq", "tp"), None), P(("seq", "tp"), None)),
        check_vma=False,
    )
```

```python
import jax
import jax.numpy as jnp
from jax import lax
from jax.experimental import pallas as pl
from jax.experimental.pallas import tpu as pltpu
from jax.sharding import PartitionSpec as P

SPAN = 256
HEADS = 3
HDIM = 128
STATE = HEADS * HDIM
PAYLOAD = STATE + 8
D = 4096
F32 = jnp.float32
BF16 = jnp.bfloat16

SHARDS = 32
FLIP_Z = [(i, i ^ 1) for i in range(SHARDS)]
ROW_Y = [[g + 2 * k for k in range(4)] for g in range(SHARDS) if g & 6 == 0]
ROW_X = [[g + 8 * k for k in range(4)] for g in range(8)]
FAR_ORDER = (0, 2, 3, 1)
LONG = pl.CostEstimate(flops=10**11, bytes_accessed=0, transcendentals=0)
NEAR_CHIPS = [[8 * g + 2 * k + core for k in range(4)] for g in range(2) for core in range(2)]

VMEM = pl.BlockSpec(memory_space=pltpu.VMEM)
HBM = pl.BlockSpec(memory_space=pltpu.HBM)
SMEM = pl.BlockSpec(memory_space=pltpu.SMEM)


def segment_of(starts_ref, positions):
    total = jnp.zeros(positions.shape, jnp.int32)
    for slot in range(3):
        total = total + (positions >= starts_ref[0, slot]).astype(jnp.int32)
    return total


def running_sums(weights, decay, column):
    dims = (((1,), (1,)), ((), ()))
    a, b = (weights, decay) if column else (decay, weights)
    return lax.dot_general(a, b, dims, precision=lax.Precision.HIGHEST, preferred_element_type=F32)


def grid_iotas():
    row = lax.broadcasted_iota(jnp.int32, (SPAN, SPAN), 0)
    col = lax.broadcasted_iota(jnp.int32, (SPAN, SPAN), 1)
    return row, col


def state_kernel(
    starts_hbm, decay_hbm, key_hbm, value_hbm, out_ref,
    starts_ref, decay_ref, key_ref, value_ref, sems,
):
    sources = (decay_hbm, starts_hbm, key_hbm, value_hbm)
    targets = (decay_ref, starts_ref, key_ref, value_ref)
    copies = [
        pltpu.make_async_copy(source, target, sems.at[k])
        for k, (source, target) in enumerate(zip(sources, targets))
    ]
    for copy in copies:
        copy.start()
    row, col = grid_iotas()
    later = (col > row).astype(F32)
    copies[0].wait()
    decay = decay_ref[...]
    tail = running_sums(later, decay, True)
    copies[1].wait()
    segment = segment_of(starts_ref, lax.broadcasted_iota(jnp.int32, (SPAN, 1), 0))
    last = segment_of(starts_ref, jnp.full((1, 1), SPAN - 1, jnp.int32))
    tail_weight = jnp.exp(tail) * (segment == last).astype(F32)
    through = jnp.exp(jnp.sum(decay, axis=1, keepdims=True)) * (last == 0).astype(F32)
    high = through.astype(BF16).astype(F32)
    low = (through - high).astype(BF16).astype(F32)
    rows = jnp.concatenate([high, low, jnp.zeros((2, 1), F32)], axis=0)
    out_ref[STATE:, :] = jnp.broadcast_to(rows, (8, HDIM)).astype(BF16)
    copies[2].wait()
    copies[3].wait()
    for h in range(HEADS):
        cut = slice(h * HDIM, (h + 1) * HDIM)
        decayed = (key_ref[:, cut].astype(F32) * tail_weight[:, h : h + 1]).astype(BF16)
        out_ref[cut, :] = lax.dot_general(
            decayed, value_ref[:, cut], (((0,), (0,)), ((), ())), preferred_element_type=F32
        ).astype(BF16)


def intra_kernel(
    starts_ref, decay_ref, query_ref, key_ref, value_ref, weight_hbm,
    out_ref, carry_ref, weight_ref, sem,
):
    copy = pltpu.make_async_copy(weight_hbm, weight_ref, sem)
    copy.start()
    row, col = grid_iotas()
    lower = row >= col
    lower_f = lower.astype(F32)
    decay = decay_ref[...]
    cum_col = running_sums(lower_f, decay, True)
    cum_row = running_sums(lower_f, decay, False)
    seg_col = segment_of(starts_ref, lax.broadcasted_iota(jnp.int32, (SPAN, 1), 0))
    seg_row = segment_of(starts_ref, lax.broadcasted_iota(jnp.int32, (1, SPAN), 1))
    same = lower & (seg_col == seg_row)
    carry_ref[...] = jnp.exp(cum_col) * (seg_col == 0).astype(F32)
    for h in range(HEADS):
        cut = slice(h * HDIM, (h + 1) * HDIM)
        spread = cum_col[:, h : h + 1] - cum_row[h : h + 1, :]
        decay_mat = jnp.exp(jnp.where(same, spread, -jnp.inf))
        scores = lax.dot_general(
            query_ref[:, cut], key_ref[:, cut], (((1,), (1,)), ((), ())), preferred_element_type=F32
        )
        weights = (scores * decay_mat).astype(BF16)
        out_ref[:, cut] = jnp.dot(weights, value_ref[:, cut], preferred_element_type=F32)
    copy.wait()


def decays(rows):
    rows = rows.astype(F32)
    return rows[0:HEADS] + rows[HEADS : 2 * HEADS]


def split_decay(decay):
    high = decay.astype(BF16).astype(F32)
    low = (decay - high).astype(BF16).astype(F32)
    return jnp.concatenate([high, low, jnp.zeros((2, HDIM), F32)], axis=0).astype(BF16)


def pair_kernel(place_ref, own_ref, other_ref, out_ref):
    odd = place_ref[0] & 1 == 1
    own_a, other_a = decays(own_ref[STATE:, :]), decays(other_ref[STATE:, :])
    later_a = jnp.where(odd, own_a, other_a)
    scales = split_decay(own_a * other_a)
    for k in range(4):
        out_ref[k, STATE:, :] = scales
    for h in range(HEADS):
        cut = slice(h * HDIM, (h + 1) * HDIM)
        own, other = own_ref[cut, :].astype(F32), other_ref[cut, :].astype(F32)
        first, second = jnp.where(odd, other, own), jnp.where(odd, own, other)
        total = (later_a[h : h + 1] * first + second).astype(BF16)
        for k in range(4):
            out_ref[k, cut, :] = total


def row_kernel(parts_ref, out_ref):
    scale = [decays(parts_ref[k, STATE:, :]) for k in range(4)]
    scales = split_decay(scale[0] * scale[1] * scale[2] * scale[3])
    for k in range(4):
        out_ref[k, STATE:, :] = scales
    for h in range(HEADS):
        cut = slice(h * HDIM, (h + 1) * HDIM)
        total = parts_ref[0, cut, :].astype(F32)
        for k in range(1, 4):
            total = scale[k][h : h + 1] * total + parts_ref[k, cut, :].astype(F32)
        total = total.astype(BF16)
        for k in range(4):
            out_ref[k, cut, :] = total


def before(parts_ref, scale, reached, h):
    cut = slice(h * HDIM, (h + 1) * HDIM)
    state = jnp.zeros((HDIM, HDIM), F32)
    through = jnp.ones((1, HDIM), F32)
    for k in range(3):
        a = scale[k][h : h + 1]
        state = jnp.where(k < reached, a * state + parts_ref[k, cut, :].astype(F32), state)
        through = jnp.where(k < reached, a * through, through)
    return state, through


def attend_kernel(
    place_ref, query_ref, intra_ref, carry_ref, other_ref, row_ref, col_ref, weight_ref,
    send_ref, keep_ref, mixed_ref, sibling_ref,
):
    odd = place_ref[0] & 1 == 1
    carry = carry_ref[...]
    row_scale = [decays(row_ref[k, STATE:, :]) for k in range(3)]
    col_scale = [decays(col_ref[k, STATE:, :]) for k in range(3)]
    other_a = decays(other_ref[STATE:, :])
    for h in range(HEADS):
        cut = slice(h * HDIM, (h + 1) * HDIM)
        inner, inner_a = before(row_ref, row_scale, (place_ref[0] >> 1) & 3, h)
        outer, _ = before(col_ref, col_scale, place_ref[0] >> 3, h)
        state = inner_a * outer + inner
        state = jnp.where(odd, other_a[h : h + 1] * state + other_ref[cut, :].astype(F32), state)
        inter = jnp.dot(query_ref[:, cut], state.astype(BF16), preferred_element_type=F32)
        mixed = intra_ref[:, cut] + inter * carry[:, h : h + 1]
        scale = lax.rsqrt(jnp.mean(mixed * mixed, axis=1, keepdims=True) + 1e-06)
        mixed_ref[:, cut] = (mixed * scale).astype(BF16)
    core, chip = place_ref[1] & 1, place_ref[1] >> 1
    for k in range(8):
        start = ((chip & 4) + (k & 3) if k & 4 else chip ^ 4 ^ FAR_ORDER[k]) * 32
        cut = slice(k * 16, (k + 1) * 16)
        own, sibling = start + core * 16, start + (1 - core) * 16
        keep_ref[cut, :] = mixed_ref[pl.ds(pl.multiple_of(own, 16), 16), :]
        sibling_ref[cut, :] = mixed_ref[pl.ds(pl.multiple_of(sibling, 16), 16), :]
    send_ref[...] = jnp.dot(
        sibling_ref[...], weight_ref[...], preferred_element_type=F32
    ).astype(BF16)


def keep_kernel(own_ref, weight_ref, out_ref):
    out_ref[...] = jnp.dot(own_ref[...], weight_ref[...], preferred_element_type=F32)


def far_kernel(keep_ref, got_ref, *out_refs):
    for k, ref in enumerate(out_refs):
        cut = slice(k * 16, (k + 1) * 16)
        ref[...] = (keep_ref[cut, :] + got_ref[cut, :].astype(F32)).astype(ref.dtype)


def near_kernel(keep_ref, got_ref, out_ref, sum_ref, sems):
    copies = []
    for k in range(4):
        cut = slice(64 + k * 16, 80 + k * 16)
        sum_ref[k] = (keep_ref[cut, :] + got_ref[cut, :].astype(F32)).astype(BF16)
        copies.append(pltpu.make_async_copy(sum_ref.at[k], out_ref.at[k], sems.at[k]))
        copies[-1].start()
    for copy in copies:
        copy.wait()


def sum_kernel(own_ref, a_ref, b_ref, c_ref, out_ref):
    total = own_ref[...] + a_ref[...].astype(F32) + b_ref[...].astype(F32) + c_ref[...].astype(F32)
    out_ref[...] = total.astype(BF16)


def fold_kernel(parts_ref, residual_ref, out_ref):
    total = residual_ref[...].astype(F32)
    for k in range(4):
        total = total + parts_ref[k].astype(F32)
    out_ref[...] = total


def finish_kernel(near_ref, far_ref, gain_ref, hidden_ref, normed_ref):
    hidden = near_ref[...] + far_ref[...].astype(F32)
    scale = lax.rsqrt(jnp.mean(hidden * hidden, axis=1, keepdims=True) + 1e-05)
    hidden_ref[...] = hidden.astype(BF16)
    normed_ref[...] = (hidden * scale * gain_ref[...]).astype(BF16)


def call(body, shapes, specs, *args, scratch=(), outs=VMEM, cost=None):
    return pl.pallas_call(
        body,
        out_shape=shapes,
        in_specs=specs,
        out_specs=jax.tree.map(lambda _: outs, shapes),
        scratch_shapes=list(scratch),
        cost_estimate=cost,
        compiler_params=pltpu.CompilerParams(vmem_limit_bytes=16 * 1024 * 1024),
    )(*args)


def of(shape, dtype):
    return jax.ShapeDtypeStruct(shape, dtype)


def shards(
    query_rows, key_rows, value_rows, log_decay, doc_starts, residual_in, out_weight, norm_gain
):
    place = jnp.stack([lax.axis_index("seq"), lax.axis_index("tp")]).astype(jnp.int32)

    local = call(
        state_kernel, pltpu.VMEM((PAYLOAD, HDIM), BF16), [HBM] * 4,
        *(
            pltpu.with_memory_space_constraint(a, pltpu.HBM)
            for a in (doc_starts, log_decay, key_rows, value_rows)
        ),
        scratch=[
            pltpu.SMEM((1, 3), jnp.int32),
            pltpu.VMEM((HEADS, SPAN), F32),
            pltpu.VMEM((SPAN, STATE), BF16),
            pltpu.VMEM((SPAN, STATE), BF16),
            pltpu.SemaphoreType.DMA((4,)),
        ],
    )
    late_query = lax.optimization_barrier((local, query_rows))[1]
    other = lax.ppermute(local, "seq", FLIP_Z)
    intra, carry, weight = call(
        intra_kernel,
        (of((SPAN, STATE), F32), of((SPAN, HEADS), F32), pltpu.VMEM((STATE, D), BF16)),
        [SMEM, VMEM, VMEM, VMEM, VMEM, HBM],
        doc_starts, log_decay, late_query, key_rows, value_rows,
        pltpu.with_memory_space_constraint(out_weight, pltpu.HBM),
        scratch=[pltpu.SemaphoreType.DMA],
    )
    other, intra, carry = lax.optimization_barrier((other, intra, carry))
    four = of((4, PAYLOAD, HDIM), BF16)
    pairs = call(pair_kernel, four, [SMEM, VMEM, VMEM], place, local, other)
    rows = lax.all_to_all(pairs, "seq", 0, 0, axis_index_groups=ROW_Y)
    totals = call(row_kernel, four, [VMEM], rows)
    cols = lax.all_to_all(totals, "seq", 0, 0, axis_index_groups=ROW_X)
    send, keep = call(
        attend_kernel, (of((SPAN // 2, D), BF16), of((SPAN // 2, STATE), BF16)),
        [SMEM] + [VMEM] * 7,
        place, query_rows, intra, carry, other, rows, cols, weight,
        scratch=[pltpu.VMEM((SPAN, STATE), BF16), pltpu.VMEM((SPAN // 2, STATE), BF16)],
    )
    got = lax.ppermute(send, "tp", [(i, i ^ 1) for i in range(16)])
    keep = call(keep_kernel, of((SPAN // 2, D), F32), [VMEM, VMEM], keep, weight)
    full = of((16, D), BF16)
    own, *parts = call(
        far_kernel, (of((16, D), F32), full, full, full), [VMEM, VMEM], keep, got
    )
    parts = [
        lax.ppermute(sent, "tp", [(i, i ^ (2 * k)) for i in range(16)])
        for k, sent in zip(FAR_ORDER[1:], parts)
    ]
    near = call(
        near_kernel, pltpu.HBM((4, 16, D), BF16), [VMEM, VMEM], keep, got,
        scratch=[pltpu.VMEM((4, 16, D), BF16), pltpu.SemaphoreType.DMA((4,))], outs=HBM,
    )
    near = lax.all_to_all(near, "tp", 0, 0, axis_index_groups=NEAR_CHIPS)
    away = call(sum_kernel, full, [VMEM] * 4, own, *parts, cost=LONG)
    far = lax.ppermute(away, "tp", [(i, i ^ 8) for i in range(16)])
    folded = call(fold_kernel, of((16, D), F32), [VMEM] * 2, near, residual_in)
    return call(finish_kernel, (full, full), [VMEM] * 3, folded, far, norm_gain[None, :])


def solution(mesh):
    return jax.shard_map(
        shards,
        mesh=mesh,
        in_specs=(
            P("seq", "tp"),
            P("seq", "tp"),
            P("seq", "tp"),
            P("tp", "seq"),
            P("seq", None),
            P(("seq", "tp"), None),
            P("tp", None),
            P(),
        ),
        out_specs=(P(("seq", "tp"), None), P(("seq", "tp"), None)),
        check_vma=False,
    )
```

```python
import jax
import jax.numpy as jnp
from jax import lax
from jax.experimental import pallas as pl
from jax.experimental.pallas import tpu as pltpu
from jax.sharding import PartitionSpec as P

SPAN = 256
HEADS = 3
HDIM = 128
STATE = HEADS * HDIM
PAYLOAD = STATE + 8
D = 4096
F32 = jnp.float32
BF16 = jnp.bfloat16

SHARDS = 32
FLIP_Z = [(i, i ^ 1) for i in range(SHARDS)]
ROW_Y = [[g + 2 * k for k in range(4)] for g in range(SHARDS) if g & 6 == 0]
ROW_X = [[g + 8 * k for k in range(4)] for g in range(8)]
FAR_ORDER = (0, 3, 2, 1)
LONG = pl.CostEstimate(flops=10**11, bytes_accessed=0, transcendentals=0)
NEAR_CHIPS = [[8 * g + 2 * k + core for k in range(4)] for g in range(2) for core in range(2)]

VMEM = pl.BlockSpec(memory_space=pltpu.VMEM)
HBM = pl.BlockSpec(memory_space=pltpu.HBM)
SMEM = pl.BlockSpec(memory_space=pltpu.SMEM)


def segment_of(starts_ref, positions):
    total = jnp.zeros(positions.shape, jnp.int32)
    for slot in range(3):
        total = total + (positions >= starts_ref[0, slot]).astype(jnp.int32)
    return total


def running_sums(weights, decay, column):
    dims = (((1,), (1,)), ((), ()))
    a, b = (weights, decay) if column else (decay, weights)
    return lax.dot_general(a, b, dims, precision=lax.Precision.HIGHEST, preferred_element_type=F32)


def grid_iotas():
    row = lax.broadcasted_iota(jnp.int32, (SPAN, SPAN), 0)
    col = lax.broadcasted_iota(jnp.int32, (SPAN, SPAN), 1)
    return row, col


def state_kernel(
    starts_hbm, decay_hbm, key_hbm, value_hbm, out_ref,
    starts_ref, decay_ref, key_ref, value_ref, sems,
):
    sources = (decay_hbm, starts_hbm, key_hbm, value_hbm)
    targets = (decay_ref, starts_ref, key_ref, value_ref)
    copies = [
        pltpu.make_async_copy(source, target, sems.at[k])
        for k, (source, target) in enumerate(zip(sources, targets))
    ]
    for copy in copies:
        copy.start()
    row, col = grid_iotas()
    later = (col > row).astype(F32)
    copies[0].wait()
    decay = decay_ref[...]
    tail = running_sums(later, decay, True)
    copies[1].wait()
    segment = segment_of(starts_ref, lax.broadcasted_iota(jnp.int32, (SPAN, 1), 0))
    last = segment_of(starts_ref, jnp.full((1, 1), SPAN - 1, jnp.int32))
    tail_weight = jnp.exp(tail) * (segment == last).astype(F32)
    through = jnp.exp(jnp.sum(decay, axis=1, keepdims=True)) * (last == 0).astype(F32)
    high = through.astype(BF16).astype(F32)
    low = (through - high).astype(BF16).astype(F32)
    rows = jnp.concatenate([high, low, jnp.zeros((2, 1), F32)], axis=0)
    out_ref[STATE:, :] = jnp.broadcast_to(rows, (8, HDIM)).astype(BF16)
    copies[2].wait()
    copies[3].wait()
    for h in range(HEADS):
        cut = slice(h * HDIM, (h + 1) * HDIM)
        decayed = (key_ref[:, cut].astype(F32) * tail_weight[:, h : h + 1]).astype(BF16)
        out_ref[cut, :] = lax.dot_general(
            decayed, value_ref[:, cut], (((0,), (0,)), ((), ())), preferred_element_type=F32
        ).astype(BF16)


def intra_kernel(
    starts_ref, decay_ref, query_ref, key_ref, value_ref, weight_hbm,
    out_ref, carry_ref, weight_ref, sem,
):
    copy = pltpu.make_async_copy(weight_hbm, weight_ref, sem)
    copy.start()
    row, col = grid_iotas()
    lower = row >= col
    lower_f = lower.astype(F32)
    decay = decay_ref[...]
    cum_col = running_sums(lower_f, decay, True)
    cum_row = running_sums(lower_f, decay, False)
    seg_col = segment_of(starts_ref, lax.broadcasted_iota(jnp.int32, (SPAN, 1), 0))
    seg_row = segment_of(starts_ref, lax.broadcasted_iota(jnp.int32, (1, SPAN), 1))
    same = lower & (seg_col == seg_row)
    carry_ref[...] = jnp.exp(cum_col) * (seg_col == 0).astype(F32)
    for h in range(HEADS):
        cut = slice(h * HDIM, (h + 1) * HDIM)
        spread = cum_col[:, h : h + 1] - cum_row[h : h + 1, :]
        decay_mat = jnp.exp(jnp.where(same, spread, -jnp.inf))
        scores = lax.dot_general(
            query_ref[:, cut], key_ref[:, cut], (((1,), (1,)), ((), ())), preferred_element_type=F32
        )
        weights = (scores * decay_mat).astype(BF16)
        out_ref[:, cut] = jnp.dot(weights, value_ref[:, cut], preferred_element_type=F32)
    copy.wait()


def decays(rows):
    rows = rows.astype(F32)
    return rows[0:HEADS] + rows[HEADS : 2 * HEADS]


def split_decay(decay):
    high = decay.astype(BF16).astype(F32)
    low = (decay - high).astype(BF16).astype(F32)
    return jnp.concatenate([high, low, jnp.zeros((2, HDIM), F32)], axis=0).astype(BF16)


def pair_kernel(place_ref, own_ref, other_ref, out_ref):
    odd = place_ref[0] & 1 == 1
    own_a, other_a = decays(own_ref[STATE:, :]), decays(other_ref[STATE:, :])
    later_a = jnp.where(odd, own_a, other_a)
    scales = split_decay(own_a * other_a)
    for k in range(4):
        out_ref[k, STATE:, :] = scales
    for h in range(HEADS):
        cut = slice(h * HDIM, (h + 1) * HDIM)
        own, other = own_ref[cut, :].astype(F32), other_ref[cut, :].astype(F32)
        first, second = jnp.where(odd, other, own), jnp.where(odd, own, other)
        total = (later_a[h : h + 1] * first + second).astype(BF16)
        for k in range(4):
            out_ref[k, cut, :] = total


def row_kernel(parts_ref, out_ref):
    scale = [decays(parts_ref[k, STATE:, :]) for k in range(4)]
    scales = split_decay(scale[0] * scale[1] * scale[2] * scale[3])
    for k in range(4):
        out_ref[k, STATE:, :] = scales
    for h in range(HEADS):
        cut = slice(h * HDIM, (h + 1) * HDIM)
        total = parts_ref[0, cut, :].astype(F32)
        for k in range(1, 4):
            total = scale[k][h : h + 1] * total + parts_ref[k, cut, :].astype(F32)
        total = total.astype(BF16)
        for k in range(4):
            out_ref[k, cut, :] = total


def before(parts_ref, scale, reached, h):
    cut = slice(h * HDIM, (h + 1) * HDIM)
    state = jnp.zeros((HDIM, HDIM), F32)
    through = jnp.ones((1, HDIM), F32)
    for k in range(3):
        a = scale[k][h : h + 1]
        state = jnp.where(k < reached, a * state + parts_ref[k, cut, :].astype(F32), state)
        through = jnp.where(k < reached, a * through, through)
    return state, through


def attend_kernel(
    place_ref, query_ref, intra_ref, carry_ref, other_ref, row_ref, col_ref, weight_ref,
    far_ref, near_ref, keep_ref, mixed_ref, sibling_ref,
):
    odd = place_ref[0] & 1 == 1
    carry = carry_ref[...]
    row_scale = [decays(row_ref[k, STATE:, :]) for k in range(3)]
    col_scale = [decays(col_ref[k, STATE:, :]) for k in range(3)]
    other_a = decays(other_ref[STATE:, :])
    for h in range(HEADS):
        cut = slice(h * HDIM, (h + 1) * HDIM)
        inner, inner_a = before(row_ref, row_scale, (place_ref[0] >> 1) & 3, h)
        outer, _ = before(col_ref, col_scale, place_ref[0] >> 3, h)
        state = inner_a * outer + inner
        state = jnp.where(odd, other_a[h : h + 1] * state + other_ref[cut, :].astype(F32), state)
        inter = jnp.dot(query_ref[:, cut], state.astype(BF16), preferred_element_type=F32)
        mixed = intra_ref[:, cut] + inter * carry[:, h : h + 1]
        scale = lax.rsqrt(jnp.mean(mixed * mixed, axis=1, keepdims=True) + 1e-06)
        mixed_ref[:, cut] = (mixed * scale).astype(BF16)
    core, chip = place_ref[1] & 1, place_ref[1] >> 1
    for k in range(8):
        start = ((chip & 4) + (k & 3) if k & 4 else chip ^ 4 ^ FAR_ORDER[k]) * 32
        cut = slice(k * 16, (k + 1) * 16)
        own, sibling = start + core * 16, start + (1 - core) * 16
        keep_ref[cut, :] = mixed_ref[pl.ds(pl.multiple_of(own, 16), 16), :]
        sibling_ref[cut, :] = mixed_ref[pl.ds(pl.multiple_of(sibling, 16), 16), :]
    send = jnp.dot(sibling_ref[...], weight_ref[...], preferred_element_type=F32).astype(BF16)
    far_ref[...] = send[:64]
    near_ref[...] = send[64:]


def keep_kernel(own_ref, weight_ref, out_ref):
    out_ref[...] = jnp.dot(own_ref[...], weight_ref[...], preferred_element_type=F32)


def far_kernel(keep_ref, got_ref, *out_refs):
    for k, ref in enumerate(out_refs):
        cut = slice(k * 16, (k + 1) * 16)
        ref[...] = (keep_ref[cut, :] + got_ref[cut, :].astype(F32)).astype(ref.dtype)


def near_kernel(keep_ref, got_ref, out_ref, sum_ref, sems):
    copies = []
    for k in range(4):
        cut = slice(64 + k * 16, 80 + k * 16)
        got = got_ref[k * 16 : (k + 1) * 16, :]
        sum_ref[k] = (keep_ref[cut, :] + got.astype(F32)).astype(BF16)
        copies.append(pltpu.make_async_copy(sum_ref.at[k], out_ref.at[k], sems.at[k]))
        copies[-1].start()
    for copy in copies:
        copy.wait()


def sum_kernel(own_ref, a_ref, b_ref, c_ref, out_ref):
    total = own_ref[...] + a_ref[...].astype(F32) + b_ref[...].astype(F32) + c_ref[...].astype(F32)
    out_ref[...] = total.astype(BF16)


def fold_kernel(parts_ref, residual_ref, out_ref):
    total = residual_ref[...].astype(F32)
    for k in range(4):
        total = total + parts_ref[k].astype(F32)
    out_ref[...] = total


def finish_kernel(near_ref, far_ref, gain_ref, hidden_ref, normed_ref):
    hidden = near_ref[...] + far_ref[...].astype(F32)
    scale = lax.rsqrt(jnp.mean(hidden * hidden, axis=1, keepdims=True) + 1e-05)
    hidden_ref[...] = hidden.astype(BF16)
    normed_ref[...] = (hidden * scale * gain_ref[...]).astype(BF16)


def call(body, shapes, specs, *args, scratch=(), outs=VMEM, cost=None):
    return pl.pallas_call(
        body,
        out_shape=shapes,
        in_specs=specs,
        out_specs=jax.tree.map(lambda _: outs, shapes),
        scratch_shapes=list(scratch),
        cost_estimate=cost,
        compiler_params=pltpu.CompilerParams(vmem_limit_bytes=16 * 1024 * 1024),
    )(*args)


def of(shape, dtype):
    return jax.ShapeDtypeStruct(shape, dtype)


def shards(
    query_rows, key_rows, value_rows, log_decay, doc_starts, residual_in, out_weight, norm_gain
):
    place = jnp.stack([lax.axis_index("seq"), lax.axis_index("tp")]).astype(jnp.int32)

    local = call(
        state_kernel, pltpu.VMEM((PAYLOAD, HDIM), BF16), [HBM] * 4,
        *(
            pltpu.with_memory_space_constraint(a, pltpu.HBM)
            for a in (doc_starts, log_decay, key_rows, value_rows)
        ),
        scratch=[
            pltpu.SMEM((1, 3), jnp.int32),
            pltpu.VMEM((HEADS, SPAN), F32),
            pltpu.VMEM((SPAN, STATE), BF16),
            pltpu.VMEM((SPAN, STATE), BF16),
            pltpu.SemaphoreType.DMA((4,)),
        ],
    )
    late_query = lax.optimization_barrier((local, query_rows))[1]
    other = lax.ppermute(local, "seq", FLIP_Z)
    intra, carry, weight = call(
        intra_kernel,
        (of((SPAN, STATE), F32), of((SPAN, HEADS), F32), pltpu.VMEM((STATE, D), BF16)),
        [SMEM, VMEM, VMEM, VMEM, VMEM, HBM],
        doc_starts, log_decay, late_query, key_rows, value_rows,
        pltpu.with_memory_space_constraint(out_weight, pltpu.HBM),
        scratch=[pltpu.SemaphoreType.DMA],
    )
    other, intra, carry = lax.optimization_barrier((other, intra, carry))
    four = of((4, PAYLOAD, HDIM), BF16)
    pairs = call(pair_kernel, four, [SMEM, VMEM, VMEM], place, local, other)
    rows = lax.all_to_all(pairs, "seq", 0, 0, axis_index_groups=ROW_Y)
    totals = call(row_kernel, four, [VMEM], rows)
    cols = lax.all_to_all(totals, "seq", 0, 0, axis_index_groups=ROW_X)
    quarter = of((SPAN // 4, D), BF16)
    far, near, keep = call(
        attend_kernel, (quarter, quarter, of((SPAN // 2, STATE), BF16)),
        [SMEM] + [VMEM] * 7,
        place, query_rows, intra, carry, other, rows, cols, weight,
        scratch=[pltpu.VMEM((SPAN, STATE), BF16), pltpu.VMEM((SPAN // 2, STATE), BF16)],
    )
    got_far = lax.ppermute(far, "tp", [(i, i ^ 1) for i in range(16)])
    got_near = lax.ppermute(near, "tp", [(i, i ^ 1) for i in range(16)])
    keep = call(keep_kernel, of((SPAN // 2, D), F32), [VMEM, VMEM], keep, weight)
    full = of((16, D), BF16)
    own, *parts = call(
        far_kernel, (of((16, D), F32), full, full, full), [VMEM, VMEM], keep, got_far
    )
    parts = [
        lax.ppermute(sent, "tp", [(i, i ^ (2 * k)) for i in range(16)])
        for k, sent in zip(FAR_ORDER[1:], parts)
    ]
    near = call(
        near_kernel, pltpu.HBM((4, 16, D), BF16), [VMEM, VMEM], keep, got_near,
        scratch=[pltpu.VMEM((4, 16, D), BF16), pltpu.SemaphoreType.DMA((4,))], outs=HBM,
    )
    near = lax.all_to_all(near, "tp", 0, 0, axis_index_groups=NEAR_CHIPS)
    away = call(sum_kernel, full, [VMEM] * 4, own, *parts, cost=LONG)
    far = lax.ppermute(away, "tp", [(i, i ^ 8) for i in range(16)])
    folded = call(fold_kernel, of((16, D), F32), [VMEM] * 2, near, residual_in)
    return call(finish_kernel, (full, full), [VMEM] * 3, folded, far, norm_gain[None, :])


def solution(mesh):
    return jax.shard_map(
        shards,
        mesh=mesh,
        in_specs=(
            P("seq", "tp"),
            P("seq", "tp"),
            P("seq", "tp"),
            P("tp", "seq"),
            P("seq", None),
            P(("seq", "tp"), None),
            P("tp", None),
            P(),
        ),
        out_specs=(P(("seq", "tp"), None), P(("seq", "tp"), None)),
        check_vma=False,
    )
```
